1024 devices in a mesh: tm: 16 (over y, core), space: 16 (over z), dp: 4 (over x).
Axes of the slice: x: 4, y: 8, z: 16, core: 2. Of those that a mesh axis runs over, the one named last changes fastest.
Arguments:
- latents: bfloat16 [4, 4096, 2048], P('dp', 'tm'), may hold values from -6 to 6
- proj_input: bfloat16 [2048, 128], replicated, may hold values from -0.125 to 0.125
- proj_output: bfloat16 [2048, 128], replicated, may hold values from -0.125 to 0.125
- scan_input: bfloat16 [4, 4096, 4096], P('dp', 'tm', 'space'), may hold values from -6 to 6
- log_decay: float32 [4, 4096, 32], P('dp', 'tm', 'space'), may hold values from -2 to 0
- att_queries: bfloat16 [4, 4096, 4096], P('dp', 'tm', 'space'), may hold values from -67.88225 to 67.88225
- att_keys: bfloat16 [4, 4096, 4096], P('dp', 'tm', 'space'), may hold values from -3 to 3
- att_values: bfloat16 [4, 4096, 4096], P('dp', 'tm', 'space'), may hold values from -6 to 6
- scan_cotangent: bfloat16 [4, 4096, 4096], P('dp', 'tm', 'space'), may hold values from -0.59765625 to 0.59765625
- window_offsets: int32 [4, 32], P('dp', 'tm'), may hold values from 0 to 63
Outputs:
- layer_out: bfloat16 [4, 4096, 4096], P('dp', 'tm', 'space')
- input_grad: bfloat16 [4, 4096, 4096], P('dp', 'tm', 'space')
- proj_grad: float32 [2048, 256], P('space')
The draws below stay inside these ranges and needn't reach their ends.
All inputs are finite; a program needn't handle non-finite values.
Results may differ from the reference program's by a relative error of at most 0.027.
Values may be sent and summed in bfloat16 or wider, within the bound.
No kernel may reach another device: no remote copies, remote signals or barrier semaphores. Data moves between devices by JAX's collectives and lax.ppermute only.
A program may use at most 32 MiB of HBM per device.

```python
import math
import jax
import jax.numpy as jnp
from jax import lax

D = 2048
N = 128
H = 32
P_SIZE = 128
W = 128
QB = 128
TOK_DEV = 256
SEQ = 4096
CLIPS = 4


def key_base(key):
    return jnp.clip(jax.random.normal(jax.random.fold_in(key, 11), (CLIPS, SEQ, H * P_SIZE), jnp.float32), -3.0, 3.0)


def draw_att_keys(key, part):
    base = key_base(key)
    return base.astype(jnp.bfloat16)


def draw_att_queries(key, part):
    query = jnp.clip(jax.random.normal(jax.random.fold_in(key, 12), (CLIPS, SEQ, H * P_SIZE), jnp.float32), -3.0, 3.0)
    return query.astype(jnp.bfloat16)


def draw_log_decay(key, part):
    parts_of_key = jax.random.split(jax.random.fold_in(key, 13), 7)
    slow = -jax.random.uniform(parts_of_key[0], (CLIPS, 1, H), jnp.float32, 0.2, 0.6) / SEQ
    fast = -1.0 / jax.random.uniform(parts_of_key[1], (CLIPS, 1, H), jnp.float32, 30.0, 50.0)
    fast_share = 0.5
    picked = jax.random.uniform(parts_of_key[2], (CLIPS, 1, H), jnp.float32) < fast_share
    base = jnp.where(picked, fast, slow)
    rough = jnp.exp(jax.random.uniform(parts_of_key[3], (CLIPS, SEQ, H), jnp.float32, -0.69, 0.69))
    blocky = jnp.exp(jax.random.uniform(parts_of_key[4], (CLIPS, SEQ // TOK_DEV, 1, H), jnp.float32, -0.69, 0.69))
    blocky = jnp.broadcast_to(blocky, (CLIPS, SEQ // TOK_DEV, TOK_DEV, H)).reshape(CLIPS, SEQ, H)
    decay_speeds = base * rough * blocky
    spots = jax.random.randint(parts_of_key[5], (CLIPS, 2, 1), 0, SEQ)
    loss_values = jnp.log(jax.random.uniform(parts_of_key[6], (CLIPS, 2, H), jnp.float32, 0.5, 0.8))
    token_places = jnp.arange(SEQ)
    hit_mask = (token_places[None, None, :] == spots).astype(jnp.float32)
    spike_train = jnp.sum(hit_mask[:, :, :, None] * loss_values[:, :, None, :], axis=1)
    return decay_speeds + spike_train


def touch_ends(entries, own_key, least, largest):
    index_at = [jax.random.randint(jax.random.fold_in(own_key, axis), (), 0, length) for axis, length in enumerate(entries.shape)]
    longest = entries.shape.index(max(entries.shape))
    next_to = index_at[:longest] + [(index_at[longest] + 1) % entries.shape[longest]] + index_at[longest + 1:]
    return entries.at[tuple(index_at)].set(least).at[tuple(next_to)].set(largest)


def spiked(values, stream_key, source, target, parts, factor):
    def block_of(axis_at):
        return (jnp.arange(values.shape[axis_at]) // (values.shape[axis_at] // parts)).reshape((-1,) + (1,) * (values.ndim - 1 - axis_at))

    first = jax.random.permutation(stream_key, parts)[block_of(target)]
    far = (block_of(target) + parts // 2) % parts
    return jnp.where((block_of(source) == first) | (block_of(source) == far), factor * values, values)


def block_scale(own_key, shape, pieces, low, high):
    factor_of = 1.0
    for dim, shards_of in pieces:
        draws = jax.random.uniform(jax.random.fold_in(jax.random.fold_in(own_key, 6), dim), (shards_of,), jnp.float32, low / len(pieces), high / len(pieces))
        factor_of = factor_of * jnp.repeat(jnp.exp(draws), shape[dim] // shards_of).reshape((-1,) + (1,) * (len(shape) - 1 - dim))
    return factor_of


def scatter_about(key, extent, scale, limit, pieces=(), kind=jnp.bfloat16):
    values = scale * jax.random.normal(key, extent, jnp.float32)
    if pieces:
        values = values * block_scale(key, extent, pieces, -0.22, 0.18)
    return jnp.clip(values, -limit, limit).astype(kind)


def heavy_noise(stream_key, dims, spread, limit, pieces, heavy, held_as=jnp.bfloat16):
    entries = spread * jax.random.normal(stream_key, dims, jnp.float32)
    if pieces:
        entries = entries * block_scale(stream_key, dims, pieces, -0.22, 0.18)
    return jnp.clip(spiked(entries, jax.random.fold_in(stream_key, 3), *heavy), -limit, limit).astype(held_as)


def setup_inputs(seed: int = 0) -> dict:
    key_of = jax.random.split(jax.random.key(seed), 11)
    return {
        "latents": heavy_noise(key_of[0], (CLIPS, SEQ, D), 1.0, 6.0, ((0, 4), (1, 16)), (1, 2, 16, 2.0)),
        "proj_input": scatter_about(key_of[1], (D, N), D ** -0.5, 0.125),
        "proj_output": scatter_about(key_of[2], (D, N), D ** -0.5, 0.125),
        "scan_input": scatter_about(key_of[3], (CLIPS, SEQ, H * P_SIZE), 1.0, 6.0, ((0, 4), (1, 16), (2, 16))),
        "log_decay": draw_log_decay(jax.random.fold_in(key_of[10], 71), 0),
        "att_queries": draw_att_queries(jax.random.fold_in(key_of[10], 71), 0),
        "att_keys": draw_att_keys(jax.random.fold_in(key_of[10], 71), 0),
        "att_values": scatter_about(key_of[7], (CLIPS, SEQ, H * P_SIZE), 1.0, 6.0, ((0, 4), (1, 16), (2, 16))),
        "scan_cotangent": scatter_about(key_of[8], (CLIPS, SEQ, H * P_SIZE), 0.1, 0.59765625, ((0, 4), (1, 16), (2, 16))),
        "window_offsets": touch_ends(jax.random.randint(key_of[9], (CLIPS, SEQ // QB), 0, W // 2), jax.random.fold_in(key_of[9], 1), 0, (W // 2) - 1).astype(jnp.int32),
    }


precise = lax.Precision.HIGHEST

def block_decay(cum_decay):
    row_count = cum_decay.shape[0]
    position = jnp.arange(row_count, dtype=jnp.int32)
    lower_mask = position[:, None] >= position[None, :]
    log_gap = cum_decay.T[:, :, None] - cum_decay.T[:, None, :]
    return jnp.exp(jnp.where(lower_mask[None], log_gap, -jnp.inf))

def reference(latents, proj_input, proj_output, scan_input, log_decay, att_queries, att_keys, att_values, scan_cotangent, window_offsets):
    state_scale = 1.0 / math.sqrt(N)
    block_count = SEQ // TOK_DEV
    row_count = TOK_DEV

    def one_clip(data):
        lat_rows, scan_rows, decay_rows, query_rows, key_rows, value_rows, cotan_rows, offset_rows = data
        b_rows = jnp.dot(lat_rows, proj_input, preferred_element_type=jnp.float32).astype(jnp.bfloat16)
        c_rows = jnp.dot(lat_rows, proj_output, preferred_element_type=jnp.float32).astype(jnp.bfloat16)
        cum_decay = jnp.cumsum(decay_rows.astype(jnp.float32).reshape(block_count, row_count, H), axis=1)
        scan_blocks = scan_rows.reshape(block_count, row_count, H, P_SIZE)
        cotan_blocks = cotan_rows.reshape(block_count, row_count, H, P_SIZE)
        b_blocks = b_rows.reshape(block_count, row_count, N)
        c_blocks = c_rows.reshape(block_count, row_count, N)
        lat_blocks = lat_rows.reshape(block_count, row_count, D)

        def mixing_of(b_blk, c_blk, cum_blk):
            decay_mat = block_decay(cum_blk)
            kernel = jnp.dot(c_blk, b_blk.T, preferred_element_type=jnp.float32) * state_scale
            return (decay_mat, (kernel[None] * decay_mat).astype(jnp.bfloat16))

        def forward(state, item):
            scan_blk, b_blk, c_blk, cum_blk = item
            decay_mat, mixing = mixing_of(b_blk, c_blk, cum_blk)
            inner = jnp.einsum('hts,shp->thp', mixing.astype(jnp.float32), scan_blk.astype(jnp.float32))
            block_total = cum_blk[-1]
            cross = jnp.exp(cum_blk)[:, :, None] * jnp.einsum('tn,hpn->thp', c_blk.astype(jnp.float32) * state_scale, state, precision=precise)
            weighted = scan_blk.astype(jnp.float32) * jnp.exp(block_total[None] - cum_blk)[:, :, None]
            fresh = jnp.einsum('shp,sn->hpn', weighted, b_blk.astype(jnp.float32), precision=precise)
            new_state = jnp.exp(block_total)[:, None, None] * state + fresh
            return (new_state, (inner + cross, state))
        zero_state = jnp.zeros((H, P_SIZE, N), jnp.float32)
        _, (scan_out, state_in) = lax.scan(forward, zero_state, (scan_blocks, b_blocks, c_blocks, cum_decay))
        normed = scan_out * lax.rsqrt(lax.optimization_barrier(jnp.mean(scan_out * scan_out, axis=-1, keepdims=True)) + 1e-05)
        key_pad = jnp.concatenate([jnp.zeros((W, H * P_SIZE), key_rows.dtype), key_rows], 0)
        value_pad = jnp.concatenate([jnp.zeros((W, H * P_SIZE), value_rows.dtype), value_rows], 0)

        def attend(block):
            start = block * row_count
            query_blk = lax.dynamic_slice_in_dim(query_rows, start, row_count, 0).reshape(row_count, H, P_SIZE)
            key_blk = lax.dynamic_slice_in_dim(key_pad, start, row_count + W, 0).reshape(row_count + W, H, P_SIZE)
            value_blk = lax.dynamic_slice_in_dim(value_pad, start, row_count + W, 0).reshape(row_count + W, H, P_SIZE)
            offset_blk = lax.dynamic_slice_in_dim(offset_rows, block * (row_count // QB), row_count // QB, 0)
            offset_each = jnp.repeat(offset_blk, QB)
            t_pos = start + jnp.arange(row_count, dtype=jnp.int32)
            s_pos = start - W + jnp.arange(row_count + W, dtype=jnp.int32)
            seen = (s_pos[None] <= t_pos[:, None]) & (s_pos[None] >= t_pos[:, None] - W + 1 + offset_each[:, None]) & (s_pos[None] >= 0)
            scores = jnp.einsum('thp,shp->hts', query_blk.astype(jnp.float32), key_blk.astype(jnp.float32)) / math.sqrt(P_SIZE)
            scores = jnp.where(seen[None], scores, -jnp.inf)
            highest = lax.optimization_barrier(jnp.max(scores, axis=-1, keepdims=True))
            expo = jnp.exp(scores - highest)
            probs = (expo / lax.optimization_barrier(jnp.sum(expo, axis=-1, keepdims=True))).astype(jnp.bfloat16)
            return jnp.einsum('hts,shp->thp', probs.astype(jnp.float32), value_blk.astype(jnp.float32))
        attended = lax.map(attend, jnp.arange(block_count, dtype=jnp.int32))
        layer_out = (normed + attended).reshape(SEQ, H * P_SIZE).astype(jnp.bfloat16)

        def backward(carry, item):
            back_state, grad_sum = carry
            scan_blk, cotan_blk, b_blk, c_blk, cum_blk, enter_blk, lat_blk = item
            decay_mat, mixing = mixing_of(b_blk, c_blk, cum_blk)
            block_total = cum_blk[-1]
            tail_fall = jnp.exp(block_total[None] - cum_blk)
            head_rise = jnp.exp(cum_blk)
            scan_f = scan_blk.astype(jnp.float32)
            cotan_f = cotan_blk.astype(jnp.float32)
            b_f = b_blk.astype(jnp.float32)
            c_f = c_blk.astype(jnp.float32)
            grad_x = jnp.einsum('hts,thp->shp', mixing.astype(jnp.float32), cotan_f)
            grad_x = grad_x + tail_fall[:, :, None] * jnp.einsum('hpn,sn->shp', back_state, b_f, precision=precise)
            product = jnp.einsum('thp,shp->hts', cotan_f, scan_f)
            weigh = (product * decay_mat * state_scale).astype(jnp.bfloat16).astype(jnp.float32)
            grad_b = jnp.einsum('hts,tn->hsn', weigh, c_f) + tail_fall.T[:, :, None] * jnp.einsum('shp,hpn->hsn', scan_f, back_state, precision=precise)
            gradient_readout = jnp.einsum('hts,sn->htn', weigh, b_f) + (head_rise.T * state_scale)[:, :, None] * jnp.einsum('thp,hpn->htn', cotan_f, enter_blk, precision=precise)
            both = jnp.concatenate([grad_b, gradient_readout], axis=-1).astype(jnp.bfloat16).astype(jnp.float32)
            head_summed = lax.optimization_barrier(jnp.sum(both, axis=0))
            grad_sum = grad_sum + jnp.dot(lat_blk.astype(jnp.float32).T, head_summed, precision=precise)
            fresh = jnp.einsum('thp,tn->hpn', cotan_f * head_rise[:, :, None], c_f * state_scale, precision=precise)
            back_state = jnp.exp(block_total)[:, None, None] * back_state + fresh
            return ((back_state, grad_sum), grad_x)
        start_carry = (zero_state, jnp.zeros((D, 2 * N), jnp.float32))
        items = (scan_blocks, cotan_blocks, b_blocks, c_blocks, cum_decay, state_in, lat_blocks)
        (_, grad_sum), grad_x = lax.scan(backward, start_carry, items, reverse=True)
        return (layer_out, grad_x.reshape(SEQ, H * P_SIZE).astype(jnp.bfloat16), grad_sum)
    layer_out, input_grad, grad_parts = lax.map(one_clip, (latents, scan_input, log_decay, att_queries, att_keys, att_values, scan_cotangent, window_offsets))
    proj_grad = lax.optimization_barrier(jnp.sum(grad_parts, axis=0)) / math.sqrt(CLIPS * SEQ)
    return (layer_out, input_grad, proj_grad)
```

```python
import functools
import math

import jax
import jax.numpy as jnp
from jax import lax
from jax.experimental import pallas as pl
from jax.experimental.pallas import tpu as pltpu
from jax.sharding import PartitionSpec as P

W = 128
QB = 128
F32 = jnp.float32
BF16 = jnp.bfloat16
VMEM = pl.BlockSpec(memory_space=pltpu.VMEM)
SMEM = pl.BlockSpec(memory_space=pltpu.SMEM)
NEG = -1e30
EXTRA = 16


def dot(a, b, left, right, precision=None):
    return lax.dot_general(
        a, b, (((left,), (right,)), ((), ())), preferred_element_type=F32, precision=precision
    )


def call(body, out, args, specs=None, flops=0, transcendentals=0, moved=0):
    return pl.pallas_call(
        body,
        out_shape=[jax.ShapeDtypeStruct(s, t) for s, t in out],
        in_specs=specs or [VMEM] * len(args),
        out_specs=[VMEM] * len(out),
        compiler_params=pltpu.CompilerParams(vmem_limit_bytes=40 * 2**20),
        cost_estimate=pl.CostEstimate(
            flops=flops, transcendentals=transcendentals, bytes_accessed=moved
        ),
    )(*args)


def three_parts(value):
    high = value.astype(BF16)
    rest = value - high.astype(F32)
    middle = rest.astype(BF16)
    return high, middle, (rest - middle.astype(F32)).astype(BF16)


def put_totals(send, at, totals):
    row = lax.broadcasted_iota(jnp.int32, (EXTRA, send.shape[1]), 0)
    extra = jnp.zeros((EXTRA, send.shape[1]), F32)
    for h, total in enumerate(totals):
        for part, value in enumerate(three_parts(total)):
            extra = jnp.where(row == 3 * h + part, value.astype(F32), extra)
    send[at : at + EXTRA, :] = extra.astype(BF16)


def pre_body(heads, place, lat, wb, wc, x, cot, ld, b_out, c_out, cumc_out, cumr_out, fresh_out,
             back_out, table_out, send, mine_out):
    rows = lat.shape[0]
    cols = x.shape[1]
    hd = cols // heads
    n = wb.shape[1]
    scale = 1.0 / math.sqrt(n)
    b = dot(lat[...], wb[...], 1, 0).astype(BF16)
    c = dot(lat[...], wc[...], 1, 0).astype(BF16)
    b_out[...] = b
    c_out[...] = c
    share = mine_out.shape[1]
    mine_out[...] = lat[:, pl.ds(pl.multiple_of(place[0] * share, share), share)]
    t = lax.broadcasted_iota(jnp.int32, (rows, rows), 0)
    s = lax.broadcasted_iota(jnp.int32, (rows, rows), 1)
    lower = (s <= t).astype(F32)
    cumc = dot(lower, ld[...], 1, 0, lax.Precision.HIGHEST)
    cumr = dot(ld[...], lower, 0, 1, lax.Precision.HIGHEST)
    cumc_out[...] = cumc
    cumr_out[...] = cumr
    total = cumc[rows - 1 : rows, :]
    tail = jnp.exp(total - cumc)
    rise = jnp.exp(cumc) * scale
    table_out[...] = jnp.zeros_like(table_out)
    totals = []
    for h in range(heads):
        at = slice(h * hd, (h + 1) * hd)
        xs = (x[:, at].astype(F32) * tail[:, h : h + 1]).astype(BF16)
        gs = (cot[:, at].astype(F32) * rise[:, h : h + 1]).astype(BF16)
        fresh = dot(xs, b, 0, 0)
        back = dot(gs, c, 0, 0)
        fresh_out[at, :] = fresh
        back_out[at, :] = back
        send[at, :] = fresh.astype(BF16)
        send[cols + h * hd : cols + (h + 1) * hd, :] = back.astype(BF16)
        totals.append(jnp.broadcast_to(total[:, h : h + 1], (1, n)))
        table_out[h : h + 1, :] = totals[h]
    put_totals(send, 2 * cols, totals)


def totals_of(got, at):
    total = got[at : at + 1, :].astype(F32)
    for part in (1, 2):
        total = total + got[at + part : at + part + 1, :].astype(F32)
    return total


def pair_body(place, got, fwd, bwd, table, send):
    cols, n = fwd.shape
    slots, hd, _ = send.shape
    hd = hd - EXTRA
    me = place[0]
    late = me % 2
    chip = me // 2
    own = jnp.where(late == 1, table[1:2, :], table[0:1, :])
    theirs = jnp.where(
        late == 1, totals_of(got, 2 * cols + 3), totals_of(got, 2 * cols)
    )
    at = pl.ds(pl.multiple_of(late * hd, hd), hd)
    to = pl.ds(pl.multiple_of(cols + late * hd, hd), hd)
    got_f, got_b = got[at, :].astype(F32), got[to, :].astype(F32)
    by_own, by_theirs = jnp.exp(own), jnp.exp(theirs)
    early = late == 0
    f = jnp.where(early, by_theirs, 1.0) * fwd[at, :] + jnp.where(early, 1.0, by_own) * got_f
    b = jnp.where(early, 1.0, by_theirs) * bwd[at, :] + jnp.where(early, by_own, 1.0) * got_b
    f, b = f.astype(BF16), b.astype(BF16)
    row = lax.broadcasted_iota(jnp.int32, (EXTRA, n), 0)
    extra = jnp.zeros((EXTRA, n), F32)
    for part, value in enumerate(three_parts(own + theirs)):
        extra = jnp.where(row == part, value.astype(F32), extra)
    extra = extra.astype(BF16)
    for slot in range(slots):
        ahead = slot // 2 > chip

        @pl.when(ahead)
        def _():
            send[slot, :hd, :] = f

        @pl.when(jnp.logical_not(ahead))
        def _():
            send[slot, :hd, :] = b

        send[slot, hd:, :] = extra


def attend_body(heads, qb, place, offsets, q, k, v, tail, out):
    rows = q.shape[0]
    hd = q.shape[1] // heads
    w = tail.shape[0]
    scale = 1.0 / math.sqrt(hd)
    i = lax.broadcasted_iota(jnp.int32, (qb, qb + w), 0)
    u = lax.broadcasted_iota(jnp.int32, (qb, qb + w), 1)
    for blk in range(rows // qb):
        off = offsets[0, blk]
        seen = (u <= i + w) & (u >= i + 1 + off)
        if blk == 0:
            seen = seen & ((u >= w) | (place[0] > 0))
        for h in range(heads):
            at = slice(h * hd, (h + 1) * hd)
            if blk == 0:
                keys = jnp.concatenate([tail[:, at], k[:qb, at]], axis=0)
                values = jnp.concatenate(
                    [tail[:, heads * hd + h * hd : heads * hd + (h + 1) * hd], v[:qb, at]], axis=0
                )
            else:
                keys = k[blk * qb - w : (blk + 1) * qb, at]
                values = v[blk * qb - w : (blk + 1) * qb, at]
            scores = dot(q[blk * qb : (blk + 1) * qb, at], keys, 1, 1) * scale
            scores = jnp.where(seen, scores, NEG)
            expo = jnp.exp(scores - jnp.max(scores, axis=-1, keepdims=True))
            probs = (expo / jnp.sum(expo, axis=-1, keepdims=True)).astype(BF16)
            out[blk * qb : (blk + 1) * qb, at] = dot(probs, values, 1, 0)


def local_body(heads, x, cot, b, c, cumc, cumr, inner_out, gx_out, both_out):
    rows = x.shape[0]
    hd = x.shape[1] // heads
    n = b.shape[1]
    scale = 1.0 / math.sqrt(n)
    t = lax.broadcasted_iota(jnp.int32, (rows, rows), 0)
    s = lax.broadcasted_iota(jnp.int32, (rows, rows), 1)
    kern = dot(c[...], b[...], 1, 1) * scale
    weigh = None
    for h in range(heads):
        at = slice(h * hd, (h + 1) * hd)
        gap = cumc[:, h : h + 1] - cumr[h : h + 1, :]
        decay = jnp.exp(jnp.where(s <= t, gap, NEG))
        mixing = (kern * decay).astype(BF16)
        inner_out[:, at] = dot(mixing, x[:, at], 1, 0)
        gx_out[:, at] = dot(mixing, cot[:, at], 0, 0)
        one = dot(cot[:, at], x[:, at], 1, 1) * decay
        weigh = one if weigh is None else weigh + one
    weigh = (weigh * scale).astype(BF16)
    both_out[:, :n] = dot(weigh, c[...], 0, 0)
    both_out[:, n:] = dot(weigh, b[...], 1, 0)


def grads_body(heads, place, got, pair, x, cot, cumc, both, out, enter_out, leave_out):
    rows = x.shape[0]
    cols = x.shape[1]
    hd = cols // heads
    slots, _, n = got.shape
    scale = 1.0 / math.sqrt(n)
    chip = place[0] // 2
    early = place[0] % 2 == 0
    gb = both[:, :n]
    gc = both[:, n:]
    for h in range(heads):
        at = slice(h * hd, (h + 1) * hd)
        decays = [jnp.exp(totals_of(got.at[2 * i + h], hd)) for i in range(slots // 2)]
        state = jnp.zeros((hd, n), F32)
        grad = jnp.zeros((hd, n), F32)
        for i in range(slots // 2):
            used = i < chip
            state = jnp.where(used, decays[i], 1.0) * state + jnp.where(used, 1.0, 0.0) * got[
                2 * i + h, :hd, :
            ].astype(F32)
        for i in reversed(range(slots // 2)):
            used = i > chip
            grad = jnp.where(used, decays[i], 1.0) * grad + jnp.where(used, 1.0, 0.0) * got[
                2 * i + h, :hd, :
            ].astype(F32)
        by_theirs = jnp.exp(totals_of(pair, 2 * cols + 3 * h))
        their_f = pair[at, :].astype(F32)
        their_b = pair[cols + h * hd : cols + (h + 1) * hd, :].astype(F32)
        state = jnp.where(early, 1.0, by_theirs) * state + jnp.where(early, 0.0, 1.0) * their_f
        grad = jnp.where(early, by_theirs, 1.0) * grad + jnp.where(early, 1.0, 0.0) * their_b
        state, grad = state.astype(BF16), grad.astype(BF16)
        enter_out[at, :] = state
        leave_out[at, :] = grad
        cum = cumc[:, h : h + 1]
        tail = jnp.exp(cumc[rows - 1 : rows, h : h + 1] - cum)
        rise = jnp.exp(cum) * scale
        gb = gb + tail * dot(x[:, at], grad, 1, 0)
        gc = gc + rise * dot(cot[:, at], state, 1, 0)
    piece = out.shape[1]
    gb, gc = gb.astype(BF16), gc.astype(BF16)
    for i in range(out.shape[0]):
        out[i, :, :n] = gb[i * piece : (i + 1) * piece, :]
        out[i, :, n:] = gc[i * piece : (i + 1) * piece, :]


def finish_body(heads, b, c, cumc, inner, gx, attended, enter, leave, layer_out, input_grad):
    rows = b.shape[0]
    hd = inner.shape[1] // heads
    n = b.shape[1]
    scale = 1.0 / math.sqrt(n)
    for h in range(heads):
        at = slice(h * hd, (h + 1) * hd)
        cum = cumc[:, h : h + 1]
        tail = jnp.exp(cumc[rows - 1 : rows, h : h + 1] - cum)
        rise = jnp.exp(cum) * scale
        y = inner[:, at] + rise * dot(c[...], enter[at, :], 1, 1)
        y = y * lax.rsqrt(jnp.mean(y * y, axis=-1, keepdims=True) + 1e-05)
        layer_out[:, at] = (y + attended[:, at]).astype(BF16)
        g = gx[:, at] + tail * dot(b[...], leave[at, :], 1, 1)
        input_grad[:, at] = g.astype(BF16)


def gather_body(scale, got, out):
    total = got[0].astype(F32)
    for i in range(1, got.shape[0]):
        total = total + got[i].astype(F32)
    total = (total * scale).astype(BF16)
    for i in range(out.shape[0]):
        out[i] = total


def project_body(mine, both, out):
    size, rows, cols = both.shape
    term = dot(mine[...], both[...].reshape(size * rows, cols), 0, 0)
    piece = out.shape[1]
    for i in range(out.shape[0]):
        out[i] = term[i * piece : (i + 1) * piece, :].astype(BF16)


def unpack_body(got, out):
    piece = got.shape[1]
    for i in range(got.shape[0]):
        out[i * piece : (i + 1) * piece, :] = got[i].astype(F32)


def shifted(block, axis, distance):
    devices = range(lax.axis_size(axis))
    route = [(i - distance, i) for i in devices if i - distance in devices]
    return lax.ppermute(block, axis, route)


def swapped(block, axis, distance):
    return lax.ppermute(block, axis, [(i, i ^ distance) for i in range(lax.axis_size(axis))])


def summed(pieces, axes, scale=1.0):
    got = lax.all_to_all(pieces, axes, 0, 0)
    copies = call(functools.partial(gather_body, scale), [(pieces.shape, BF16)], (got,))[0]
    return lax.all_to_all(copies, axes, 0, 0)


def on_device(latents, proj_input, proj_output, scan_input, log_decay, att_queries, att_keys,
              att_values, scan_cotangent, window_offsets):
    _, rows, width = latents.shape
    heads = log_decay.shape[2]
    cols = scan_input.shape[2]
    hd = cols // heads
    n = proj_input.shape[1]
    share = width // lax.axis_size("space")
    assert heads == 2
    tm = lax.axis_size("tm")
    me = lax.axis_index("tm")
    lat, x, ld = latents[0], scan_input[0], log_decay[0]
    q, k, v, cot = att_queries[0], att_keys[0], att_values[0], scan_cotangent[0]

    tails = shifted(jnp.concatenate([k[rows - W :], v[rows - W :]], axis=1), "tm", 1)
    state = ((cols, n), F32)
    wire = ((2 * cols + EXTRA, n), BF16)
    b, c, cumc, cumr, fwd, bwd, table, send, mine = call(
        functools.partial(pre_body, heads),
        [((rows, n), BF16), ((rows, n), BF16), ((rows, heads), F32), ((heads, rows), F32), state, state,
         ((24, n), F32), wire, ((rows, share), BF16)],
        (lax.axis_index("space")[None], lat, proj_input, proj_output, x, cot, ld),
        [SMEM] + [VMEM] * 6,
        flops=2 * rows * width * 2 * n + 4 * rows * cols * n,
    )
    attended = call(
        functools.partial(attend_body, heads, QB),
        [((rows, cols), F32)],
        (me[None], window_offsets, q, k, v, tails),
        [SMEM, SMEM] + [VMEM] * 4,
        flops=4 * rows * 2 * W * cols,
        transcendentals=rows * 2 * W * heads,
    )[0]
    inner, gx, both = call(
        functools.partial(local_body, heads),
        [((rows, cols), F32), ((rows, cols), F32), ((rows, 2 * n), F32)],
        (x, cot, b, c, cumc, cumr),
        flops=8 * rows * rows * cols,
        transcendentals=rows * rows * heads,
    )
    pair = swapped(send, "tm", 1)
    spread = call(
        pair_body,
        [((tm, hd + EXTRA, n), BF16)],
        (me[None], pair, fwd, bwd, table),
        [SMEM] + [VMEM] * 4,
    )[0]
    got = lax.all_to_all(spread, "tm", 0, 0)
    space = lax.axis_size("space")
    both, enter, leave = call(
        functools.partial(grads_body, heads),
        [((space, rows // space, 2 * n), BF16), ((cols, n), BF16), ((cols, n), BF16)],
        (me[None], got, pair, x, cot, cumc, both),
        [SMEM] + [VMEM] * 6,
        flops=4 * rows * cols * n,
    )
    layer_out, input_grad = call(
        functools.partial(finish_body, heads),
        [((rows, cols), BF16), ((rows, cols), BF16)],
        (b, c, cumc, inner, gx, attended, enter, leave),
        flops=4 * rows * cols * n,
    )
    both = summed(both, ("space",))
    others = tm * lax.axis_size("dp")
    term = call(
        project_body,
        [((others, share // others, 2 * n), BF16)],
        (mine, both),
        flops=2 * rows * share * 2 * n,
    )[0]
    term = summed(term, ("tm", "dp"), 1.0 / math.sqrt(rows * others))
    proj_grad = call(unpack_body, [((share, 2 * n), F32)], (term,))[0]
    return layer_out[None], input_grad[None], proj_grad


def solution(mesh):
    wide = P("dp", "tm", "space")
    return jax.shard_map(
        on_device,
        mesh=mesh,
        in_specs=(P("dp", "tm", None), P(), P(), wide, wide, wide, wide, wide, wide, P("dp", "tm")),
        out_specs=(wide, wide, P("space", None)),
        check_vma=False,
    )
```

```python
import functools
import math

import jax
import jax.numpy as jnp
from jax import lax
from jax.experimental import pallas as pl
from jax.experimental.pallas import tpu as pltpu
from jax.sharding import PartitionSpec as P

W = 128
QB = 128
F32 = jnp.float32
BF16 = jnp.bfloat16
VMEM = pl.BlockSpec(memory_space=pltpu.VMEM)
HBM = pl.BlockSpec(memory_space=pltpu.HBM)
SMEM = pl.BlockSpec(memory_space=pltpu.SMEM)
NEG = -1e30
EXTRA = 16


def dot(a, b, left, right, precision=None):
    return lax.dot_general(
        a, b, (((left,), (right,)), ((), ())), preferred_element_type=F32, precision=precision
    )


def call(body, out, args, specs=None, scratch=(), flops=0, transcendentals=0, moved=0):
    return pl.pallas_call(
        body,
        out_shape=[jax.ShapeDtypeStruct(s, t) for s, t in out],
        in_specs=specs or [VMEM] * len(args),
        out_specs=[VMEM] * len(out),
        scratch_shapes=scratch,
        compiler_params=pltpu.CompilerParams(vmem_limit_bytes=40 * 2**20),
        cost_estimate=pl.CostEstimate(
            flops=flops, transcendentals=transcendentals, bytes_accessed=moved
        ),
    )(*args)


def three_parts(value):
    high = value.astype(BF16)
    rest = value - high.astype(F32)
    middle = rest.astype(BF16)
    return high, middle, (rest - middle.astype(F32)).astype(BF16)


def put_totals(send, at, totals):
    row = lax.broadcasted_iota(jnp.int32, (EXTRA, send.shape[1]), 0)
    extra = jnp.zeros((EXTRA, send.shape[1]), F32)
    for h, total in enumerate(totals):
        for part, value in enumerate(three_parts(total)):
            extra = jnp.where(row == 3 * h + part, value.astype(F32), extra)
    send[at : at + EXTRA, :] = extra.astype(BF16)


def pre_body(heads, place, lat_in, wb_in, wc_in, x_in, cot_in, ld_in, b_out, c_out, cumc_out, cumr_out,
             fresh_out, back_out, table_out, send, mine_out, lat, wb, wc, x, cot, ld, sems):
    pairs = ((ld_in, ld), (lat_in, lat), (wb_in, wb), (wc_in, wc), (x_in, x), (cot_in, cot))
    copies = [pltpu.make_async_copy(src, dst, sems.at[i]) for i, (src, dst) in enumerate(pairs)]
    for copy in copies:
        copy.start()
    rows = lat.shape[0]
    cols = x.shape[1]
    hd = cols // heads
    n = wb.shape[1]
    scale = 1.0 / math.sqrt(n)
    t = lax.broadcasted_iota(jnp.int32, (rows, rows), 0)
    s = lax.broadcasted_iota(jnp.int32, (rows, rows), 1)
    lower = (s <= t).astype(F32)
    copies[0].wait()
    cumc = dot(lower, ld[...], 1, 1, lax.Precision.HIGHEST)
    cumr = dot(ld[...], lower, 1, 1, lax.Precision.HIGHEST)
    cumc_out[...] = cumc
    cumr_out[...] = cumr
    total = cumc[rows - 1 : rows, :]
    tail = jnp.exp(total - cumc)
    rise = jnp.exp(cumc) * scale
    table_out[...] = jnp.zeros_like(table_out)
    totals = []
    for h in range(heads):
        totals.append(jnp.broadcast_to(total[:, h : h + 1], (1, n)))
        table_out[h : h + 1, :] = totals[h]
    put_totals(send, 2 * cols, totals)
    copies[1].wait()
    share = mine_out.shape[1]
    mine_out[...] = lat[:, pl.ds(pl.multiple_of(place[0] * share, share), share)]
    copies[2].wait()
    b = dot(lat[...], wb[...], 1, 0).astype(BF16)
    b_out[...] = b
    copies[3].wait()
    c = dot(lat[...], wc[...], 1, 0).astype(BF16)
    c_out[...] = c
    copies[4].wait()
    copies[5].wait()
    for h in range(heads):
        at = slice(h * hd, (h + 1) * hd)
        xs = (x[:, at].astype(F32) * tail[:, h : h + 1]).astype(BF16)
        gs = (cot[:, at].astype(F32) * rise[:, h : h + 1]).astype(BF16)
        fresh = dot(xs, b, 0, 0)
        back = dot(gs, c, 0, 0)
        fresh_out[at, :] = fresh
        back_out[at, :] = back
        send[at, :] = fresh.astype(BF16)
        send[cols + h * hd : cols + (h + 1) * hd, :] = back.astype(BF16)


def totals_of(got, at):
    total = got[at : at + 1, :].astype(F32)
    for part in (1, 2):
        total = total + got[at + part : at + part + 1, :].astype(F32)
    return total


def pair_body(place, got, fwd, bwd, table, send):
    cols, n = fwd.shape
    slots, hd, _ = send.shape
    hd = hd - EXTRA
    me = place[0]
    late = me % 2
    chip = me // 2
    own = jnp.where(late == 1, table[1:2, :], table[0:1, :])
    theirs = jnp.where(
        late == 1, totals_of(got, 2 * cols + 3), totals_of(got, 2 * cols)
    )
    at = pl.ds(pl.multiple_of(late * hd, hd), hd)
    to = pl.ds(pl.multiple_of(cols + late * hd, hd), hd)
    got_f, got_b = got[at, :].astype(F32), got[to, :].astype(F32)
    by_own, by_theirs = jnp.exp(own), jnp.exp(theirs)
    early = late == 0
    f = jnp.where(early, by_theirs, 1.0) * fwd[at, :] + jnp.where(early, 1.0, by_own) * got_f
    b = jnp.where(early, 1.0, by_theirs) * bwd[at, :] + jnp.where(early, by_own, 1.0) * got_b
    row = lax.broadcasted_iota(jnp.int32, (EXTRA, n), 0)
    extra = jnp.zeros((EXTRA, n), F32)
    for part, value in enumerate(three_parts(own + theirs)):
        extra = jnp.where(row == part, value.astype(F32), extra)
    extra = extra.astype(BF16)
    for slot in range(slots):
        send[slot, :hd, :] = jnp.where(slot // 2 > chip, f, b).astype(BF16)
        send[slot, hd:, :] = extra


def attend(heads, qb, place, offsets, q, k, v, tail, out):
    rows = q.shape[0]
    hd = q.shape[1] // heads
    w = tail.shape[0]
    scale = 1.0 / math.sqrt(hd)
    i = lax.broadcasted_iota(jnp.int32, (qb, qb + w), 0)
    u = lax.broadcasted_iota(jnp.int32, (qb, qb + w), 1)
    for blk in range(rows // qb):
        off = offsets[0, blk]
        seen = (u <= i + w) & (u >= i + 1 + off)
        if blk == 0:
            seen = seen & ((u >= w) | (place[0] > 0))
        for h in range(heads):
            at = slice(h * hd, (h + 1) * hd)
            if blk == 0:
                keys = jnp.concatenate([tail[:, at], k[:qb, at]], axis=0)
                values = jnp.concatenate(
                    [tail[:, heads * hd + h * hd : heads * hd + (h + 1) * hd], v[:qb, at]], axis=0
                )
            else:
                keys = k[blk * qb - w : (blk + 1) * qb, at]
                values = v[blk * qb - w : (blk + 1) * qb, at]
            scores = dot(q[blk * qb : (blk + 1) * qb, at], keys, 1, 1) * scale
            scores = jnp.where(seen, scores, NEG)
            expo = jnp.exp(scores - jnp.max(scores, axis=-1, keepdims=True))
            probs = (expo / jnp.sum(expo, axis=-1, keepdims=True)).astype(BF16)
            out[blk * qb : (blk + 1) * qb, at] = dot(probs, values, 1, 0)


def middle_body(heads, qb, place, offsets, q, k, v, tail, x, cot, b, c, cumc, cumr, attended_out,
                inner_out, gx_out, both_out):
    attend(heads, qb, place, offsets, q, k, v, tail, attended_out)
    rows = x.shape[0]
    hd = x.shape[1] // heads
    n = b.shape[1]
    scale = 1.0 / math.sqrt(n)
    t = lax.broadcasted_iota(jnp.int32, (rows, rows), 0)
    s = lax.broadcasted_iota(jnp.int32, (rows, rows), 1)
    kern = dot(c[...], b[...], 1, 1) * scale
    weigh = None
    for h in range(heads):
        at = slice(h * hd, (h + 1) * hd)
        gap = cumc[:, h : h + 1] - cumr[h : h + 1, :]
        decay = jnp.exp(jnp.where(s <= t, gap, NEG))
        mixing = (kern * decay).astype(BF16)
        inner_out[:, at] = dot(mixing, x[:, at], 1, 0)
        gx_out[:, at] = dot(mixing, cot[:, at], 0, 0)
        one = dot(cot[:, at], x[:, at], 1, 1) * decay
        weigh = one if weigh is None else weigh + one
    weigh = (weigh * scale).astype(BF16)
    both_out[:, :n] = dot(weigh, c[...], 0, 0)
    both_out[:, n:] = dot(weigh, b[...], 1, 0)


def grads_body(heads, place, got, pair, x, cot, cumc, both, out, enter_out, leave_out):
    rows = x.shape[0]
    cols = x.shape[1]
    hd = cols // heads
    slots, _, n = got.shape
    scale = 1.0 / math.sqrt(n)
    chip = place[0] // 2
    early = place[0] % 2 == 0
    gb = both[:, :n]
    gc = both[:, n:]
    for h in range(heads):
        at = slice(h * hd, (h + 1) * hd)
        decays = [jnp.exp(totals_of(got.at[2 * i + h], hd)) for i in range(slots // 2)]
        state = jnp.zeros((hd, n), F32)
        grad = jnp.zeros((hd, n), F32)
        for i in range(slots // 2):
            used = i < chip
            state = jnp.where(used, decays[i], 1.0) * state + jnp.where(used, 1.0, 0.0) * got[
                2 * i + h, :hd, :
            ].astype(F32)
        for i in reversed(range(slots // 2)):
            used = i > chip
            grad = jnp.where(used, decays[i], 1.0) * grad + jnp.where(used, 1.0, 0.0) * got[
                2 * i + h, :hd, :
            ].astype(F32)
        by_theirs = jnp.exp(totals_of(pair, 2 * cols + 3 * h))
        their_f = pair[at, :].astype(F32)
        their_b = pair[cols + h * hd : cols + (h + 1) * hd, :].astype(F32)
        state = jnp.where(early, 1.0, by_theirs) * state + jnp.where(early, 0.0, 1.0) * their_f
        grad = jnp.where(early, by_theirs, 1.0) * grad + jnp.where(early, 1.0, 0.0) * their_b
        state, grad = state.astype(BF16), grad.astype(BF16)
        enter_out[at, :] = state
        leave_out[at, :] = grad
        cum = cumc[:, h : h + 1]
        tail = jnp.exp(cumc[rows - 1 : rows, h : h + 1] - cum)
        rise = jnp.exp(cum) * scale
        gb = gb + tail * dot(x[:, at], grad, 1, 0)
        gc = gc + rise * dot(cot[:, at], state, 1, 0)
    piece = out.shape[1]
    gb, gc = gb.astype(BF16), gc.astype(BF16)
    for i in range(out.shape[0]):
        out[i, :, :n] = gb[i * piece : (i + 1) * piece, :]
        out[i, :, n:] = gc[i * piece : (i + 1) * piece, :]


def finish_body(heads, b, c, cumc, inner, gx, attended, enter, leave, layer_out, input_grad):
    rows = b.shape[0]
    hd = inner.shape[1] // heads
    n = b.shape[1]
    scale = 1.0 / math.sqrt(n)
    for h in range(heads):
        at = slice(h * hd, (h + 1) * hd)
        cum = cumc[:, h : h + 1]
        tail = jnp.exp(cumc[rows - 1 : rows, h : h + 1] - cum)
        rise = jnp.exp(cum) * scale
        y = inner[:, at] + rise * dot(c[...], enter[at, :], 1, 1)
        y = y * lax.rsqrt(jnp.mean(y * y, axis=-1, keepdims=True) + 1e-05)
        layer_out[:, at] = (y + attended[:, at]).astype(BF16)
        g = gx[:, at] + tail * dot(b[...], leave[at, :], 1, 1)
        input_grad[:, at] = g.astype(BF16)


def gather_body(scale, got, out):
    total = got[0].astype(F32)
    for i in range(1, got.shape[0]):
        total = total + got[i].astype(F32)
    total = (total * scale).astype(BF16)
    for i in range(out.shape[0]):
        out[i] = total


def project_body(mine, both, out):
    size, rows, cols = both.shape
    term = dot(mine[...], both[...].reshape(size * rows, cols), 0, 0)
    piece = out.shape[1]
    for i in range(out.shape[0]):
        out[i] = term[i * piece : (i + 1) * piece, :].astype(BF16)


def unpack_body(got, out):
    piece = got.shape[1]
    for i in range(got.shape[0]):
        out[i * piece : (i + 1) * piece, :] = got[i].astype(F32)


def shifted(block, axis, distance):
    devices = range(lax.axis_size(axis))
    route = [(i - distance, i) for i in devices if i - distance in devices]
    return lax.ppermute(block, axis, route)


def swapped(block, axis, distance):
    return lax.ppermute(block, axis, [(i, i ^ distance) for i in range(lax.axis_size(axis))])


def summed(pieces, axes, scale=1.0):
    got = lax.all_to_all(pieces, axes, 0, 0)
    copies = call(functools.partial(gather_body, scale), [(pieces.shape, BF16)], (got,))[0]
    return lax.all_to_all(copies, axes, 0, 0)


def on_device(latents, proj_input, proj_output, scan_input, log_decay, att_queries, att_keys,
              att_values, scan_cotangent, window_offsets):
    _, rows, width = latents.shape
    heads = log_decay.shape[2]
    cols = scan_input.shape[2]
    hd = cols // heads
    n = proj_input.shape[1]
    share = width // lax.axis_size("space")
    assert heads == 2
    tm = lax.axis_size("tm")
    me = lax.axis_index("tm")
    lat, x, ld = latents[0], scan_input[0], log_decay[0].T
    q, k, v, cot = att_queries[0], att_keys[0], att_values[0], scan_cotangent[0]

    inputs = [
        pltpu.with_memory_space_constraint(a, pltpu.HBM)
        for a in (lat, proj_input, proj_output, x, cot, ld)
    ]
    tails = shifted(jnp.concatenate([k[rows - W :], v[rows - W :]], axis=1), "tm", 1)
    state = ((cols, n), F32)
    wire = ((2 * cols + EXTRA, n), BF16)
    b, c, cumc, cumr, fwd, bwd, table, send, mine = call(
        functools.partial(pre_body, heads),
        [((rows, n), BF16), ((rows, n), BF16), ((rows, heads), F32), ((heads, rows), F32), state, state,
         ((24, n), F32), wire, ((rows, share), BF16)],
        (lax.axis_index("space")[None], *inputs),
        [SMEM] + [HBM] * 6,
        [pltpu.VMEM(a.shape, a.dtype) for a in inputs] + [pltpu.SemaphoreType.DMA((6,))],
        flops=2 * rows * width * 2 * n + 4 * rows * cols * n,
    )
    attended, inner, gx, both = call(
        functools.partial(middle_body, heads, QB),
        [((rows, cols), F32), ((rows, cols), F32), ((rows, cols), F32), ((rows, 2 * n), F32)],
        (me[None], window_offsets, q, k, v, tails, x, cot, b, c, cumc, cumr),
        [SMEM, SMEM] + [VMEM] * 10,
        flops=8 * rows * rows * cols + 4 * rows * 2 * W * cols,
        transcendentals=rows * rows * heads + rows * 2 * W * heads,
    )
    pair = swapped(send, "tm", 1)
    spread = call(
        pair_body,
        [((tm, hd + EXTRA, n), BF16)],
        (me[None], pair, fwd, bwd, table),
        [SMEM] + [VMEM] * 4,
    )[0]
    got = lax.all_to_all(spread, "tm", 0, 0)
    space = lax.axis_size("space")
    both, enter, leave = call(
        functools.partial(grads_body, heads),
        [((space, rows // space, 2 * n), BF16), ((cols, n), BF16), ((cols, n), BF16)],
        (me[None], got, pair, x, cot, cumc, both),
        [SMEM] + [VMEM] * 6,
        flops=4 * rows * cols * n,
    )
    layer_out, input_grad = call(
        functools.partial(finish_body, heads),
        [((rows, cols), BF16), ((rows, cols), BF16)],
        (b, c, cumc, inner, gx, attended, enter, leave),
        flops=4 * rows * cols * n,
    )
    both = summed(both, ("space",))
    others = tm * lax.axis_size("dp")
    term = call(
        project_body,
        [((others, share // others, 2 * n), BF16)],
        (mine, both),
        flops=2 * rows * share * 2 * n,
    )[0]
    term = summed(term, ("tm", "dp"), 1.0 / math.sqrt(rows * others))
    proj_grad = call(unpack_body, [((share, 2 * n), F32)], (term,))[0]
    return layer_out[None], input_grad[None], proj_grad


def solution(mesh):
    wide = P("dp", "tm", "space")
    return jax.shard_map(
        on_device,
        mesh=mesh,
        in_specs=(P("dp", "tm", None), P(), P(), wide, wide, wide, wide, wide, wide, P("dp", "tm")),
        out_specs=(wide, wide, P("space", None)),
        check_vma=False,
    )
```

```python
import functools
import math

import jax
import jax.numpy as jnp
from jax import lax
from jax.experimental import pallas as pl
from jax.experimental.pallas import tpu as pltpu
from jax.sharding import PartitionSpec as P

W = 128
QB = 128
F32 = jnp.float32
BF16 = jnp.bfloat16
VMEM = pl.BlockSpec(memory_space=pltpu.VMEM)
HBM = pl.BlockSpec(memory_space=pltpu.HBM)
SMEM = pl.BlockSpec(memory_space=pltpu.SMEM)
NEG = -1e30
EXTRA = 16


def dot(a, b, left, right, precision=None):
    return lax.dot_general(
        a, b, (((left,), (right,)), ((), ())), preferred_element_type=F32, precision=precision
    )


def call(body, out, args, specs=None, scratch=(), flops=0, transcendentals=0, moved=0):
    return pl.pallas_call(
        body,
        out_shape=[jax.ShapeDtypeStruct(s, t) for s, t in out],
        in_specs=specs or [VMEM] * len(args),
        out_specs=[VMEM] * len(out),
        scratch_shapes=scratch,
        compiler_params=pltpu.CompilerParams(vmem_limit_bytes=40 * 2**20),
        cost_estimate=pl.CostEstimate(
            flops=flops, transcendentals=transcendentals, bytes_accessed=moved
        ),
    )(*args)


def three_parts(value):
    high = value.astype(BF16)
    rest = value - high.astype(F32)
    middle = rest.astype(BF16)
    return high, middle, (rest - middle.astype(F32)).astype(BF16)


def put_totals(send, at, totals):
    row = lax.broadcasted_iota(jnp.int32, (EXTRA, send.shape[1]), 0)
    extra = jnp.zeros((EXTRA, send.shape[1]), F32)
    for h, total in enumerate(totals):
        for part, value in enumerate(three_parts(total)):
            extra = jnp.where(row == 3 * h + part, value.astype(F32), extra)
    send[at : at + EXTRA, :] = extra.astype(BF16)


def pre_body(heads, place, lat_in, wb_in, wc_in, x_in, cot_in, ld_in, b_out, c_out, cumc_out, cumr_out,
             fresh_out, back_out, table_out, send, mine_out, lat, wb, wc, x, cot, ld, sems):
    pairs = ((ld_in, ld), (lat_in, lat), (wb_in, wb), (wc_in, wc), (x_in, x), (cot_in, cot))
    copies = [pltpu.make_async_copy(src, dst, sems.at[i]) for i, (src, dst) in enumerate(pairs)]
    for copy in copies:
        copy.start()
    rows = lat.shape[0]
    cols = x.shape[1]
    hd = cols // heads
    n = wb.shape[1]
    scale = 1.0 / math.sqrt(n)
    t = lax.broadcasted_iota(jnp.int32, (rows, rows), 0)
    s = lax.broadcasted_iota(jnp.int32, (rows, rows), 1)
    lower = (s <= t).astype(F32)
    copies[0].wait()
    cumc = dot(lower, ld[...], 1, 1, lax.Precision.HIGHEST)
    cumr = dot(ld[...], lower, 1, 1, lax.Precision.HIGHEST)
    cumc_out[...] = cumc
    cumr_out[...] = cumr
    total = cumc[rows - 1 : rows, :]
    tail = jnp.exp(total - cumc)
    rise = jnp.exp(cumc) * scale
    table_out[...] = jnp.zeros_like(table_out)
    totals = []
    for h in range(heads):
        totals.append(jnp.broadcast_to(total[:, h : h + 1], (1, n)))
        table_out[h : h + 1, :] = totals[h]
    put_totals(send, 2 * cols, totals)
    copies[1].wait()
    share = mine_out.shape[1]
    mine_out[...] = lat[:, pl.ds(pl.multiple_of(place[0] * share, share), share)]
    copies[2].wait()
    b = dot(lat[...], wb[...], 1, 0).astype(BF16)
    b_out[...] = b
    copies[3].wait()
    c = dot(lat[...], wc[...], 1, 0).astype(BF16)
    c_out[...] = c
    copies[4].wait()
    copies[5].wait()
    for h in range(heads):
        at = slice(h * hd, (h + 1) * hd)
        xs = (x[:, at].astype(F32) * tail[:, h : h + 1]).astype(BF16)
        gs = (cot[:, at].astype(F32) * rise[:, h : h + 1]).astype(BF16)
        fresh = dot(xs, b, 0, 0)
        back = dot(gs, c, 0, 0)
        fresh_out[at, :] = fresh
        back_out[at, :] = back
        send[at, :] = fresh.astype(BF16)
        send[cols + h * hd : cols + (h + 1) * hd, :] = back.astype(BF16)


def totals_of(got, at):
    total = got[at : at + 1, :].astype(F32)
    for part in (1, 2):
        total = total + got[at + part : at + part + 1, :].astype(F32)
    return total


def pair_body(place, got, fwd, bwd, table, send):
    cols, n = fwd.shape
    slots, hd, _ = send.shape
    hd = hd - EXTRA
    me = place[0]
    late = me % 2
    chip = me // 2
    own = jnp.where(late == 1, table[1:2, :], table[0:1, :])
    theirs = jnp.where(
        late == 1, totals_of(got, 2 * cols + 3), totals_of(got, 2 * cols)
    )
    at = pl.ds(pl.multiple_of(late * hd, hd), hd)
    to = pl.ds(pl.multiple_of(cols + late * hd, hd), hd)
    got_f, got_b = got[at, :].astype(F32), got[to, :].astype(F32)
    by_own, by_theirs = jnp.exp(own), jnp.exp(theirs)
    early = late == 0
    f = jnp.where(early, by_theirs, 1.0) * fwd[at, :] + jnp.where(early, 1.0, by_own) * got_f
    b = jnp.where(early, 1.0, by_theirs) * bwd[at, :] + jnp.where(early, by_own, 1.0) * got_b
    row = lax.broadcasted_iota(jnp.int32, (EXTRA, n), 0)
    extra = jnp.zeros((EXTRA, n), F32)
    for part, value in enumerate(three_parts(own + theirs)):
        extra = jnp.where(row == part, value.astype(F32), extra)
    extra = extra.astype(BF16)
    for slot in range(slots):
        send[slot, :hd, :] = jnp.where(slot > chip, f, b).astype(BF16)
        send[slot, hd:, :] = extra


def scan_body(place, got, pair, fwd, bwd, table, keep, send):
    cols, n = fwd.shape
    slots, hd, _ = got.shape
    hd = hd - EXTRA
    late = place[0] % 2
    chip = place[0] // 2
    early = late == 0
    decays = [jnp.exp(totals_of(got.at[i], hd)) for i in range(slots)]
    state = jnp.zeros((hd, n), F32)
    grad = jnp.zeros((hd, n), F32)
    for i in range(slots):
        used = i < chip
        state = jnp.where(used, decays[i], 1.0) * state
        state = state + jnp.where(used, 1.0, 0.0) * got[i, :hd, :].astype(F32)
    for i in reversed(range(slots)):
        used = i > chip
        grad = jnp.where(used, decays[i], 1.0) * grad
        grad = grad + jnp.where(used, 1.0, 0.0) * got[i, :hd, :].astype(F32)
    by_own = jnp.exp(jnp.where(early, table[0:1, :], table[1:2, :]))
    by_theirs = jnp.exp(
        jnp.where(early, totals_of(pair, 2 * cols), totals_of(pair, 2 * cols + 3))
    )
    at = pl.ds(pl.multiple_of(late * hd, hd), hd)
    to = pl.ds(pl.multiple_of(cols + late * hd, hd), hd)
    after = jnp.where(early, fwd[at, :], pair[at, :].astype(F32))
    after = after + jnp.where(early, by_own, by_theirs) * state
    before = jnp.where(early, pair[to, :].astype(F32), bwd[at, :])
    before = before + jnp.where(early, by_theirs, by_own) * grad
    keep[:hd, :] = jnp.where(early, state, after).astype(BF16)
    keep[hd:, :] = jnp.where(early, before, grad).astype(BF16)
    send[:hd, :] = jnp.where(early, after, state).astype(BF16)
    send[hd:, :] = jnp.where(early, grad, before).astype(BF16)


def attend_body(heads, qb, place, offsets, q, k, v, tail, out):
    rows = q.shape[0]
    hd = q.shape[1] // heads
    w = tail.shape[0]
    scale = 1.0 / math.sqrt(hd)
    i = lax.broadcasted_iota(jnp.int32, (qb, qb + w), 0)
    u = lax.broadcasted_iota(jnp.int32, (qb, qb + w), 1)
    for blk in range(rows // qb):
        off = offsets[0, blk]
        seen = (u <= i + w) & (u >= i + 1 + off)
        if blk == 0:
            seen = seen & ((u >= w) | (place[0] > 0))
        for h in range(heads):
            at = slice(h * hd, (h + 1) * hd)
            if blk == 0:
                keys = jnp.concatenate([tail[:, at], k[:qb, at]], axis=0)
                values = jnp.concatenate(
                    [tail[:, heads * hd + h * hd : heads * hd + (h + 1) * hd], v[:qb, at]], axis=0
                )
            else:
                keys = k[blk * qb - w : (blk + 1) * qb, at]
                values = v[blk * qb - w : (blk + 1) * qb, at]
            scores = dot(q[blk * qb : (blk + 1) * qb, at], keys, 1, 1) * scale
            scores = jnp.where(seen, scores, NEG)
            expo = jnp.exp(scores - jnp.max(scores, axis=-1, keepdims=True))
            probs = (expo / jnp.sum(expo, axis=-1, keepdims=True)).astype(BF16)
            out[blk * qb : (blk + 1) * qb, at] = dot(probs, values, 1, 0)


def local_body(heads, x, cot, b, c, cumc, cumr, inner_out, gx_out, both_out):
    rows = x.shape[0]
    hd = x.shape[1] // heads
    n = b.shape[1]
    scale = 1.0 / math.sqrt(n)
    t = lax.broadcasted_iota(jnp.int32, (rows, rows), 0)
    s = lax.broadcasted_iota(jnp.int32, (rows, rows), 1)
    kern = dot(c[...], b[...], 1, 1) * scale
    weigh = None
    for h in range(heads):
        at = slice(h * hd, (h + 1) * hd)
        gap = cumc[:, h : h + 1] - cumr[h : h + 1, :]
        decay = jnp.exp(jnp.where(s <= t, gap, NEG))
        mixing = (kern * decay).astype(BF16)
        inner_out[:, at] = dot(mixing, x[:, at], 1, 0)
        gx_out[:, at] = dot(mixing, cot[:, at], 0, 0)
        one = dot(cot[:, at], x[:, at], 1, 1) * decay
        weigh = one if weigh is None else weigh + one
    weigh = (weigh * scale).astype(BF16)
    both_out[:, :n] = dot(weigh, c[...], 0, 0)
    both_out[:, n:] = dot(weigh, b[...], 1, 0)


def grads_body(heads, place, keep, got, x, cot, cumc, both, out, enter_out, leave_out):
    rows = x.shape[0]
    cols = x.shape[1]
    hd = cols // heads
    n = keep.shape[1]
    scale = 1.0 / math.sqrt(n)
    gb = both[:, :n]
    gc = both[:, n:]
    for h in range(heads):
        at = slice(h * hd, (h + 1) * hd)
        mine = place[0] % 2 == h
        state = jnp.where(mine, keep[:hd, :].astype(F32), got[:hd, :].astype(F32)).astype(BF16)
        grad = jnp.where(mine, keep[hd:, :].astype(F32), got[hd:, :].astype(F32)).astype(BF16)
        enter_out[at, :] = state
        leave_out[at, :] = grad
        cum = cumc[:, h : h + 1]
        tail = jnp.exp(cumc[rows - 1 : rows, h : h + 1] - cum)
        rise = jnp.exp(cum) * scale
        gb = gb + tail * dot(x[:, at], grad, 1, 0)
        gc = gc + rise * dot(cot[:, at], state, 1, 0)
    piece = out.shape[1]
    gb, gc = gb.astype(BF16), gc.astype(BF16)
    for i in range(out.shape[0]):
        out[i, :, :n] = gb[i * piece : (i + 1) * piece, :]
        out[i, :, n:] = gc[i * piece : (i + 1) * piece, :]


def finish_body(heads, b, c, cumc, inner, gx, attended, enter, leave, layer_out, input_grad):
    rows = b.shape[0]
    hd = inner.shape[1] // heads
    n = b.shape[1]
    scale = 1.0 / math.sqrt(n)
    for h in range(heads):
        at = slice(h * hd, (h + 1) * hd)
        cum = cumc[:, h : h + 1]
        tail = jnp.exp(cumc[rows - 1 : rows, h : h + 1] - cum)
        rise = jnp.exp(cum) * scale
        y = inner[:, at] + rise * dot(c[...], enter[at, :], 1, 1)
        y = y * lax.rsqrt(jnp.mean(y * y, axis=-1, keepdims=True) + 1e-05)
        layer_out[:, at] = (y + attended[:, at]).astype(BF16)
        g = gx[:, at] + tail * dot(b[...], leave[at, :], 1, 1)
        input_grad[:, at] = g.astype(BF16)


def gather_body(scale, got, *rest):
    out = rest[-1]
    total = got[0].astype(F32)
    for i in range(1, got.shape[0]):
        total = total + got[i].astype(F32)
    total = (total * scale).astype(BF16)
    for i in range(out.shape[0]):
        out[i] = total


def project_body(mine, both, out):
    size, rows, cols = both.shape
    term = dot(mine[...], both[...].reshape(size * rows, cols), 0, 0)
    piece = out.shape[1]
    for i in range(out.shape[0]):
        out[i] = term[i * piece : (i + 1) * piece, :].astype(BF16)


def unpack_body(got, out):
    piece = got.shape[1]
    for i in range(got.shape[0]):
        out[i * piece : (i + 1) * piece, :] = got[i].astype(F32)


def shifted(block, axis, distance):
    devices = range(lax.axis_size(axis))
    route = [(i - distance, i) for i in devices if i - distance in devices]
    return lax.ppermute(block, axis, route)


def swapped(block, axis, distance):
    return lax.ppermute(block, axis, [(i, i ^ distance) for i in range(lax.axis_size(axis))])


def summed(pieces, axes, scale=1.0, beside=()):
    got = lax.all_to_all(pieces, axes, 0, 0)
    copies = call(
        functools.partial(gather_body, scale),
        [(pieces.shape, BF16)],
        (got, *(pltpu.with_memory_space_constraint(a, pltpu.HBM) for a in beside)),
        [VMEM] + [HBM] * len(beside),
    )[0]
    return lax.all_to_all(copies, axes, 0, 0)


def on_device(latents, proj_input, proj_output, scan_input, log_decay, att_queries, att_keys,
              att_values, scan_cotangent, window_offsets):
    _, rows, width = latents.shape
    heads = log_decay.shape[2]
    cols = scan_input.shape[2]
    hd = cols // heads
    n = proj_input.shape[1]
    share = width // lax.axis_size("space")
    assert heads == 2
    tm = lax.axis_size("tm")
    me = lax.axis_index("tm")
    lat, x, ld = latents[0], scan_input[0], log_decay[0].T
    q, k, v, cot = att_queries[0], att_keys[0], att_values[0], scan_cotangent[0]

    inputs = [
        pltpu.with_memory_space_constraint(a, pltpu.HBM)
        for a in (lat, proj_input, proj_output, x, cot, ld)
    ]
    tails = shifted(jnp.concatenate([k[rows - W :], v[rows - W :]], axis=1), "tm", 1)
    state = ((cols, n), F32)
    wire = ((2 * cols + EXTRA, n), BF16)
    b, c, cumc, cumr, fwd, bwd, table, send, mine = call(
        functools.partial(pre_body, heads),
        [((rows, n), BF16), ((rows, n), BF16), ((rows, heads), F32), ((heads, rows), F32), state, state,
         ((24, n), F32), wire, ((rows, share), BF16)],
        (lax.axis_index("space")[None], *inputs),
        [SMEM] + [HBM] * 6,
        [pltpu.VMEM(a.shape, a.dtype) for a in inputs] + [pltpu.SemaphoreType.DMA((6,))],
        flops=2 * rows * width * 2 * n + 4 * rows * cols * n,
    )
    attended = call(
        functools.partial(attend_body, heads, QB),
        [((rows, cols), F32)],
        (me[None], window_offsets, q, k, v, tails),
        [SMEM, SMEM] + [VMEM] * 4,
        flops=4 * rows * 2 * W * cols,
        transcendentals=rows * 2 * W * heads,
    )[0]
    inner, gx, both = call(
        functools.partial(local_body, heads),
        [((rows, cols), F32), ((rows, cols), F32), ((rows, 2 * n), F32)],
        (x, cot, b, c, cumc, cumr),
        flops=8 * rows * rows * cols,
        transcendentals=rows * rows * heads,
    )
    pair = swapped(send, "tm", 1)
    spread = call(
        pair_body,
        [((tm // 2, hd + EXTRA, n), BF16)],
        (me[None], pair, fwd, bwd, table),
        [SMEM] + [VMEM] * 4,
    )[0]
    same_core = [list(range(core, tm, 2)) for core in range(2)]
    got = lax.all_to_all(spread, "tm", 0, 0, axis_index_groups=same_core)
    keep, send = call(
        scan_body,
        [((2 * hd, n), BF16), ((2 * hd, n), BF16)],
        (me[None], got, pair, fwd, bwd, table),
        [SMEM] + [VMEM] * 5,
    )
    got = swapped(send, "tm", 1)
    space = lax.axis_size("space")
    both, enter, leave = call(
        functools.partial(grads_body, heads),
        [((space, rows // space, 2 * n), BF16), ((cols, n), BF16), ((cols, n), BF16)],
        (me[None], keep, got, x, cot, cumc, both),
        [SMEM] + [VMEM] * 6,
        flops=4 * rows * cols * n,
    )
    layer_out, input_grad = call(
        functools.partial(finish_body, heads),
        [((rows, cols), BF16), ((rows, cols), BF16)],
        (b, c, cumc, inner, gx, attended, enter, leave),
        flops=4 * rows * cols * n,
    )
    both = summed(both, ("space",), beside=(layer_out,))
    others = tm * lax.axis_size("dp")
    term = call(
        project_body,
        [((others, share // others, 2 * n), BF16)],
        (mine, both),
        flops=2 * rows * share * 2 * n,
    )[0]
    term = summed(term, ("tm", "dp"), 1.0 / math.sqrt(rows * others))
    proj_grad = call(unpack_body, [((share, 2 * n), F32)], (term,))[0]
    return layer_out[None], input_grad[None], proj_grad


def solution(mesh):
    wide = P("dp", "tm", "space")
    return jax.shard_map(
        on_device,
        mesh=mesh,
        in_specs=(P("dp", "tm", None), P(), P(), wide, wide, wide, wide, wide, wide, P("dp", "tm")),
        out_specs=(wide, wide, P("space", None)),
        check_vma=False,
    )
```

```python
import functools
import math

import jax
import jax.numpy as jnp
from jax import lax
from jax.experimental import pallas as pl
from jax.experimental.pallas import tpu as pltpu
from jax.sharding import PartitionSpec as P

W = 128
QB = 128
F32 = jnp.float32
BF16 = jnp.bfloat16
VMEM = pl.BlockSpec(memory_space=pltpu.VMEM)
HBM = pl.BlockSpec(memory_space=pltpu.HBM)
SMEM = pl.BlockSpec(memory_space=pltpu.SMEM)
NEG = -1e30
EXTRA = 16
CHUNKS = 4


def dot(a, b, left, right, precision=None):
    return lax.dot_general(
        a, b, (((left,), (right,)), ((), ())), preferred_element_type=F32, precision=precision
    )


def call(body, out, args, specs=None, scratch=(), flops=0, transcendentals=0, moved=0):
    return pl.pallas_call(
        body,
        out_shape=[jax.ShapeDtypeStruct(s, t) for s, t in out],
        in_specs=specs or [VMEM] * len(args),
        out_specs=[VMEM] * len(out),
        scratch_shapes=scratch,
        compiler_params=pltpu.CompilerParams(vmem_limit_bytes=40 * 2**20),
        cost_estimate=pl.CostEstimate(
            flops=flops, transcendentals=transcendentals, bytes_accessed=moved
        ),
    )(*args)


def three_parts(value):
    high = value.astype(BF16)
    rest = value - high.astype(F32)
    middle = rest.astype(BF16)
    return high, middle, (rest - middle.astype(F32)).astype(BF16)


def put_totals(send, at, totals):
    row = lax.broadcasted_iota(jnp.int32, (EXTRA, send.shape[1]), 0)
    extra = jnp.zeros((EXTRA, send.shape[1]), F32)
    for h, total in enumerate(totals):
        for part, value in enumerate(three_parts(total)):
            extra = jnp.where(row == 3 * h + part, value.astype(F32), extra)
    send[at : at + EXTRA, :] = extra.astype(BF16)


def pre_body(heads, place, lat_in, wb_in, wc_in, x_in, cot_in, ld_in, b_out, c_out, cumc_out, cumr_out,
             fresh_out, back_out, table_out, send, mine_out, lat, w, x, cot, ld, sems):
    n = wb_in.shape[1]
    chunks = CHUNKS
    deep = lat.shape[1] // chunks
    pairs = [(ld_in, ld)]
    for i in range(chunks):
        part = slice(i * deep, (i + 1) * deep)
        pairs.append((wb_in.at[part, :], w.at[part, :n]))
        pairs.append((wc_in.at[part, :], w.at[part, n:]))
        pairs.append((lat_in.at[:, part], lat.at[:, part]))
    pairs += [(x_in, x), (cot_in, cot)]
    copies = [pltpu.make_async_copy(src, dst, sems.at[i]) for i, (src, dst) in enumerate(pairs)]
    for copy in copies:
        copy.start()
    rows = lat.shape[0]
    cols = x.shape[1]
    hd = cols // heads
    scale = 1.0 / math.sqrt(n)
    t = lax.broadcasted_iota(jnp.int32, (rows, rows), 0)
    s = lax.broadcasted_iota(jnp.int32, (rows, rows), 1)
    lower = (s <= t).astype(F32)
    copies[0].wait()
    cumc = dot(lower, ld[...], 1, 1, lax.Precision.HIGHEST)
    cumr = dot(ld[...], lower, 1, 1, lax.Precision.HIGHEST)
    cumc_out[...] = cumc
    cumr_out[...] = cumr
    total = cumc[rows - 1 : rows, :]
    tail = jnp.exp(total - cumc)
    rise = jnp.exp(cumc) * scale
    table_out[...] = jnp.zeros_like(table_out)
    totals = []
    for h in range(heads):
        totals.append(jnp.broadcast_to(total[:, h : h + 1], (1, n)))
        table_out[h : h + 1, :] = totals[h]
    put_totals(send, 2 * cols, totals)
    projected = None
    for i in range(chunks):
        for copy in copies[1 + 3 * i : 4 + 3 * i]:
            copy.wait()
        part = slice(i * deep, (i + 1) * deep)
        one = dot(lat[:, part], w[part, :], 1, 0)
        projected = one if projected is None else projected + one
    b = projected[:, :n].astype(BF16)
    c = projected[:, n:].astype(BF16)
    b_out[...] = b
    c_out[...] = c
    for copy in copies[-2:]:
        copy.wait()
    share = mine_out.shape[1]
    mine_out[...] = lat[:, pl.ds(pl.multiple_of(place[0] * share, share), share)]
    for h in range(heads):
        at = slice(h * hd, (h + 1) * hd)
        xs = (x[:, at].astype(F32) * tail[:, h : h + 1]).astype(BF16)
        gs = (cot[:, at].astype(F32) * rise[:, h : h + 1]).astype(BF16)
        fresh = dot(xs, b, 0, 0)
        back = dot(gs, c, 0, 0)
        fresh_out[at, :] = fresh
        back_out[at, :] = back
        send[at, :] = fresh.astype(BF16)
        send[cols + h * hd : cols + (h + 1) * hd, :] = back.astype(BF16)


def totals_of(got, at):
    total = got[at : at + 1, :].astype(F32)
    for part in (1, 2):
        total = total + got[at + part : at + part + 1, :].astype(F32)
    return total


def pair_body(place, got, fwd, bwd, table, _, send):
    cols, n = fwd.shape
    slots, hd, _ = send.shape
    hd = hd - EXTRA
    me = place[0]
    late = me % 2
    chip = me // 2
    own = jnp.where(late == 1, table[1:2, :], table[0:1, :])
    theirs = jnp.where(
        late == 1, totals_of(got, 2 * cols + 3), totals_of(got, 2 * cols)
    )
    at = pl.ds(pl.multiple_of(late * hd, hd), hd)
    to = pl.ds(pl.multiple_of(cols + late * hd, hd), hd)
    got_f, got_b = got[at, :].astype(F32), got[to, :].astype(F32)
    by_own, by_theirs = jnp.exp(own), jnp.exp(theirs)
    early = late == 0
    f = jnp.where(early, by_theirs, 1.0) * fwd[at, :] + jnp.where(early, 1.0, by_own) * got_f
    b = jnp.where(early, 1.0, by_theirs) * bwd[at, :] + jnp.where(early, by_own, 1.0) * got_b
    row = lax.broadcasted_iota(jnp.int32, (EXTRA, n), 0)
    extra = jnp.zeros((EXTRA, n), F32)
    for part, value in enumerate(three_parts(own + theirs)):
        extra = jnp.where(row == part, value.astype(F32), extra)
    extra = extra.astype(BF16)
    for slot in range(slots):
        send[slot, :hd, :] = jnp.where(slot > chip, f, b).astype(BF16)
        send[slot, hd:, :] = extra


def scan_body(place, got, pair, fwd, bwd, table, keep, send):
    cols, n = fwd.shape
    slots, hd, _ = got.shape
    hd = hd - EXTRA
    late = place[0] % 2
    chip = place[0] // 2
    early = late == 0
    decays = [jnp.exp(totals_of(got.at[i], hd)) for i in range(slots)]
    state = jnp.zeros((hd, n), F32)
    grad = jnp.zeros((hd, n), F32)
    for i in range(slots):
        used = i < chip
        state = jnp.where(used, decays[i], 1.0) * state
        state = state + jnp.where(used, 1.0, 0.0) * got[i, :hd, :].astype(F32)
    for i in reversed(range(slots)):
        used = i > chip
        grad = jnp.where(used, decays[i], 1.0) * grad
        grad = grad + jnp.where(used, 1.0, 0.0) * got[i, :hd, :].astype(F32)
    by_own = jnp.exp(jnp.where(early, table[0:1, :], table[1:2, :]))
    by_theirs = jnp.exp(
        jnp.where(early, totals_of(pair, 2 * cols), totals_of(pair, 2 * cols + 3))
    )
    at = pl.ds(pl.multiple_of(late * hd, hd), hd)
    to = pl.ds(pl.multiple_of(cols + late * hd, hd), hd)
    after = jnp.where(early, fwd[at, :], pair[at, :].astype(F32))
    after = after + jnp.where(early, by_own, by_theirs) * state
    before = jnp.where(early, pair[to, :].astype(F32), bwd[at, :])
    before = before + jnp.where(early, by_theirs, by_own) * grad
    keep[:hd, :] = jnp.where(early, state, after).astype(BF16)
    keep[hd:, :] = jnp.where(early, before, grad).astype(BF16)
    send[:hd, :] = jnp.where(early, after, state).astype(BF16)
    send[hd:, :] = jnp.where(early, grad, before).astype(BF16)


def attend_body(heads, qb, place, offsets_in, q, k, v, tail, out, offsets, sem):
    copy = pltpu.make_async_copy(offsets_in, offsets, sem)
    copy.start()
    rows = q.shape[0]
    hd = q.shape[1] // heads
    w = tail.shape[0]
    scale = 1.0 / math.sqrt(hd)
    i = lax.broadcasted_iota(jnp.int32, (qb, qb + w), 0)
    u = lax.broadcasted_iota(jnp.int32, (qb, qb + w), 1)

    def window(own, blk, at, behind):
        if blk == 0:
            return jnp.concatenate([tail[:, behind], own[:qb, at]], axis=0)
        return own[blk * qb - w : (blk + 1) * qb, at]

    places = [(blk, h) for blk in range(rows // qb) for h in range(heads)]
    scores = []
    for blk, h in places:
        at = slice(h * hd, (h + 1) * hd)
        keys = window(k, blk, at, at)
        scores.append(dot(q[blk * qb : (blk + 1) * qb, at], keys, 1, 1) * scale)
    copy.wait()
    for (blk, h), score in zip(places, scores):
        at = slice(h * hd, (h + 1) * hd)
        seen = (u <= i + w) & (u >= i + 1 + offsets[0, blk])
        if blk == 0:
            seen = seen & ((u >= w) | (place[0] > 0))
        score = jnp.where(seen, score, NEG)
        expo = jnp.exp(score - jnp.max(score, axis=-1, keepdims=True))
        probs = (expo / jnp.sum(expo, axis=-1, keepdims=True)).astype(BF16)
        values = window(v, blk, at, slice((heads + h) * hd, (heads + h + 1) * hd))
        out[blk * qb : (blk + 1) * qb, at] = dot(probs, values, 1, 0)


def local_body(heads, x, cot, b, c, cumc, cumr, inner_out, gx_out, both_out, token):
    token[...] = jnp.zeros_like(token)
    rows = x.shape[0]
    hd = x.shape[1] // heads
    n = b.shape[1]
    scale = 1.0 / math.sqrt(n)
    t = lax.broadcasted_iota(jnp.int32, (rows, rows), 0)
    s = lax.broadcasted_iota(jnp.int32, (rows, rows), 1)
    kern = dot(c[...], b[...], 1, 1) * scale
    weigh = None
    for h in range(heads):
        at = slice(h * hd, (h + 1) * hd)
        gap = cumc[:, h : h + 1] - cumr[h : h + 1, :]
        decay = jnp.exp(jnp.where(s <= t, gap, NEG))
        mixing = (kern * decay).astype(BF16)
        inner_out[:, at] = dot(mixing, x[:, at], 1, 0)
        gx_out[:, at] = dot(mixing, cot[:, at], 0, 0)
        one = dot(cot[:, at], x[:, at], 1, 1) * decay
        weigh = one if weigh is None else weigh + one
    weigh = (weigh * scale).astype(BF16)
    both_out[:, :n] = dot(weigh, c[...], 0, 0)
    both_out[:, n:] = dot(weigh, b[...], 1, 0)


def grads_body(heads, place, keep, got, x, cot, cumc, both, out, enter_out, leave_out):
    rows = x.shape[0]
    cols = x.shape[1]
    hd = cols // heads
    n = keep.shape[1]
    scale = 1.0 / math.sqrt(n)
    gb = both[:, :n]
    gc = both[:, n:]
    for h in range(heads):
        at = slice(h * hd, (h + 1) * hd)
        mine = place[0] % 2 == h
        state = jnp.where(mine, keep[:hd, :].astype(F32), got[:hd, :].astype(F32)).astype(BF16)
        grad = jnp.where(mine, keep[hd:, :].astype(F32), got[hd:, :].astype(F32)).astype(BF16)
        enter_out[at, :] = state
        leave_out[at, :] = grad
        cum = cumc[:, h : h + 1]
        tail = jnp.exp(cumc[rows - 1 : rows, h : h + 1] - cum)
        rise = jnp.exp(cum) * scale
        gb = gb + tail * dot(x[:, at], grad, 1, 0)
        gc = gc + rise * dot(cot[:, at], state, 1, 0)
    piece = out.shape[1]
    gb, gc = gb.astype(BF16), gc.astype(BF16)
    for i in range(out.shape[0]):
        out[i, :, :n] = gb[i * piece : (i + 1) * piece, :]
        out[i, :, n:] = gc[i * piece : (i + 1) * piece, :]


def finish_body(heads, b, c, cumc, inner, gx, attended, enter, leave, layer_out, input_grad):
    rows = b.shape[0]
    hd = inner.shape[1] // heads
    n = b.shape[1]
    scale = 1.0 / math.sqrt(n)
    for h in range(heads):
        at = slice(h * hd, (h + 1) * hd)
        cum = cumc[:, h : h + 1]
        tail = jnp.exp(cumc[rows - 1 : rows, h : h + 1] - cum)
        rise = jnp.exp(cum) * scale
        y = inner[:, at] + rise * dot(c[...], enter[at, :], 1, 1)
        y = y * lax.rsqrt(jnp.mean(y * y, axis=-1, keepdims=True) + 1e-05)
        layer_out[:, at] = (y + attended[:, at]).astype(BF16)
        g = gx[:, at] + tail * dot(b[...], leave[at, :], 1, 1)
        input_grad[:, at] = g.astype(BF16)


def gather_body(scale, got, *rest):
    out = rest[-1]
    total = got[0].astype(F32)
    for i in range(1, got.shape[0]):
        total = total + got[i].astype(F32)
    total = (total * scale).astype(BF16)
    for i in range(out.shape[0]):
        out[i] = total


def project_body(mine, both, out):
    size, rows, cols = both.shape
    term = dot(mine[...], both[...].reshape(size * rows, cols), 0, 0)
    piece = out.shape[1]
    for i in range(out.shape[0]):
        out[i] = term[i * piece : (i + 1) * piece, :].astype(BF16)


def unpack_body(got, out):
    piece = got.shape[1]
    for i in range(got.shape[0]):
        out[i * piece : (i + 1) * piece, :] = got[i].astype(F32)


def shifted(block, axis, distance):
    devices = range(lax.axis_size(axis))
    route = [(i - distance, i) for i in devices if i - distance in devices]
    return lax.ppermute(block, axis, route)


def swapped(block, axis, distance):
    return lax.ppermute(block, axis, [(i, i ^ distance) for i in range(lax.axis_size(axis))])


def gathered(scale, got, copies, beside=()):
    return call(
        functools.partial(gather_body, scale),
        [((copies, *got.shape[1:]), BF16)],
        (got, *(pltpu.with_memory_space_constraint(a, pltpu.HBM) for a in beside)),
        [VMEM] + [HBM] * len(beside),
    )[0]


def summed(pieces, axes, scale=1.0):
    got = lax.all_to_all(pieces, axes, 0, 0)
    return lax.all_to_all(gathered(scale, got, pieces.shape[0]), axes, 0, 0)


def summed_in_groups(pieces, axis, beside):
    near = pieces.shape[0]
    far = lax.axis_size(axis) // near
    inside = [[near * g + i for i in range(near)] for g in range(far)]
    across = [[i + near * g for g in range(far)] for i in range(near)]
    got = lax.all_to_all(pieces, axis, 0, 0, axis_index_groups=inside)
    got = lax.all_to_all(gathered(1.0, got, far), axis, 0, 0, axis_index_groups=across)
    return lax.all_to_all(gathered(1.0, got, near, beside), axis, 0, 0, axis_index_groups=inside)


def on_device(latents, proj_input, proj_output, scan_input, log_decay, att_queries, att_keys,
              att_values, scan_cotangent, window_offsets):
    _, rows, width = latents.shape
    heads = log_decay.shape[2]
    cols = scan_input.shape[2]
    hd = cols // heads
    n = proj_input.shape[1]
    share = width // lax.axis_size("space")
    assert heads == 2
    tm = lax.axis_size("tm")
    me = lax.axis_index("tm")
    lat, x, ld = latents[0], scan_input[0], log_decay[0].T
    q, k, v, cot = att_queries[0], att_keys[0], att_values[0], scan_cotangent[0]

    inputs = [
        pltpu.with_memory_space_constraint(a, pltpu.HBM)
        for a in (lat, proj_input, proj_output, x, cot, ld)
    ]
    tails = shifted(jnp.concatenate([k[rows - W :], v[rows - W :]], axis=1), "tm", 1)
    state = ((cols, n), F32)
    wire = ((2 * cols + EXTRA, n), BF16)
    b, c, cumc, cumr, fwd, bwd, table, send, mine = call(
        functools.partial(pre_body, heads),
        [((rows, n), BF16), ((rows, n), BF16), ((rows, heads), F32), ((heads, rows), F32), state, state,
         ((24, n), F32), wire, ((rows, share), BF16)],
        (lax.axis_index("space")[None], *inputs),
        [SMEM] + [HBM] * 6,
        [
            pltpu.VMEM((rows, width), BF16),
            pltpu.VMEM((width, 2 * n), BF16),
            pltpu.VMEM((rows, cols), BF16),
            pltpu.VMEM((rows, cols), BF16),
            pltpu.VMEM((heads, rows), F32),
            pltpu.SemaphoreType.DMA((3 * CHUNKS + 3,)),
        ],
        flops=2 * rows * width * 2 * n + 4 * rows * cols * n,
    )
    attended = call(
        functools.partial(attend_body, heads, QB),
        [((rows, cols), F32)],
        (me[None], pltpu.with_memory_space_constraint(window_offsets, pltpu.HBM), q, k, v, tails),
        [SMEM, HBM] + [VMEM] * 4,
        [pltpu.SMEM(window_offsets.shape, jnp.int32), pltpu.SemaphoreType.DMA],
        flops=4 * rows * 2 * W * cols,
        transcendentals=rows * 2 * W * heads,
    )[0]
    inner, gx, both, token = call(
        functools.partial(local_body, heads),
        [((rows, cols), F32), ((rows, cols), F32), ((rows, 2 * n), F32), ((8, n), F32)],
        (x, cot, b, c, cumc, cumr),
        flops=8 * rows * rows * cols,
        transcendentals=rows * rows * heads,
    )
    pair = swapped(send, "tm", 1)
    spread = call(
        pair_body,
        [((tm // 2, hd + EXTRA, n), BF16)],
        (me[None], pair, fwd, bwd, table, token),
        [SMEM] + [VMEM] * 5,
    )[0]
    same_core = [list(range(core, tm, 2)) for core in range(2)]
    got = lax.all_to_all(spread, "tm", 0, 0, axis_index_groups=same_core)
    keep, send = call(
        scan_body,
        [((2 * hd, n), BF16), ((2 * hd, n), BF16)],
        (me[None], got, pair, fwd, bwd, table),
        [SMEM] + [VMEM] * 5,
    )
    got = swapped(send, "tm", 1)
    near = math.gcd(lax.axis_size("space"), 4)
    both, enter, leave = call(
        functools.partial(grads_body, heads),
        [((near, rows // near, 2 * n), BF16), ((cols, n), BF16), ((cols, n), BF16)],
        (me[None], keep, got, x, cot, cumc, both),
        [SMEM] + [VMEM] * 6,
        flops=4 * rows * cols * n,
    )
    layer_out, input_grad = call(
        functools.partial(finish_body, heads),
        [((rows, cols), BF16), ((rows, cols), BF16)],
        (b, c, cumc, inner, gx, attended, enter, leave),
        flops=4 * rows * cols * n,
    )
    both = summed_in_groups(both, "space", (layer_out,))
    others = tm * lax.axis_size("dp")
    term = call(
        project_body,
        [((others, share // others, 2 * n), BF16)],
        (mine, both),
        flops=2 * rows * share * 2 * n,
    )[0]
    term = summed(term, ("tm", "dp"), 1.0 / math.sqrt(rows * others))
    proj_grad = call(unpack_body, [((share, 2 * n), F32)], (term,))[0]
    return layer_out[None], input_grad[None], proj_grad


def solution(mesh):
    wide = P("dp", "tm", "space")
    return jax.shard_map(
        on_device,
        mesh=mesh,
        in_specs=(P("dp", "tm", None), P(), P(), wide, wide, wide, wide, wide, wide, P("dp", "tm")),
        out_specs=(wide, wide, P("space", None)),
        check_vma=False,
    )
```

```python
import functools
import math

import jax
import jax.numpy as jnp
from jax import lax
from jax.experimental import pallas as pl
from jax.experimental.pallas import tpu as pltpu
from jax.sharding import PartitionSpec as P

W = 128
QB = 128
F32 = jnp.float32
BF16 = jnp.bfloat16
VMEM = pl.BlockSpec(memory_space=pltpu.VMEM)
HBM = pl.BlockSpec(memory_space=pltpu.HBM)
SMEM = pl.BlockSpec(memory_space=pltpu.SMEM)
NEG = -1e30
EXTRA = 16
CHUNKS = 2


def dot(a, b, left, right, precision=None):
    return lax.dot_general(
        a, b, (((left,), (right,)), ((), ())), preferred_element_type=F32, precision=precision
    )


def call(body, out, args, specs=None, scratch=(), flops=0, transcendentals=0, moved=0):
    return pl.pallas_call(
        body,
        out_shape=[jax.ShapeDtypeStruct(s, t) for s, t in out],
        in_specs=specs or [VMEM] * len(args),
        out_specs=[VMEM] * len(out),
        scratch_shapes=scratch,
        compiler_params=pltpu.CompilerParams(vmem_limit_bytes=40 * 2**20),
        cost_estimate=pl.CostEstimate(
            flops=flops, transcendentals=transcendentals, bytes_accessed=moved
        ),
    )(*args)


def three_parts(value):
    high = value.astype(BF16)
    rest = value - high.astype(F32)
    middle = rest.astype(BF16)
    return high, middle, (rest - middle.astype(F32)).astype(BF16)


def put_totals(send, at, totals):
    row = lax.broadcasted_iota(jnp.int32, (EXTRA, send.shape[1]), 0)
    extra = jnp.zeros((EXTRA, send.shape[1]), F32)
    for h, total in enumerate(totals):
        for part, value in enumerate(three_parts(total)):
            extra = jnp.where(row == 3 * h + part, value.astype(F32), extra)
    send[at : at + EXTRA, :] = extra.astype(BF16)


def pre_body(heads, place, lat_in, wb_in, wc_in, x_in, cot_in, ld_in, b_out, c_out, cumc_out, cumr_out,
             fresh_out, back_out, table_out, send, mine_out, lat, w, x, cot, ld, sems):
    n = wb_in.shape[1]
    chunks = CHUNKS
    deep = lat.shape[1] // chunks
    pairs = [(ld_in, ld), (x_in, x), (cot_in, cot)]
    for i in range(chunks):
        part = slice(i * deep, (i + 1) * deep)
        pairs.append((wb_in.at[part, :], w.at[part, :n]))
        pairs.append((wc_in.at[part, :], w.at[part, n:]))
        pairs.append((lat_in.at[:, part], lat.at[:, part]))
    copies = [pltpu.make_async_copy(src, dst, sems.at[i]) for i, (src, dst) in enumerate(pairs)]
    for copy in copies:
        copy.start()
    rows = lat.shape[0]
    cols = x.shape[1]
    hd = cols // heads
    scale = 1.0 / math.sqrt(n)
    down = lax.broadcasted_iota(jnp.int32, (rows, rows), 0)
    along = lax.broadcasted_iota(jnp.int32, (rows, rows), 1)
    copies[0].wait()
    cumr = dot(ld[...], (down <= along).astype(F32), 1, 0, lax.Precision.HIGHEST)
    cumc = dot((along <= down).astype(F32), ld[...], 1, 1, lax.Precision.HIGHEST)
    cumc_out[...] = cumc
    cumr_out[...] = cumr
    tail = jnp.exp(cumr[:, rows - 1 : rows] - cumr)
    rise = jnp.exp(cumr) * scale
    table_out[...] = jnp.zeros_like(table_out)
    totals = []
    for h in range(heads):
        totals.append(jnp.broadcast_to(cumc[rows - 1 : rows, h : h + 1], (1, n)))
        table_out[h : h + 1, :] = totals[h]
    put_totals(send, 2 * cols, totals)
    copies[1].wait()
    copies[2].wait()
    decayed = []
    for h in range(heads):
        at = slice(h * hd, (h + 1) * hd)
        xs = (x[:, at].astype(F32).T * tail[h : h + 1, :]).astype(BF16)
        gs = (cot[:, at].astype(F32).T * rise[h : h + 1, :]).astype(BF16)
        decayed.append((xs, gs))
    projected = None
    for i in range(chunks):
        for copy in copies[3 + 3 * i : 6 + 3 * i]:
            copy.wait()
        part = slice(i * deep, (i + 1) * deep)
        one = dot(lat[:, part], w[part, :], 1, 0)
        projected = one if projected is None else projected + one
    b = projected[:, :n].astype(BF16)
    c = projected[:, n:].astype(BF16)
    for h, (xs, gs) in enumerate(decayed):
        at = slice(h * hd, (h + 1) * hd)
        fresh = dot(xs, b, 1, 0)
        back = dot(gs, c, 1, 0)
        fresh_out[at, :] = fresh
        back_out[at, :] = back
        send[at, :] = fresh.astype(BF16)
        send[cols + h * hd : cols + (h + 1) * hd, :] = back.astype(BF16)
    b_out[...] = b
    c_out[...] = c
    share = mine_out.shape[1]
    mine_out[...] = lat[:, pl.ds(pl.multiple_of(place[0] * share, share), share)]


def totals_of(got, at):
    total = got[at : at + 1, :].astype(F32)
    for part in (1, 2):
        total = total + got[at + part : at + part + 1, :].astype(F32)
    return total


def pair_body(place, got, fwd, bwd, table, _, send):
    cols, n = fwd.shape
    slots, hd, _ = send.shape
    hd = hd - EXTRA
    me = place[0]
    late = me % 2
    chip = me // 2
    own = jnp.where(late == 1, table[1:2, :], table[0:1, :])
    theirs = jnp.where(
        late == 1, totals_of(got, 2 * cols + 3), totals_of(got, 2 * cols)
    )
    at = pl.ds(pl.multiple_of(late * hd, hd), hd)
    to = pl.ds(pl.multiple_of(cols + late * hd, hd), hd)
    got_f, got_b = got[at, :].astype(F32), got[to, :].astype(F32)
    by_own, by_theirs = jnp.exp(own), jnp.exp(theirs)
    early = late == 0
    f = jnp.where(early, by_theirs, 1.0) * fwd[at, :] + jnp.where(early, 1.0, by_own) * got_f
    b = jnp.where(early, 1.0, by_theirs) * bwd[at, :] + jnp.where(early, by_own, 1.0) * got_b
    row = lax.broadcasted_iota(jnp.int32, (EXTRA, n), 0)
    extra = jnp.zeros((EXTRA, n), F32)
    for part, value in enumerate(three_parts(own + theirs)):
        extra = jnp.where(row == part, value.astype(F32), extra)
    extra = extra.astype(BF16)
    for slot in range(slots):
        send[slot, :hd, :] = jnp.where(slot > chip, f, b).astype(BF16)
        send[slot, hd:, :] = extra


def scan_body(place, got, pair, fwd, bwd, table, keep, send):
    cols, n = fwd.shape
    slots, hd, _ = got.shape
    hd = hd - EXTRA
    late = place[0] % 2
    chip = place[0] // 2
    early = late == 0
    decays = [jnp.exp(totals_of(got.at[i], hd)) for i in range(slots)]
    state = jnp.zeros((hd, n), F32)
    grad = jnp.zeros((hd, n), F32)
    for i in range(slots):
        used = i < chip
        state = jnp.where(used, decays[i], 1.0) * state
        state = state + jnp.where(used, 1.0, 0.0) * got[i, :hd, :].astype(F32)
    for i in reversed(range(slots)):
        used = i > chip
        grad = jnp.where(used, decays[i], 1.0) * grad
        grad = grad + jnp.where(used, 1.0, 0.0) * got[i, :hd, :].astype(F32)
    by_own = jnp.exp(jnp.where(early, table[0:1, :], table[1:2, :]))
    by_theirs = jnp.exp(
        jnp.where(early, totals_of(pair, 2 * cols), totals_of(pair, 2 * cols + 3))
    )
    at = pl.ds(pl.multiple_of(late * hd, hd), hd)
    to = pl.ds(pl.multiple_of(cols + late * hd, hd), hd)
    after = jnp.where(early, fwd[at, :], pair[at, :].astype(F32))
    after = after + jnp.where(early, by_own, by_theirs) * state
    before = jnp.where(early, pair[to, :].astype(F32), bwd[at, :])
    before = before + jnp.where(early, by_theirs, by_own) * grad
    keep[:hd, :] = jnp.where(early, state, after).astype(BF16)
    keep[hd:, :] = jnp.where(early, before, grad).astype(BF16)
    send[:hd, :] = jnp.where(early, after, state).astype(BF16)
    send[hd:, :] = jnp.where(early, grad, before).astype(BF16)


def attend_body(heads, qb, place, offsets_in, q, k, v, tail, out, offsets, sem):
    copy = pltpu.make_async_copy(offsets_in, offsets, sem)
    copy.start()
    rows = q.shape[0]
    hd = q.shape[1] // heads
    w = tail.shape[0]
    scale = 1.0 / math.sqrt(hd)
    i = lax.broadcasted_iota(jnp.int32, (qb, qb + w), 0)
    u = lax.broadcasted_iota(jnp.int32, (qb, qb + w), 1)

    def window(own, blk, at, behind):
        if blk == 0:
            return jnp.concatenate([tail[:, behind], own[:qb, at]], axis=0)
        return own[blk * qb - w : (blk + 1) * qb, at]

    places = [(blk, h) for blk in range(rows // qb) for h in range(heads)]
    scores = []
    for blk, h in places:
        at = slice(h * hd, (h + 1) * hd)
        keys = window(k, blk, at, at)
        scores.append(dot(q[blk * qb : (blk + 1) * qb, at], keys, 1, 1) * scale)
    copy.wait()
    for (blk, h), score in zip(places, scores):
        at = slice(h * hd, (h + 1) * hd)
        seen = (u <= i + w) & (u >= i + 1 + offsets[0, blk])
        if blk == 0:
            seen = seen & ((u >= w) | (place[0] > 0))
        score = jnp.where(seen, score, NEG)
        expo = jnp.exp(score - jnp.max(score, axis=-1, keepdims=True))
        probs = (expo / jnp.sum(expo, axis=-1, keepdims=True)).astype(BF16)
        values = window(v, blk, at, slice((heads + h) * hd, (heads + h + 1) * hd))
        out[blk * qb : (blk + 1) * qb, at] = dot(probs, values, 1, 0)


def local_body(heads, x, cot, b, c, cumc, cumr, inner_out, gx_out, both_out, token):
    token[...] = jnp.zeros_like(token)
    rows = x.shape[0]
    hd = x.shape[1] // heads
    n = b.shape[1]
    scale = 1.0 / math.sqrt(n)
    t = lax.broadcasted_iota(jnp.int32, (rows, rows), 0)
    s = lax.broadcasted_iota(jnp.int32, (rows, rows), 1)
    kern = dot(c[...], b[...], 1, 1) * scale
    weigh = None
    for h in range(heads):
        at = slice(h * hd, (h + 1) * hd)
        gap = cumc[:, h : h + 1] - cumr[h : h + 1, :]
        decay = jnp.exp(jnp.where(s <= t, gap, NEG))
        mixing = (kern * decay).astype(BF16)
        inner_out[:, at] = dot(mixing, x[:, at], 1, 0)
        gx_out[:, at] = dot(mixing, cot[:, at], 0, 0)
        one = dot(cot[:, at], x[:, at], 1, 1) * decay
        weigh = one if weigh is None else weigh + one
    weigh = (weigh * scale).astype(BF16)
    both_out[:, :n] = dot(weigh, c[...], 0, 0)
    both_out[:, n:] = dot(weigh, b[...], 1, 0)


def grads_body(heads, place, keep, got, x, cot, cumc, both, out, enter_out, leave_out):
    rows = x.shape[0]
    cols = x.shape[1]
    hd = cols // heads
    n = keep.shape[1]
    scale = 1.0 / math.sqrt(n)
    gb = both[:, :n]
    gc = both[:, n:]
    for h in range(heads):
        at = slice(h * hd, (h + 1) * hd)
        mine = place[0] % 2 == h
        state = jnp.where(mine, keep[:hd, :].astype(F32), got[:hd, :].astype(F32)).astype(BF16)
        grad = jnp.where(mine, keep[hd:, :].astype(F32), got[hd:, :].astype(F32)).astype(BF16)
        enter_out[at, :] = state
        leave_out[at, :] = grad
        cum = cumc[:, h : h + 1]
        tail = jnp.exp(cumc[rows - 1 : rows, h : h + 1] - cum)
        rise = jnp.exp(cum) * scale
        gb = gb + tail * dot(x[:, at], grad, 1, 0)
        gc = gc + rise * dot(cot[:, at], state, 1, 0)
    piece = out.shape[1]
    gb, gc = gb.astype(BF16), gc.astype(BF16)
    for i in range(out.shape[0]):
        out[i, :, :n] = gb[i * piece : (i + 1) * piece, :]
        out[i, :, n:] = gc[i * piece : (i + 1) * piece, :]


def finish_body(heads, b, c, cumc, inner, gx, attended, enter, leave, layer_out, input_grad):
    rows = b.shape[0]
    hd = inner.shape[1] // heads
    n = b.shape[1]
    scale = 1.0 / math.sqrt(n)
    for h in range(heads):
        at = slice(h * hd, (h + 1) * hd)
        cum = cumc[:, h : h + 1]
        tail = jnp.exp(cumc[rows - 1 : rows, h : h + 1] - cum)
        rise = jnp.exp(cum) * scale
        y = inner[:, at] + rise * dot(c[...], enter[at, :], 1, 1)
        y = y * lax.rsqrt(jnp.mean(y * y, axis=-1, keepdims=True) + 1e-05)
        layer_out[:, at] = (y + attended[:, at]).astype(BF16)
        g = gx[:, at] + tail * dot(b[...], leave[at, :], 1, 1)
        input_grad[:, at] = g.astype(BF16)


def gather_body(scale, got, *rest):
    out = rest[-1]
    total = got[0].astype(F32)
    for i in range(1, got.shape[0]):
        total = total + got[i].astype(F32)
    total = (total * scale).astype(BF16)
    for i in range(out.shape[0]):
        out[i] = total


def project_body(mine, both, out):
    size, rows, cols = both.shape
    term = dot(mine[...], both[...].reshape(size * rows, cols), 0, 0)
    piece = out.shape[1]
    for i in range(out.shape[0]):
        out[i] = term[i * piece : (i + 1) * piece, :].astype(BF16)


def unpack_body(got, out):
    piece = got.shape[1]
    for i in range(got.shape[0]):
        out[i * piece : (i + 1) * piece, :] = got[i].astype(F32)


def shifted(block, axis, distance):
    devices = range(lax.axis_size(axis))
    route = [(i - distance, i) for i in devices if i - distance in devices]
    return lax.ppermute(block, axis, route)


def swapped(block, axis, distance):
    return lax.ppermute(block, axis, [(i, i ^ distance) for i in range(lax.axis_size(axis))])


def gathered(scale, got, copies, beside=()):
    return call(
        functools.partial(gather_body, scale),
        [((copies, *got.shape[1:]), BF16)],
        (got, *beside),
        [VMEM] + [HBM if a.size > 2**14 else VMEM for a in beside],
    )[0]


def summed(pieces, axes, scale, beside):
    got = lax.all_to_all(pieces, axes, 0, 0)
    return lax.all_to_all(gathered(scale, got, pieces.shape[0], beside), axes, 0, 0)


def summed_in_groups(pieces, axis, beside):
    near = pieces.shape[0]
    far = lax.axis_size(axis) // near
    inside = [[near * g + i for i in range(near)] for g in range(far)]
    across = [[i + near * g for g in range(far)] for i in range(near)]
    got = lax.all_to_all(pieces, axis, 0, 0, axis_index_groups=inside)
    got = lax.all_to_all(gathered(1.0, got, far), axis, 0, 0, axis_index_groups=across)
    return lax.all_to_all(gathered(1.0, got, near, beside), axis, 0, 0, axis_index_groups=inside)


def on_device(latents, proj_input, proj_output, scan_input, log_decay, att_queries, att_keys,
              att_values, scan_cotangent, window_offsets):
    _, rows, width = latents.shape
    heads = log_decay.shape[2]
    cols = scan_input.shape[2]
    hd = cols // heads
    n = proj_input.shape[1]
    share = width // lax.axis_size("space")
    assert heads == 2
    tm = lax.axis_size("tm")
    me = lax.axis_index("tm")
    lat, x, ld = latents[0], scan_input[0], log_decay[0].T
    q, k, v, cot = att_queries[0], att_keys[0], att_values[0], scan_cotangent[0]

    inputs = [
        pltpu.with_memory_space_constraint(a, pltpu.HBM)
        for a in (lat, proj_input, proj_output, x, cot, ld)
    ]
    tails = shifted(jnp.concatenate([k[rows - W :], v[rows - W :]], axis=1), "tm", 1)
    state = ((cols, n), F32)
    wire = ((2 * cols + EXTRA, n), BF16)
    b, c, cumc, cumr, fwd, bwd, table, send, mine = call(
        functools.partial(pre_body, heads),
        [((rows, n), BF16), ((rows, n), BF16), ((rows, heads), F32), ((heads, rows), F32), state, state,
         ((24, n), F32), wire, ((rows, share), BF16)],
        (lax.axis_index("space")[None], *inputs),
        [SMEM] + [HBM] * 6,
        [
            pltpu.VMEM((rows, width), BF16),
            pltpu.VMEM((width, 2 * n), BF16),
            pltpu.VMEM((rows, cols), BF16),
            pltpu.VMEM((rows, cols), BF16),
            pltpu.VMEM((heads, rows), F32),
            pltpu.SemaphoreType.DMA((3 * CHUNKS + 3,)),
        ],
        flops=2 * rows * width * 2 * n + 4 * rows * cols * n,
    )
    attended = call(
        functools.partial(attend_body, heads, QB),
        [((rows, cols), F32)],
        (me[None], pltpu.with_memory_space_constraint(window_offsets, pltpu.HBM), q, k, v, tails),
        [SMEM, HBM] + [VMEM] * 4,
        [pltpu.SMEM(window_offsets.shape, jnp.int32), pltpu.SemaphoreType.DMA],
        flops=4 * rows * 2 * W * cols,
        transcendentals=rows * 2 * W * heads,
    )[0]
    inner, gx, both, token = call(
        functools.partial(local_body, heads),
        [((rows, cols), F32), ((rows, cols), F32), ((rows, 2 * n), F32), ((8, n), F32)],
        (x, cot, b, c, cumc, cumr),
        flops=8 * rows * rows * cols,
        transcendentals=rows * rows * heads,
    )
    pair = swapped(send, "tm", 1)
    spread = call(
        pair_body,
        [((tm // 2, hd + EXTRA, n), BF16)],
        (me[None], pair, fwd, bwd, table, token),
        [SMEM] + [VMEM] * 5,
    )[0]
    same_core = [list(range(core, tm, 2)) for core in range(2)]
    got = lax.all_to_all(spread, "tm", 0, 0, axis_index_groups=same_core)
    keep, send = call(
        scan_body,
        [((2 * hd, n), BF16), ((2 * hd, n), BF16)],
        (me[None], got, pair, fwd, bwd, table),
        [SMEM] + [VMEM] * 5,
    )
    got = swapped(send, "tm", 1)
    near = math.gcd(lax.axis_size("space"), 4)
    both, enter, leave = call(
        functools.partial(grads_body, heads),
        [((near, rows // near, 2 * n), BF16), ((cols, n), BF16), ((cols, n), BF16)],
        (me[None], keep, got, x, cot, cumc, both),
        [SMEM] + [VMEM] * 6,
        flops=4 * rows * cols * n,
    )
    layer_out, input_grad = call(
        functools.partial(finish_body, heads),
        [((rows, cols), BF16), ((rows, cols), BF16)],
        (b, c, cumc, inner, gx, attended, enter, leave),
        flops=4 * rows * cols * n,
    )
    both = summed_in_groups(both, "space", (tails[:16, :n],))
    others = tm * lax.axis_size("dp")
    term = call(
        project_body,
        [((others, share // others, 2 * n), BF16)],
        (mine, both),
        flops=2 * rows * share * 2 * n,
    )[0]
    done = pltpu.with_memory_space_constraint(layer_out, pltpu.HBM)
    term = summed(term, ("tm", "dp"), 1.0 / math.sqrt(rows * others), (done,))
    proj_grad = call(unpack_body, [((share, 2 * n), F32)], (term,))[0]
    return layer_out[None], input_grad[None], proj_grad


def solution(mesh):
    wide = P("dp", "tm", "space")
    return jax.shard_map(
        on_device,
        mesh=mesh,
        in_specs=(P("dp", "tm", None), P(), P(), wide, wide, wide, wide, wide, wide, P("dp", "tm")),
        out_specs=(wide, wide, P("space", None)),
        check_vma=False,
    )
```

```python
import functools
import math

import jax
import jax.numpy as jnp
from jax import lax
from jax.experimental import pallas as pl
from jax.experimental.pallas import tpu as pltpu
from jax.sharding import PartitionSpec as P

W = 128
QB = 128
F32 = jnp.float32
BF16 = jnp.bfloat16
VMEM = pl.BlockSpec(memory_space=pltpu.VMEM)
HBM = pl.BlockSpec(memory_space=pltpu.HBM)
SMEM = pl.BlockSpec(memory_space=pltpu.SMEM)
NEG = -1e30
EXTRA = 8
CHUNKS = 2


def dot(a, b, left, right, precision=None):
    return lax.dot_general(
        a, b, (((left,), (right,)), ((), ())), preferred_element_type=F32, precision=precision
    )


def call(body, out, args, specs=None, scratch=(), flops=0, transcendentals=0, moved=0):
    return pl.pallas_call(
        body,
        out_shape=[jax.ShapeDtypeStruct(s, t) for s, t in out],
        in_specs=specs or [VMEM] * len(args),
        out_specs=[VMEM] * len(out),
        scratch_shapes=scratch,
        compiler_params=pltpu.CompilerParams(vmem_limit_bytes=40 * 2**20),
        cost_estimate=pl.CostEstimate(
            flops=flops, transcendentals=transcendentals, bytes_accessed=moved
        ),
    )(*args)


def three_parts(value):
    high = value.astype(BF16)
    rest = value - high.astype(F32)
    middle = rest.astype(BF16)
    return high, middle, (rest - middle.astype(F32)).astype(BF16)


def put_totals(send, at, totals):
    row = lax.broadcasted_iota(jnp.int32, (EXTRA, send.shape[1]), 0)
    extra = jnp.zeros((EXTRA, send.shape[1]), F32)
    for h, total in enumerate(totals):
        for part, value in enumerate(three_parts(total)):
            extra = jnp.where(row == 3 * h + part, value.astype(F32), extra)
    send[at : at + EXTRA, :] = extra.astype(BF16)


def pre_body(heads, place, lat_in, wb_in, wc_in, x_in, cot_in, ld_in, b_out, c_out, cumc_out, cumr_out,
             fresh_out, back_out, table_out, send, mine_out, lat, w, x, cot, ld, sems):
    n = wb_in.shape[1]
    chunks = CHUNKS
    deep = lat.shape[1] // chunks
    pairs = [(ld_in, ld), (x_in, x), (cot_in, cot)]
    for i in range(chunks):
        part = slice(i * deep, (i + 1) * deep)
        pairs.append((wb_in.at[part, :], w.at[part, :n]))
        pairs.append((wc_in.at[part, :], w.at[part, n:]))
        pairs.append((lat_in.at[:, part], lat.at[:, part]))
    copies = [pltpu.make_async_copy(src, dst, sems.at[i]) for i, (src, dst) in enumerate(pairs)]
    for copy in copies:
        copy.start()
    rows = lat.shape[0]
    cols = x.shape[1]
    hd = cols // heads
    scale = 1.0 / math.sqrt(n)
    down = lax.broadcasted_iota(jnp.int32, (rows, rows), 0)
    along = lax.broadcasted_iota(jnp.int32, (rows, rows), 1)
    copies[0].wait()
    cumr = dot(ld[...], (down <= along).astype(F32), 1, 0, lax.Precision.HIGHEST)
    cumc = dot((along <= down).astype(F32), ld[...], 1, 1, lax.Precision.HIGHEST)
    cumc_out[...] = cumc
    cumr_out[...] = cumr
    tail = jnp.exp(cumr[:, rows - 1 : rows] - cumr)
    rise = jnp.exp(cumr) * scale
    table_out[...] = jnp.zeros_like(table_out)
    totals = []
    for h in range(heads):
        totals.append(jnp.broadcast_to(cumc[rows - 1 : rows, h : h + 1], (1, n)))
        table_out[h : h + 1, :] = totals[h]
    put_totals(send, 2 * cols, totals)
    copies[1].wait()
    copies[2].wait()
    decayed = []
    for h in range(heads):
        at = slice(h * hd, (h + 1) * hd)
        xs = (x[:, at].astype(F32).T * tail[h : h + 1, :]).astype(BF16)
        gs = (cot[:, at].astype(F32).T * rise[h : h + 1, :]).astype(BF16)
        decayed.append((xs, gs))
    projected = None
    for i in range(chunks):
        for copy in copies[3 + 3 * i : 6 + 3 * i]:
            copy.wait()
        part = slice(i * deep, (i + 1) * deep)
        one = dot(lat[:, part], w[part, :], 1, 0)
        projected = one if projected is None else projected + one
    b = projected[:, :n].astype(BF16)
    c = projected[:, n:].astype(BF16)
    for h, (xs, gs) in enumerate(decayed):
        at = slice(h * hd, (h + 1) * hd)
        fresh = dot(xs, b, 1, 0)
        back = dot(gs, c, 1, 0)
        fresh_out[at, :] = fresh
        back_out[at, :] = back
        send[at, :] = fresh.astype(BF16)
        send[cols + h * hd : cols + (h + 1) * hd, :] = back.astype(BF16)
    b_out[...] = b
    c_out[...] = c
    share = mine_out.shape[1]
    mine_out[...] = lat[:, pl.ds(pl.multiple_of(place[0] * share, share), share)]


def totals_of(got, at):
    total = got[at : at + 1, :].astype(F32)
    for part in (1, 2):
        total = total + got[at + part : at + part + 1, :].astype(F32)
    return total


def pair_body(place, got, fwd, bwd, table, _, send):
    cols, n = fwd.shape
    slots, hd, _ = send.shape
    hd = hd - EXTRA
    me = place[0]
    late = me % 2
    chip = me // 2
    own = jnp.where(late == 1, table[1:2, :], table[0:1, :])
    theirs = jnp.where(
        late == 1, totals_of(got, 2 * cols + 3), totals_of(got, 2 * cols)
    )
    at = pl.ds(pl.multiple_of(late * hd, hd), hd)
    to = pl.ds(pl.multiple_of(cols + late * hd, hd), hd)
    got_f, got_b = got[at, :].astype(F32), got[to, :].astype(F32)
    by_own, by_theirs = jnp.exp(own), jnp.exp(theirs)
    early = late == 0
    f = jnp.where(early, by_theirs, 1.0) * fwd[at, :] + jnp.where(early, 1.0, by_own) * got_f
    b = jnp.where(early, 1.0, by_theirs) * bwd[at, :] + jnp.where(early, by_own, 1.0) * got_b
    row = lax.broadcasted_iota(jnp.int32, (EXTRA, n), 0)
    extra = jnp.zeros((EXTRA, n), F32)
    for part, value in enumerate(three_parts(own + theirs)):
        extra = jnp.where(row == part, value.astype(F32), extra)
    extra = extra.astype(BF16)
    for slot in range(slots):
        send[slot, :hd, :] = jnp.where(slot > chip, f, b).astype(BF16)
        send[slot, hd:, :] = extra


def scan_body(place, got, pair, fwd, bwd, table, keep, send):
    cols, n = fwd.shape
    slots, hd, _ = got.shape
    hd = hd - EXTRA
    late = place[0] % 2
    chip = place[0] // 2
    early = late == 0
    decays = [jnp.exp(totals_of(got.at[i], hd)) for i in range(slots)]
    state = jnp.zeros((hd, n), F32)
    grad = jnp.zeros((hd, n), F32)
    for i in range(slots):
        used = i < chip
        state = jnp.where(used, decays[i], 1.0) * state
        state = state + jnp.where(used, 1.0, 0.0) * got[i, :hd, :].astype(F32)
    for i in reversed(range(slots)):
        used = i > chip
        grad = jnp.where(used, decays[i], 1.0) * grad
        grad = grad + jnp.where(used, 1.0, 0.0) * got[i, :hd, :].astype(F32)
    by_own = jnp.exp(jnp.where(early, table[0:1, :], table[1:2, :]))
    by_theirs = jnp.exp(
        jnp.where(early, totals_of(pair, 2 * cols), totals_of(pair, 2 * cols + 3))
    )
    at = pl.ds(pl.multiple_of(late * hd, hd), hd)
    to = pl.ds(pl.multiple_of(cols + late * hd, hd), hd)
    after = jnp.where(early, fwd[at, :], pair[at, :].astype(F32))
    after = after + jnp.where(early, by_own, by_theirs) * state
    before = jnp.where(early, pair[to, :].astype(F32), bwd[at, :])
    before = before + jnp.where(early, by_theirs, by_own) * grad
    keep[:hd, :] = jnp.where(early, state, after).astype(BF16)
    keep[hd:, :] = jnp.where(early, before, grad).astype(BF16)
    send[:hd, :] = jnp.where(early, after, state).astype(BF16)
    send[hd:, :] = jnp.where(early, grad, before).astype(BF16)


def attend_body(heads, qb, place, offsets_in, q, k, v, tail, normed, out, offsets, sem):
    copy = pltpu.make_async_copy(offsets_in, offsets, sem)
    copy.start()
    rows = q.shape[0]
    hd = q.shape[1] // heads
    w = tail.shape[0]
    scale = 1.0 / math.sqrt(hd)
    i = lax.broadcasted_iota(jnp.int32, (qb, qb + w), 0)
    u = lax.broadcasted_iota(jnp.int32, (qb, qb + w), 1)

    def window(own, blk, at, behind):
        if blk == 0:
            return jnp.concatenate([tail[:, behind], own[:qb, at]], axis=0)
        return own[blk * qb - w : (blk + 1) * qb, at]

    places = [(blk, h) for blk in range(rows // qb) for h in range(heads)]
    scores = []
    for blk, h in places:
        at = slice(h * hd, (h + 1) * hd)
        keys = window(k, blk, at, at)
        scores.append(dot(q[blk * qb : (blk + 1) * qb, at], keys, 1, 1) * scale)
    copy.wait()
    for (blk, h), score in zip(places, scores):
        at = slice(h * hd, (h + 1) * hd)
        seen = (u <= i + w) & (u >= i + 1 + offsets[0, blk])
        if blk == 0:
            seen = seen & ((u >= w) | (place[0] > 0))
        score = jnp.where(seen, score, NEG)
        expo = jnp.exp(score - jnp.max(score, axis=-1, keepdims=True))
        probs = (expo / jnp.sum(expo, axis=-1, keepdims=True)).astype(BF16)
        values = window(v, blk, at, slice((heads + h) * hd, (heads + h + 1) * hd))
        own = slice(blk * qb, (blk + 1) * qb)
        out[own, at] = (normed[own, at] + dot(probs, values, 1, 0)).astype(BF16)


def local_body(heads, x, cot, b, c, cumc, cumr, inner_out, gx_out, both_out, token):
    token[...] = jnp.zeros_like(token)
    rows = x.shape[0]
    hd = x.shape[1] // heads
    n = b.shape[1]
    scale = 1.0 / math.sqrt(n)
    t = lax.broadcasted_iota(jnp.int32, (rows, rows), 0)
    s = lax.broadcasted_iota(jnp.int32, (rows, rows), 1)
    kern = dot(c[...], b[...], 1, 1) * scale
    weigh = None
    for h in range(heads):
        at = slice(h * hd, (h + 1) * hd)
        gap = cumc[:, h : h + 1] - cumr[h : h + 1, :]
        decay = jnp.exp(jnp.where(s <= t, gap, NEG))
        mixing = (kern * decay).astype(BF16)
        inner_out[:, at] = dot(mixing, x[:, at], 1, 0)
        gx_out[:, at] = dot(mixing, cot[:, at], 0, 0)
        one = dot(cot[:, at], x[:, at], 1, 1) * decay
        weigh = one if weigh is None else weigh + one
    weigh = (weigh * scale).astype(BF16)
    both_out[:, :n] = dot(weigh, c[...], 0, 0)
    both_out[:, n:] = dot(weigh, b[...], 1, 0)


def grads_body(heads, place, keep, got, x, cot, cumc, both, out, enter_out, leave_out):
    rows = x.shape[0]
    cols = x.shape[1]
    hd = cols // heads
    n = keep.shape[1]
    scale = 1.0 / math.sqrt(n)
    gb = both[:, :n]
    gc = both[:, n:]
    for h in range(heads):
        at = slice(h * hd, (h + 1) * hd)
        mine = place[0] % 2 == h
        state = jnp.where(mine, keep[:hd, :].astype(F32), got[:hd, :].astype(F32)).astype(BF16)
        grad = jnp.where(mine, keep[hd:, :].astype(F32), got[hd:, :].astype(F32)).astype(BF16)
        enter_out[at, :] = state
        leave_out[at, :] = grad
        cum = cumc[:, h : h + 1]
        tail = jnp.exp(cumc[rows - 1 : rows, h : h + 1] - cum)
        rise = jnp.exp(cum) * scale
        gb = gb + tail * dot(x[:, at], grad, 1, 0)
        gc = gc + rise * dot(cot[:, at], state, 1, 0)
    piece = out.shape[1]
    gb, gc = gb.astype(BF16), gc.astype(BF16)
    for i in range(out.shape[0]):
        out[i, :, :n] = gb[i * piece : (i + 1) * piece, :]
        out[i, :, n:] = gc[i * piece : (i + 1) * piece, :]


def finish_body(heads, b, c, cumc, inner, gx, enter, leave, normed_out, input_grad):
    rows = b.shape[0]
    hd = inner.shape[1] // heads
    n = b.shape[1]
    scale = 1.0 / math.sqrt(n)
    for h in range(heads):
        at = slice(h * hd, (h + 1) * hd)
        cum = cumc[:, h : h + 1]
        tail = jnp.exp(cumc[rows - 1 : rows, h : h + 1] - cum)
        rise = jnp.exp(cum) * scale
        y = inner[:, at] + rise * dot(c[...], enter[at, :], 1, 1)
        y = y * lax.rsqrt(jnp.mean(y * y, axis=-1, keepdims=True) + 1e-05)
        normed_out[:, at] = y
        g = gx[:, at] + tail * dot(b[...], leave[at, :], 1, 1)
        input_grad[:, at] = g.astype(BF16)


def gather_body(scale, got, *rest):
    out = rest[-1]
    total = got[0].astype(F32)
    for i in range(1, got.shape[0]):
        total = total + got[i].astype(F32)
    total = (total * scale).astype(BF16)
    for i in range(out.shape[0]):
        out[i] = total


def project_body(mine, both, out):
    size, rows, cols = both.shape
    term = dot(mine[...], both[...].reshape(size * rows, cols), 0, 0)
    piece = out.shape[1]
    for i in range(out.shape[0]):
        out[i] = term[i * piece : (i + 1) * piece, :].astype(BF16)


def unpack_body(got, out):
    piece = got.shape[1]
    for i in range(got.shape[0]):
        out[i * piece : (i + 1) * piece, :] = got[i].astype(F32)


def shifted(block, axis, distance):
    devices = range(lax.axis_size(axis))
    route = [(i - distance, i) for i in devices if i - distance in devices]
    return lax.ppermute(block, axis, route)


def swapped(block, axis, distance):
    return lax.ppermute(block, axis, [(i, i ^ distance) for i in range(lax.axis_size(axis))])


def gathered(scale, got, copies, beside=()):
    return call(
        functools.partial(gather_body, scale),
        [((copies, *got.shape[1:]), BF16)],
        (got, *beside),
        [VMEM] + [HBM] * len(beside),
    )[0]


def summed(pieces, axes, scale):
    got = lax.all_to_all(pieces, axes, 0, 0)
    return lax.all_to_all(gathered(scale, got, pieces.shape[0]), axes, 0, 0)


def summed_in_groups(pieces, axis, beside):
    near = pieces.shape[0]
    far = lax.axis_size(axis) // near
    inside = [[near * g + i for i in range(near)] for g in range(far)]
    across = [[i + near * g for g in range(far)] for i in range(near)]
    got = lax.all_to_all(pieces, axis, 0, 0, axis_index_groups=inside)
    got = lax.all_to_all(gathered(1.0, got, far), axis, 0, 0, axis_index_groups=across)
    return lax.all_to_all(gathered(1.0, got, near, beside), axis, 0, 0, axis_index_groups=inside)


def on_device(latents, proj_input, proj_output, scan_input, log_decay, att_queries, att_keys,
              att_values, scan_cotangent, window_offsets):
    _, rows, width = latents.shape
    heads = log_decay.shape[2]
    cols = scan_input.shape[2]
    hd = cols // heads
    n = proj_input.shape[1]
    share = width // lax.axis_size("space")
    assert heads == 2
    tm = lax.axis_size("tm")
    me = lax.axis_index("tm")
    lat, x, ld = latents[0], scan_input[0], log_decay[0].T
    q, k, v, cot = att_queries[0], att_keys[0], att_values[0], scan_cotangent[0]

    inputs = [
        pltpu.with_memory_space_constraint(a, pltpu.HBM)
        for a in (lat, proj_input, proj_output, x, cot, ld)
    ]
    tails = shifted(jnp.concatenate([k[rows - W :], v[rows - W :]], axis=1), "tm", 1)
    state = ((cols, n), F32)
    wire = ((2 * cols + EXTRA, n), BF16)
    b, c, cumc, cumr, fwd, bwd, table, send, mine = call(
        functools.partial(pre_body, heads),
        [((rows, n), BF16), ((rows, n), BF16), ((rows, heads), F32), ((heads, rows), F32), state, state,
         ((24, n), F32), wire, ((rows, share), BF16)],
        (lax.axis_index("space")[None], *inputs),
        [SMEM] + [HBM] * 6,
        [
            pltpu.VMEM((rows, width), BF16),
            pltpu.VMEM((width, 2 * n), BF16),
            pltpu.VMEM((rows, cols), BF16),
            pltpu.VMEM((rows, cols), BF16),
            pltpu.VMEM((heads, rows), F32),
            pltpu.SemaphoreType.DMA((3 * CHUNKS + 3,)),
        ],
        flops=2 * rows * width * 2 * n + 4 * rows * cols * n,
    )
    inner, gx, both, token = call(
        functools.partial(local_body, heads),
        [((rows, cols), F32), ((rows, cols), F32), ((rows, 2 * n), F32), ((8, n), F32)],
        (x, cot, b, c, cumc, cumr),
        flops=8 * rows * rows * cols,
        transcendentals=rows * rows * heads,
    )
    pair = swapped(send, "tm", 1)
    spread = call(
        pair_body,
        [((tm // 2, hd + EXTRA, n), BF16)],
        (me[None], pair, fwd, bwd, table, token),
        [SMEM] + [VMEM] * 5,
    )[0]
    same_core = [list(range(core, tm, 2)) for core in range(2)]
    got = lax.all_to_all(spread, "tm", 0, 0, axis_index_groups=same_core)
    keep, send = call(
        scan_body,
        [((2 * hd, n), BF16), ((2 * hd, n), BF16)],
        (me[None], got, pair, fwd, bwd, table),
        [SMEM] + [VMEM] * 5,
    )
    got = swapped(send, "tm", 1)
    near = math.gcd(lax.axis_size("space"), 4)
    both, enter, leave = call(
        functools.partial(grads_body, heads),
        [((near, rows // near, 2 * n), BF16), ((cols, n), BF16), ((cols, n), BF16)],
        (me[None], keep, got, x, cot, cumc, both),
        [SMEM] + [VMEM] * 6,
        flops=4 * rows * cols * n,
    )
    normed, input_grad = call(
        functools.partial(finish_body, heads),
        [((rows, cols), F32), ((rows, cols), BF16)],
        (b, c, cumc, inner, gx, enter, leave),
        flops=4 * rows * cols * n,
    )
    layer_out = call(
        functools.partial(attend_body, heads, QB),
        [((rows, cols), BF16)],
        (me[None], pltpu.with_memory_space_constraint(window_offsets, pltpu.HBM), q, k, v, tails, normed),
        [SMEM, HBM] + [VMEM] * 5,
        [pltpu.SMEM(window_offsets.shape, jnp.int32), pltpu.SemaphoreType.DMA],
        flops=4 * rows * 2 * W * cols,
        transcendentals=rows * 2 * W * heads,
    )[0]
    done = pltpu.with_memory_space_constraint(layer_out, pltpu.HBM)
    both = summed_in_groups(both, "space", (done,))
    others = tm * lax.axis_size("dp")
    term = call(
        project_body,
        [((others, share // others, 2 * n), BF16)],
        (mine, both),
        flops=2 * rows * share * 2 * n,
    )[0]
    term = summed(term, ("tm", "dp"), 1.0 / math.sqrt(rows * others))
    proj_grad = call(unpack_body, [((share, 2 * n), F32)], (term,))[0]
    return layer_out[None], input_grad[None], proj_grad


def solution(mesh):
    wide = P("dp", "tm", "space")
    return jax.shard_map(
        on_device,
        mesh=mesh,
        in_specs=(P("dp", "tm", None), P(), P(), wide, wide, wide, wide, wide, wide, P("dp", "tm")),
        out_specs=(wide, wide, P("space", None)),
        check_vma=False,
    )
```

```python
import functools
import math

import jax
import jax.numpy as jnp
from jax import lax
from jax.experimental import pallas as pl
from jax.experimental.pallas import tpu as pltpu
from jax.sharding import PartitionSpec as P

W = 128
QB = 128
F32 = jnp.float32
BF16 = jnp.bfloat16
VMEM = pl.BlockSpec(memory_space=pltpu.VMEM)
HBM = pl.BlockSpec(memory_space=pltpu.HBM)
SMEM = pl.BlockSpec(memory_space=pltpu.SMEM)
NEG = -1e30
EXTRA = 8
CHUNKS = 2


def dot(a, b, left, right, precision=None):
    return lax.dot_general(
        a, b, (((left,), (right,)), ((), ())), preferred_element_type=F32, precision=precision
    )


def call(body, out, args, specs=None, scratch=(), flops=0, transcendentals=0, moved=0):
    return pl.pallas_call(
        body,
        out_shape=[jax.ShapeDtypeStruct(s, t) for s, t in out],
        in_specs=specs or [VMEM] * len(args),
        out_specs=[VMEM] * len(out),
        scratch_shapes=scratch,
        compiler_params=pltpu.CompilerParams(vmem_limit_bytes=40 * 2**20),
        cost_estimate=pl.CostEstimate(
            flops=flops, transcendentals=transcendentals, bytes_accessed=moved
        ),
    )(*args)


def three_parts(value):
    high = value.astype(BF16)
    rest = value - high.astype(F32)
    middle = rest.astype(BF16)
    return high, middle, (rest - middle.astype(F32)).astype(BF16)


def put_totals(send, at, totals):
    row = lax.broadcasted_iota(jnp.int32, (EXTRA, send.shape[1]), 0)
    extra = jnp.zeros((EXTRA, send.shape[1]), F32)
    for h, total in enumerate(totals):
        for part, value in enumerate(three_parts(total)):
            extra = jnp.where(row == 3 * h + part, value.astype(F32), extra)
    send[at : at + EXTRA, :] = extra.astype(BF16)


def pre_body(heads, share, place, lat_in, wb_in, wc_in, x_in, cot_in, ld_in, b_out, c_out, cumc_out, cumr_out,
             fresh_out, back_out, table_out, send, mine_out, lat, w, x, cot, ld, sems):
    n = wb_in.shape[1]
    width = lat.shape[1]
    chunks = CHUNKS
    deep = lat.shape[1] // chunks
    pairs = [(ld_in, ld), (x_in, x), (cot_in, cot)]
    for i in range(chunks):
        part = slice(i * deep, (i + 1) * deep)
        pairs.append((wb_in.at[part, :], w.at[part, :n]))
        pairs.append((wc_in.at[part, :], w.at[part, n:]))
        pairs.append((lat_in.at[:, part], lat.at[:, part]))
    copies = [pltpu.make_async_copy(src, dst, sems.at[i]) for i, (src, dst) in enumerate(pairs)]
    for copy in copies:
        copy.start()
    rows = lat.shape[0]
    cols = x.shape[1]
    hd = cols // heads
    scale = 1.0 / math.sqrt(n)
    down = lax.broadcasted_iota(jnp.int32, (rows, rows), 0)
    along = lax.broadcasted_iota(jnp.int32, (rows, rows), 1)
    copies[0].wait()
    cumr = dot(ld[...], (down <= along).astype(F32), 1, 0, lax.Precision.HIGHEST)
    cumc = dot((along <= down).astype(F32), ld[...], 1, 1, lax.Precision.HIGHEST)
    cumc_out[...] = cumc
    cumr_out[...] = cumr
    tail = jnp.exp(cumr[:, rows - 1 : rows] - cumr)
    rise = jnp.exp(cumr) * scale
    table_out[...] = jnp.zeros_like(table_out)
    totals = []
    for h in range(heads):
        totals.append(jnp.broadcast_to(cumc[rows - 1 : rows, h : h + 1], (1, n)))
        table_out[h : h + 1, :] = totals[h]
    put_totals(send, 2 * cols, totals)
    copies[1].wait()
    copies[2].wait()
    decayed = []
    for h in range(heads):
        at = slice(h * hd, (h + 1) * hd)
        xs = (x[:, at].astype(F32).T * tail[h : h + 1, :]).astype(BF16)
        gs = (cot[:, at].astype(F32).T * rise[h : h + 1, :]).astype(BF16)
        decayed.append((xs, gs))
    projected = None
    for i in range(chunks):
        for copy in copies[3 + 3 * i : 6 + 3 * i]:
            copy.wait()
        part = slice(i * deep, (i + 1) * deep)
        one = dot(lat[:, part], w[part, :], 1, 0)
        projected = one if projected is None else projected + one
    b = projected[:, :n].astype(BF16)
    c = projected[:, n:].astype(BF16)
    for h, (xs, gs) in enumerate(decayed):
        at = slice(h * hd, (h + 1) * hd)
        fresh = dot(xs, b, 1, 0)
        back = dot(gs, c, 1, 0)
        fresh_out[at, :] = fresh
        back_out[at, :] = back
        send[at, :] = fresh.astype(BF16)
        send[cols + h * hd : cols + (h + 1) * hd, :] = back.astype(BF16)
    b_out[...] = b
    c_out[...] = c
    far = mine_out.shape[1] // share
    near = width // mine_out.shape[1]
    for g in range(far):
        start = pl.multiple_of((near * g + place[0] % near) * share, share)
        mine_out[:, g * share : (g + 1) * share] = lat[:, pl.ds(start, share)]


def totals_of(got, at):
    total = got[at : at + 1, :].astype(F32)
    for part in (1, 2):
        total = total + got[at + part : at + part + 1, :].astype(F32)
    return total


def pair_body(place, got, fwd, bwd, table, _, send):
    cols, n = fwd.shape
    slots, hd, _ = send.shape
    hd = hd - EXTRA
    me = place[0]
    late = me % 2
    chip = me // 2
    own = jnp.where(late == 1, table[1:2, :], table[0:1, :])
    theirs = jnp.where(
        late == 1, totals_of(got, 2 * cols + 3), totals_of(got, 2 * cols)
    )
    at = pl.ds(pl.multiple_of(late * hd, hd), hd)
    to = pl.ds(pl.multiple_of(cols + late * hd, hd), hd)
    got_f, got_b = got[at, :].astype(F32), got[to, :].astype(F32)
    by_own, by_theirs = jnp.exp(own), jnp.exp(theirs)
    early = late == 0
    f = jnp.where(early, by_theirs, 1.0) * fwd[at, :] + jnp.where(early, 1.0, by_own) * got_f
    b = jnp.where(early, 1.0, by_theirs) * bwd[at, :] + jnp.where(early, by_own, 1.0) * got_b
    row = lax.broadcasted_iota(jnp.int32, (EXTRA, n), 0)
    extra = jnp.zeros((EXTRA, n), F32)
    for part, value in enumerate(three_parts(own + theirs)):
        extra = jnp.where(row == part, value.astype(F32), extra)
    extra = extra.astype(BF16)
    for slot in range(slots):
        send[slot, :hd, :] = jnp.where(slot > chip, f, b).astype(BF16)
        send[slot, hd:, :] = extra


def scan_body(place, got, pair, fwd, bwd, table, keep, send):
    cols, n = fwd.shape
    slots, hd, _ = got.shape
    hd = hd - EXTRA
    late = place[0] % 2
    chip = place[0] // 2
    early = late == 0
    decays = [jnp.exp(totals_of(got.at[i], hd)) for i in range(slots)]
    state = jnp.zeros((hd, n), F32)
    grad = jnp.zeros((hd, n), F32)
    for i in range(slots):
        used = i < chip
        state = jnp.where(used, decays[i], 1.0) * state
        state = state + jnp.where(used, 1.0, 0.0) * got[i, :hd, :].astype(F32)
    for i in reversed(range(slots)):
        used = i > chip
        grad = jnp.where(used, decays[i], 1.0) * grad
        grad = grad + jnp.where(used, 1.0, 0.0) * got[i, :hd, :].astype(F32)
    by_own = jnp.exp(jnp.where(early, table[0:1, :], table[1:2, :]))
    by_theirs = jnp.exp(
        jnp.where(early, totals_of(pair, 2 * cols), totals_of(pair, 2 * cols + 3))
    )
    at = pl.ds(pl.multiple_of(late * hd, hd), hd)
    to = pl.ds(pl.multiple_of(cols + late * hd, hd), hd)
    after = jnp.where(early, fwd[at, :], pair[at, :].astype(F32))
    after = after + jnp.where(early, by_own, by_theirs) * state
    before = jnp.where(early, pair[to, :].astype(F32), bwd[at, :])
    before = before + jnp.where(early, by_theirs, by_own) * grad
    keep[:hd, :] = jnp.where(early, state, after).astype(BF16)
    keep[hd:, :] = jnp.where(early, before, grad).astype(BF16)
    send[:hd, :] = jnp.where(early, after, state).astype(BF16)
    send[hd:, :] = jnp.where(early, grad, before).astype(BF16)


def attend_body(heads, qb, place, offsets_in, q, k, v, tail, normed, out, offsets, sem):
    copy = pltpu.make_async_copy(offsets_in, offsets, sem)
    copy.start()
    rows = q.shape[0]
    hd = q.shape[1] // heads
    w = tail.shape[0]
    scale = 1.0 / math.sqrt(hd)
    i = lax.broadcasted_iota(jnp.int32, (qb, qb + w), 0)
    u = lax.broadcasted_iota(jnp.int32, (qb, qb + w), 1)

    def window(own, blk, at, behind):
        if blk == 0:
            return jnp.concatenate([tail[:, behind], own[:qb, at]], axis=0)
        return own[blk * qb - w : (blk + 1) * qb, at]

    places = [(blk, h) for blk in range(rows // qb) for h in range(heads)]
    scores = []
    for blk, h in places:
        at = slice(h * hd, (h + 1) * hd)
        keys = window(k, blk, at, at)
        scores.append(dot(q[blk * qb : (blk + 1) * qb, at], keys, 1, 1) * scale)
    copy.wait()
    for (blk, h), score in zip(places, scores):
        at = slice(h * hd, (h + 1) * hd)
        seen = (u <= i + w) & (u >= i + 1 + offsets[0, blk])
        if blk == 0:
            seen = seen & ((u >= w) | (place[0] > 0))
        score = jnp.where(seen, score, NEG)
        expo = jnp.exp(score - jnp.max(score, axis=-1, keepdims=True))
        probs = (expo / jnp.sum(expo, axis=-1, keepdims=True)).astype(BF16)
        values = window(v, blk, at, slice((heads + h) * hd, (heads + h + 1) * hd))
        own = slice(blk * qb, (blk + 1) * qb)
        out[own, at] = (normed[own, at] + dot(probs, values, 1, 0)).astype(BF16)


def local_body(heads, x, cot, b, c, cumc, cumr, inner_out, gx_out, both_out, token):
    token[...] = jnp.zeros_like(token)
    rows = x.shape[0]
    hd = x.shape[1] // heads
    n = b.shape[1]
    scale = 1.0 / math.sqrt(n)
    t = lax.broadcasted_iota(jnp.int32, (rows, rows), 0)
    s = lax.broadcasted_iota(jnp.int32, (rows, rows), 1)
    kern = dot(c[...], b[...], 1, 1) * scale
    weigh = None
    for h in range(heads):
        at = slice(h * hd, (h + 1) * hd)
        gap = cumc[:, h : h + 1] - cumr[h : h + 1, :]
        decay = jnp.exp(jnp.where(s <= t, gap, NEG))
        mixing = (kern * decay).astype(BF16)
        inner_out[:, at] = dot(mixing, x[:, at], 1, 0)
        gx_out[:, at] = dot(mixing, cot[:, at], 0, 0)
        one = dot(cot[:, at], x[:, at], 1, 1) * decay
        weigh = one if weigh is None else weigh + one
    weigh = (weigh * scale).astype(BF16)
    both_out[:, :n] = dot(weigh, c[...], 0, 0)
    both_out[:, n:] = dot(weigh, b[...], 1, 0)


def grads_body(heads, place, keep, got, x, cot, cumc, both, out, enter_out, leave_out):
    rows = x.shape[0]
    cols = x.shape[1]
    hd = cols // heads
    n = keep.shape[1]
    scale = 1.0 / math.sqrt(n)
    gb = both[:, :n]
    gc = both[:, n:]
    for h in range(heads):
        at = slice(h * hd, (h + 1) * hd)
        mine = place[0] % 2 == h
        state = jnp.where(mine, keep[:hd, :].astype(F32), got[:hd, :].astype(F32)).astype(BF16)
        grad = jnp.where(mine, keep[hd:, :].astype(F32), got[hd:, :].astype(F32)).astype(BF16)
        enter_out[at, :] = state
        leave_out[at, :] = grad
        cum = cumc[:, h : h + 1]
        tail = jnp.exp(cumc[rows - 1 : rows, h : h + 1] - cum)
        rise = jnp.exp(cum) * scale
        gb = gb + tail * dot(x[:, at], grad, 1, 0)
        gc = gc + rise * dot(cot[:, at], state, 1, 0)
    gb, gc = gb.astype(BF16), gc.astype(BF16)
    for i in range(out.shape[0]):
        out[i, :, :n] = gb
        out[i, :, n:] = gc


def finish_body(heads, b, c, cumc, inner, gx, enter, leave, normed_out, input_grad):
    rows = b.shape[0]
    hd = inner.shape[1] // heads
    n = b.shape[1]
    scale = 1.0 / math.sqrt(n)
    for h in range(heads):
        at = slice(h * hd, (h + 1) * hd)
        cum = cumc[:, h : h + 1]
        tail = jnp.exp(cumc[rows - 1 : rows, h : h + 1] - cum)
        rise = jnp.exp(cum) * scale
        y = inner[:, at] + rise * dot(c[...], enter[at, :], 1, 1)
        y = y * lax.rsqrt(jnp.mean(y * y, axis=-1, keepdims=True) + 1e-05)
        normed_out[:, at] = y
        g = gx[:, at] + tail * dot(b[...], leave[at, :], 1, 1)
        input_grad[:, at] = g.astype(BF16)


def added(got):
    total = got[0].astype(F32)
    for i in range(1, got.shape[0]):
        total = total + got[i].astype(F32)
    return total


def project_body(share, mine, got, out):
    term = dot(mine[...], added(got).astype(BF16), 0, 0)
    far = term.shape[0] // share
    piece = out.shape[1] // far
    for k in range(out.shape[0]):
        for g in range(far):
            rows = slice(g * share + k * piece, g * share + (k + 1) * piece)
            out[k, g * piece : (g + 1) * piece, :] = term[rows, :].astype(BF16)


def spread_body(far, got, out):
    total = added(got).astype(BF16).astype(F32)
    piece = out.shape[1]
    clips = out.shape[0] // far
    for i in range(out.shape[0]):
        g = i // clips
        out[i] = total[g * piece : (g + 1) * piece, :].astype(BF16)


def gather_body(scale, got, _, out):
    total = (added(got) * scale).astype(BF16)
    for i in range(out.shape[0]):
        out[i] = total


def unpack_body(got, out):
    piece = got.shape[1]
    for i in range(got.shape[0]):
        out[i * piece : (i + 1) * piece, :] = got[i].astype(F32)


def shifted(block, axis, distance):
    devices = range(lax.axis_size(axis))
    route = [(i - distance, i) for i in devices if i - distance in devices]
    return lax.ppermute(block, axis, route)


def swapped(block, axis, distance):
    return lax.ppermute(block, axis, [(i, i ^ distance) for i in range(lax.axis_size(axis))])


def on_device(latents, proj_input, proj_output, scan_input, log_decay, att_queries, att_keys,
              att_values, scan_cotangent, window_offsets):
    _, rows, width = latents.shape
    heads = log_decay.shape[2]
    cols = scan_input.shape[2]
    hd = cols // heads
    n = proj_input.shape[1]
    share = width // lax.axis_size("space")
    assert heads == 2
    near = math.gcd(lax.axis_size("space"), 4)
    far = lax.axis_size("space") // near
    tm = lax.axis_size("tm")
    me = lax.axis_index("tm")
    lat, x, ld = latents[0], scan_input[0], log_decay[0].T
    q, k, v, cot = att_queries[0], att_keys[0], att_values[0], scan_cotangent[0]

    inputs = [
        pltpu.with_memory_space_constraint(a, pltpu.HBM)
        for a in (lat, proj_input, proj_output, x, cot, ld)
    ]
    state = ((cols, n), F32)
    wire = ((2 * cols + EXTRA, n), BF16)
    b, c, cumc, cumr, fwd, bwd, table, send, mine = call(
        functools.partial(pre_body, heads, share),
        [((rows, n), BF16), ((rows, n), BF16), ((rows, heads), F32), ((heads, rows), F32), state, state,
         ((24, n), F32), wire, ((rows, share * far), BF16)],
        (lax.axis_index("space")[None], *inputs),
        [SMEM] + [HBM] * 6,
        [
            pltpu.VMEM((rows, width), BF16),
            pltpu.VMEM((width, 2 * n), BF16),
            pltpu.VMEM((rows, cols), BF16),
            pltpu.VMEM((rows, cols), BF16),
            pltpu.VMEM((heads, rows), F32),
            pltpu.SemaphoreType.DMA((3 * CHUNKS + 3,)),
        ],
        flops=2 * rows * width * 2 * n + 4 * rows * cols * n,
    )
    inner, gx, both, token = call(
        functools.partial(local_body, heads),
        [((rows, cols), F32), ((rows, cols), F32), ((rows, 2 * n), F32), ((8, n), F32)],
        (x, cot, b, c, cumc, cumr),
        flops=8 * rows * rows * cols,
        transcendentals=rows * rows * heads,
    )
    pair = swapped(send, "tm", 1)
    spread = call(
        pair_body,
        [((tm // 2, hd + EXTRA, n), BF16)],
        (me[None], pair, fwd, bwd, table, token),
        [SMEM] + [VMEM] * 5,
    )[0]
    same_core = [list(range(core, tm, 2)) for core in range(2)]
    got = lax.all_to_all(spread, "tm", 0, 0, axis_index_groups=same_core)
    keep, send = call(
        scan_body,
        [((2 * hd, n), BF16), ((2 * hd, n), BF16)],
        (me[None], got, pair, fwd, bwd, table),
        [SMEM] + [VMEM] * 5,
    )
    got = swapped(send, "tm", 1)
    both, enter, leave = call(
        functools.partial(grads_body, heads),
        [((near, rows, 2 * n), BF16), ((cols, n), BF16), ((cols, n), BF16)],
        (me[None], keep, got, x, cot, cumc, both),
        [SMEM] + [VMEM] * 6,
        flops=4 * rows * cols * n,
    )
    normed, input_grad = call(
        functools.partial(finish_body, heads),
        [((rows, cols), F32), ((rows, cols), BF16)],
        (b, c, cumc, inner, gx, enter, leave),
        flops=4 * rows * cols * n,
    )
    clips = lax.axis_size("dp")
    inside = [[near * g + i for i in range(near)] for g in range(far)]
    across = [
        [(near * g + i) * clips + clip for g in range(far) for clip in range(clips)] for i in range(near)
    ]
    piece = share // tm
    got = lax.all_to_all(both, "space", 0, 0, axis_index_groups=inside)
    term = call(
        functools.partial(project_body, share),
        [((tm, far * piece, 2 * n), BF16)],
        (mine, got),
        flops=2 * rows * share * far * 2 * n,
    )[0]
    got = lax.all_to_all(term, "tm", 0, 0)
    term = call(functools.partial(spread_body, far), [((far * clips, piece, 2 * n), BF16)], (got,))[0]
    last_k, last_v, term = lax.optimization_barrier((k, v, term))
    tails = shifted(jnp.concatenate([last_k[rows - W :], last_v[rows - W :]], axis=1), "tm", 1)
    layer_out = call(
        functools.partial(attend_body, heads, QB),
        [((rows, cols), BF16)],
        (me[None], pltpu.with_memory_space_constraint(window_offsets, pltpu.HBM), q, k, v, tails, normed),
        [SMEM, HBM] + [VMEM] * 5,
        [pltpu.SMEM(window_offsets.shape, jnp.int32), pltpu.SemaphoreType.DMA],
        flops=4 * rows * 2 * W * cols,
        transcendentals=rows * 2 * W * heads,
    )[0]
    done = pltpu.with_memory_space_constraint(layer_out, pltpu.HBM)
    got = lax.all_to_all(term, ("space", "dp"), 0, 0, axis_index_groups=across)
    term = call(
        functools.partial(gather_body, 1.0 / math.sqrt(rows * tm * clips)),
        [((tm, piece, 2 * n), BF16)],
        (got, done),
        [VMEM, HBM],
    )[0]
    got = lax.all_to_all(term, "tm", 0, 0)
    proj_grad = call(unpack_body, [((share, 2 * n), F32)], (got,))[0]
    return layer_out[None], input_grad[None], proj_grad


def solution(mesh):
    wide = P("dp", "tm", "space")
    return jax.shard_map(
        on_device,
        mesh=mesh,
        in_specs=(P("dp", "tm", None), P(), P(), wide, wide, wide, wide, wide, wide, P("dp", "tm")),
        out_specs=(wide, wide, P("space", None)),
        check_vma=False,
    )
```

```python
import functools
import math

import jax
import jax.numpy as jnp
from jax import lax
from jax.experimental import pallas as pl
from jax.experimental.pallas import tpu as pltpu
from jax.sharding import PartitionSpec as P

W = 128
QB = 128
F32 = jnp.float32
BF16 = jnp.bfloat16
VMEM = pl.BlockSpec(memory_space=pltpu.VMEM)
HBM = pl.BlockSpec(memory_space=pltpu.HBM)
SMEM = pl.BlockSpec(memory_space=pltpu.SMEM)
NEG = -1e30
EXTRA = 8
CHUNKS = 2


def dot(a, b, left, right, precision=None):
    return lax.dot_general(
        a, b, (((left,), (right,)), ((), ())), preferred_element_type=F32, precision=precision
    )


def call(body, out, args, specs=None, scratch=(), flops=0, transcendentals=0, moved=0):
    return pl.pallas_call(
        body,
        out_shape=[jax.ShapeDtypeStruct(s, t) for s, t in out],
        in_specs=specs or [VMEM] * len(args),
        out_specs=[VMEM] * len(out),
        scratch_shapes=scratch,
        compiler_params=pltpu.CompilerParams(vmem_limit_bytes=40 * 2**20),
        cost_estimate=pl.CostEstimate(
            flops=flops, transcendentals=transcendentals, bytes_accessed=moved
        ),
    )(*args)


def three_parts(value):
    high = value.astype(BF16)
    rest = value - high.astype(F32)
    middle = rest.astype(BF16)
    return high, middle, (rest - middle.astype(F32)).astype(BF16)


def put_totals(send, at, totals):
    row = lax.broadcasted_iota(jnp.int32, (EXTRA, send.shape[1]), 0)
    extra = jnp.zeros((EXTRA, send.shape[1]), F32)
    for h, total in enumerate(totals):
        for part, value in enumerate(three_parts(total)):
            extra = jnp.where(row == 3 * h + part, value.astype(F32), extra)
    send[at : at + EXTRA, :] = extra.astype(BF16)


def pre_body(heads, share, place, lat_in, wb_in, wc_in, x_in, cot_in, ld_in, b_out, c_out, cumc_out, cumr_out,
             fresh_out, back_out, table_out, send, mine_out, lat, w, x, cot, ld, sems):
    n = wb_in.shape[1]
    width = lat.shape[1]
    chunks = CHUNKS
    deep = lat.shape[1] // chunks
    pairs = [(ld_in, ld), (x_in, x), (cot_in, cot)]
    for i in range(chunks):
        part = slice(i * deep, (i + 1) * deep)
        pairs.append((wb_in.at[part, :], w.at[part, :n]))
        pairs.append((wc_in.at[part, :], w.at[part, n:]))
        pairs.append((lat_in.at[:, part], lat.at[:, part]))
    copies = [pltpu.make_async_copy(src, dst, sems.at[i]) for i, (src, dst) in enumerate(pairs)]
    for copy in copies:
        copy.start()
    rows = lat.shape[0]
    cols = x.shape[1]
    hd = cols // heads
    scale = 1.0 / math.sqrt(n)
    down = lax.broadcasted_iota(jnp.int32, (rows, rows), 0)
    along = lax.broadcasted_iota(jnp.int32, (rows, rows), 1)
    copies[0].wait()
    cumr = dot(ld[...], (down <= along).astype(F32), 1, 0, lax.Precision.HIGHEST)
    cumc = dot((along <= down).astype(F32), ld[...], 1, 1, lax.Precision.HIGHEST)
    cumc_out[...] = cumc
    cumr_out[...] = cumr
    tail = jnp.exp(cumr[:, rows - 1 : rows] - cumr)
    rise = jnp.exp(cumr) * scale
    table_out[...] = jnp.zeros_like(table_out)
    totals = []
    for h in range(heads):
        totals.append(jnp.broadcast_to(cumc[rows - 1 : rows, h : h + 1], (1, n)))
        table_out[h : h + 1, :] = totals[h]
    put_totals(send, 2 * cols, totals)
    copies[1].wait()
    copies[2].wait()
    decayed = []
    for h in range(heads):
        at = slice(h * hd, (h + 1) * hd)
        xs = (x[:, at].astype(F32).T * tail[h : h + 1, :]).astype(BF16)
        gs = (cot[:, at].astype(F32).T * rise[h : h + 1, :]).astype(BF16)
        decayed.append((xs, gs))
    projected = None
    for i in range(chunks):
        for copy in copies[3 + 3 * i : 6 + 3 * i]:
            copy.wait()
        part = slice(i * deep, (i + 1) * deep)
        one = dot(lat[:, part], w[part, :], 1, 0)
        projected = one if projected is None else projected + one
    b = projected[:, :n].astype(BF16)
    c = projected[:, n:].astype(BF16)
    for h, (xs, gs) in enumerate(decayed):
        at = slice(h * hd, (h + 1) * hd)
        fresh = dot(xs, b, 1, 0)
        back = dot(gs, c, 1, 0)
        fresh_out[at, :] = fresh
        back_out[at, :] = back
        send[at, :] = fresh.astype(BF16)
        send[cols + h * hd : cols + (h + 1) * hd, :] = back.astype(BF16)
    b_out[...] = b
    c_out[...] = c
    far = mine_out.shape[1] // share
    near = width // mine_out.shape[1]
    for g in range(far):
        start = pl.multiple_of((near * g + place[0] % near) * share, share)
        mine_out[:, g * share : (g + 1) * share] = lat[:, pl.ds(start, share)]


def totals_of(got, at):
    total = got[at : at + 1, :].astype(F32)
    for part in (1, 2):
        total = total + got[at + part : at + part + 1, :].astype(F32)
    return total


def pair_body(place, got, fwd, bwd, table, _, send):
    cols, n = fwd.shape
    slots, hd, _ = send.shape
    hd = hd - EXTRA
    me = place[0]
    late = me % 2
    chip = me // 2
    own = jnp.where(late == 1, table[1:2, :], table[0:1, :])
    theirs = jnp.where(
        late == 1, totals_of(got, 2 * cols + 3), totals_of(got, 2 * cols)
    )
    at = pl.ds(pl.multiple_of(late * hd, hd), hd)
    to = pl.ds(pl.multiple_of(cols + late * hd, hd), hd)
    got_f, got_b = got[at, :].astype(F32), got[to, :].astype(F32)
    by_own, by_theirs = jnp.exp(own), jnp.exp(theirs)
    early = late == 0
    f = jnp.where(early, by_theirs, 1.0) * fwd[at, :] + jnp.where(early, 1.0, by_own) * got_f
    b = jnp.where(early, 1.0, by_theirs) * bwd[at, :] + jnp.where(early, by_own, 1.0) * got_b
    row = lax.broadcasted_iota(jnp.int32, (EXTRA, n), 0)
    extra = jnp.zeros((EXTRA, n), F32)
    for part, value in enumerate(three_parts(own + theirs)):
        extra = jnp.where(row == part, value.astype(F32), extra)
    extra = extra.astype(BF16)
    for slot in range(slots):
        send[slot, :hd, :] = jnp.where(slot > chip, f, b).astype(BF16)
        send[slot, hd:, :] = extra


def scan_body(place, got, pair, fwd, bwd, table, keep, send):
    cols, n = fwd.shape
    slots, hd, _ = got.shape
    hd = hd - EXTRA
    late = place[0] % 2
    chip = place[0] // 2
    early = late == 0
    decays = [jnp.exp(totals_of(got.at[i], hd)) for i in range(slots)]
    state = jnp.zeros((hd, n), F32)
    grad = jnp.zeros((hd, n), F32)
    for i in range(slots):
        used = i < chip
        state = jnp.where(used, decays[i], 1.0) * state
        state = state + jnp.where(used, 1.0, 0.0) * got[i, :hd, :].astype(F32)
    for i in reversed(range(slots)):
        used = i > chip
        grad = jnp.where(used, decays[i], 1.0) * grad
        grad = grad + jnp.where(used, 1.0, 0.0) * got[i, :hd, :].astype(F32)
    by_own = jnp.exp(jnp.where(early, table[0:1, :], table[1:2, :]))
    by_theirs = jnp.exp(
        jnp.where(early, totals_of(pair, 2 * cols), totals_of(pair, 2 * cols + 3))
    )
    at = pl.ds(pl.multiple_of(late * hd, hd), hd)
    to = pl.ds(pl.multiple_of(cols + late * hd, hd), hd)
    after = jnp.where(early, fwd[at, :], pair[at, :].astype(F32))
    after = after + jnp.where(early, by_own, by_theirs) * state
    before = jnp.where(early, pair[to, :].astype(F32), bwd[at, :])
    before = before + jnp.where(early, by_theirs, by_own) * grad
    keep[:hd, :] = jnp.where(early, state, after).astype(BF16)
    keep[hd:, :] = jnp.where(early, before, grad).astype(BF16)
    send[:hd, :] = jnp.where(early, after, state).astype(BF16)
    send[hd:, :] = jnp.where(early, grad, before).astype(BF16)


def attend_body(heads, qb, place, offsets_in, q, k, v, tail, normed, out, offsets, sem):
    copy = pltpu.make_async_copy(offsets_in, offsets, sem)
    copy.start()
    rows = q.shape[0]
    hd = q.shape[1] // heads
    w = tail.shape[0]
    scale = 1.0 / math.sqrt(hd)
    i = lax.broadcasted_iota(jnp.int32, (qb, qb + w), 0)
    u = lax.broadcasted_iota(jnp.int32, (qb, qb + w), 1)

    def window(own, blk, at, behind):
        if blk == 0:
            return jnp.concatenate([tail[:, behind], own[:qb, at]], axis=0)
        return own[blk * qb - w : (blk + 1) * qb, at]

    places = [(blk, h) for blk in range(rows // qb) for h in range(heads)]
    scores = []
    for blk, h in places:
        at = slice(h * hd, (h + 1) * hd)
        keys = window(k, blk, at, at)
        scores.append(dot(q[blk * qb : (blk + 1) * qb, at], keys, 1, 1) * scale)
    copy.wait()
    for (blk, h), score in zip(places, scores):
        at = slice(h * hd, (h + 1) * hd)
        seen = (u <= i + w) & (u >= i + 1 + offsets[0, blk])
        if blk == 0:
            seen = seen & ((u >= w) | (place[0] > 0))
        score = jnp.where(seen, score, NEG)
        expo = jnp.exp(score - jnp.max(score, axis=-1, keepdims=True))
        probs = (expo / jnp.sum(expo, axis=-1, keepdims=True)).astype(BF16)
        values = window(v, blk, at, slice((heads + h) * hd, (heads + h + 1) * hd))
        own = slice(blk * qb, (blk + 1) * qb)
        out[own, at] = (normed[own, at] + dot(probs, values, 1, 0)).astype(BF16)


def local_body(heads, x, cot, b, c, cumc, cumr, inner_out, gx_out, both_out, token):
    token[...] = jnp.zeros_like(token)
    rows = x.shape[0]
    hd = x.shape[1] // heads
    n = b.shape[1]
    scale = 1.0 / math.sqrt(n)
    t = lax.broadcasted_iota(jnp.int32, (rows, rows), 0)
    s = lax.broadcasted_iota(jnp.int32, (rows, rows), 1)
    kern = dot(c[...], b[...], 1, 1) * scale
    weigh = None
    for h in range(heads):
        at = slice(h * hd, (h + 1) * hd)
        gap = cumc[:, h : h + 1] - cumr[h : h + 1, :]
        decay = jnp.exp(jnp.where(s <= t, gap, NEG))
        mixing = (kern * decay).astype(BF16)
        inner_out[:, at] = dot(mixing, x[:, at], 1, 0)
        gx_out[:, at] = dot(mixing, cot[:, at], 0, 0)
        one = dot(cot[:, at], x[:, at], 1, 1) * decay
        weigh = one if weigh is None else weigh + one
    weigh = (weigh * scale).astype(BF16)
    both_out[:, :n] = dot(weigh, c[...], 0, 0)
    both_out[:, n:] = dot(weigh, b[...], 1, 0)


def grads_body(heads, place, keep, got, x, cot, cumc, both, out, enter_out, leave_out):
    rows = x.shape[0]
    cols = x.shape[1]
    hd = cols // heads
    n = keep.shape[1]
    scale = 1.0 / math.sqrt(n)
    gb = both[:, :n]
    gc = both[:, n:]
    for h in range(heads):
        at = slice(h * hd, (h + 1) * hd)
        mine = place[0] % 2 == h
        state = jnp.where(mine, keep[:hd, :].astype(F32), got[:hd, :].astype(F32)).astype(BF16)
        grad = jnp.where(mine, keep[hd:, :].astype(F32), got[hd:, :].astype(F32)).astype(BF16)
        enter_out[at, :] = state
        leave_out[at, :] = grad
        cum = cumc[:, h : h + 1]
        tail = jnp.exp(cumc[rows - 1 : rows, h : h + 1] - cum)
        rise = jnp.exp(cum) * scale
        gb = gb + tail * dot(x[:, at], grad, 1, 0)
        gc = gc + rise * dot(cot[:, at], state, 1, 0)
    gb, gc = gb.astype(BF16), gc.astype(BF16)
    out[:, :n] = gb
    out[:, n:] = gc


def finish_body(heads, b, c, cumc, inner, gx, enter, leave, normed_out, input_grad):
    rows = b.shape[0]
    hd = inner.shape[1] // heads
    n = b.shape[1]
    scale = 1.0 / math.sqrt(n)
    for h in range(heads):
        at = slice(h * hd, (h + 1) * hd)
        cum = cumc[:, h : h + 1]
        tail = jnp.exp(cumc[rows - 1 : rows, h : h + 1] - cum)
        rise = jnp.exp(cum) * scale
        y = inner[:, at] + rise * dot(c[...], enter[at, :], 1, 1)
        y = y * lax.rsqrt(jnp.mean(y * y, axis=-1, keepdims=True) + 1e-05)
        normed_out[:, at] = y
        g = gx[:, at] + tail * dot(b[...], leave[at, :], 1, 1)
        input_grad[:, at] = g.astype(BF16)


def added(got):
    total = got[0].astype(F32)
    for i in range(1, got.shape[0]):
        total = total + got[i].astype(F32)
    return total


def pass_on_body(own, got, out):
    out[...] = (own[...].astype(F32) + got[...].astype(F32)).astype(BF16)


def project_body(share, mine, own, got, _, out):
    heads_sum = (own[...].astype(F32) + got[...].astype(F32)).astype(BF16)
    term = dot(mine[...], heads_sum, 0, 0)
    far = term.shape[0] // share
    piece = out.shape[1] // far
    for k in range(out.shape[0]):
        for g in range(far):
            rows = slice(g * share + k * piece, g * share + (k + 1) * piece)
            out[k, g * piece : (g + 1) * piece, :] = term[rows, :].astype(BF16)


def spread_body(far, got, out):
    total = added(got).astype(BF16).astype(F32)
    piece = out.shape[1]
    clips = out.shape[0] // far
    for i in range(out.shape[0]):
        g = i // clips
        out[i] = total[g * piece : (g + 1) * piece, :].astype(BF16)


def gather_body(scale, got, out):
    total = (added(got) * scale).astype(BF16)
    for i in range(out.shape[0]):
        out[i] = total


def unpack_body(got, out):
    piece = got.shape[1]
    for i in range(got.shape[0]):
        out[i * piece : (i + 1) * piece, :] = got[i].astype(F32)


def shifted(block, axis, distance):
    devices = range(lax.axis_size(axis))
    route = [(i - distance, i) for i in devices if i - distance in devices]
    return lax.ppermute(block, axis, route)


def swapped(block, axis, distance):
    return lax.ppermute(block, axis, [(i, i ^ distance) for i in range(lax.axis_size(axis))])


def on_device(latents, proj_input, proj_output, scan_input, log_decay, att_queries, att_keys,
              att_values, scan_cotangent, window_offsets):
    _, rows, width = latents.shape
    heads = log_decay.shape[2]
    cols = scan_input.shape[2]
    hd = cols // heads
    n = proj_input.shape[1]
    share = width // lax.axis_size("space")
    assert heads == 2
    near = math.gcd(lax.axis_size("space"), 4)
    far = lax.axis_size("space") // near
    tm = lax.axis_size("tm")
    me = lax.axis_index("tm")
    lat, x, ld = latents[0], scan_input[0], log_decay[0].T
    q, k, v, cot = att_queries[0], att_keys[0], att_values[0], scan_cotangent[0]

    inputs = [
        pltpu.with_memory_space_constraint(a, pltpu.HBM)
        for a in (lat, proj_input, proj_output, x, cot, ld)
    ]
    state = ((cols, n), F32)
    wire = ((2 * cols + EXTRA, n), BF16)
    b, c, cumc, cumr, fwd, bwd, table, send, mine = call(
        functools.partial(pre_body, heads, share),
        [((rows, n), BF16), ((rows, n), BF16), ((rows, heads), F32), ((heads, rows), F32), state, state,
         ((24, n), F32), wire, ((rows, share * far), BF16)],
        (lax.axis_index("space")[None], *inputs),
        [SMEM] + [HBM] * 6,
        [
            pltpu.VMEM((rows, width), BF16),
            pltpu.VMEM((width, 2 * n), BF16),
            pltpu.VMEM((rows, cols), BF16),
            pltpu.VMEM((rows, cols), BF16),
            pltpu.VMEM((heads, rows), F32),
            pltpu.SemaphoreType.DMA((3 * CHUNKS + 3,)),
        ],
        flops=2 * rows * width * 2 * n + 4 * rows * cols * n,
    )
    inner, gx, both, token = call(
        functools.partial(local_body, heads),
        [((rows, cols), F32), ((rows, cols), F32), ((rows, 2 * n), F32), ((8, n), F32)],
        (x, cot, b, c, cumc, cumr),
        flops=8 * rows * rows * cols,
        transcendentals=rows * rows * heads,
    )
    pair = swapped(send, "tm", 1)
    spread = call(
        pair_body,
        [((tm // 2, hd + EXTRA, n), BF16)],
        (me[None], pair, fwd, bwd, table, token),
        [SMEM] + [VMEM] * 5,
    )[0]
    same_core = [list(range(core, tm, 2)) for core in range(2)]
    got = lax.all_to_all(spread, "tm", 0, 0, axis_index_groups=same_core)
    keep, send = call(
        scan_body,
        [((2 * hd, n), BF16), ((2 * hd, n), BF16)],
        (me[None], got, pair, fwd, bwd, table),
        [SMEM] + [VMEM] * 5,
    )
    got = swapped(send, "tm", 1)
    both, enter, leave = call(
        functools.partial(grads_body, heads),
        [((rows, 2 * n), BF16), ((cols, n), BF16), ((cols, n), BF16)],
        (me[None], keep, got, x, cot, cumc, both),
        [SMEM] + [VMEM] * 6,
        flops=4 * rows * cols * n,
    )
    normed, input_grad = call(
        functools.partial(finish_body, heads),
        [((rows, cols), F32), ((rows, cols), BF16)],
        (b, c, cumc, inner, gx, enter, leave),
        flops=4 * rows * cols * n,
    )
    clips = lax.axis_size("dp")
    across = [
        [(near * g + i) * clips + clip for g in range(far) for clip in range(clips)] for i in range(near)
    ]
    piece = share // tm
    distance = 1
    got = swapped(both, "space", distance)
    while 2 * distance < near:
        both = call(pass_on_body, [((rows, 2 * n), BF16)], (both, got))[0]
        distance *= 2
        got = swapped(both, "space", distance)
    tails = shifted(jnp.concatenate([k[rows - W :], v[rows - W :]], axis=1), "tm", 1)
    layer_out = call(
        functools.partial(attend_body, heads, QB),
        [((rows, cols), BF16)],
        (me[None], pltpu.with_memory_space_constraint(window_offsets, pltpu.HBM), q, k, v, tails, normed),
        [SMEM, HBM] + [VMEM] * 5,
        [pltpu.SMEM(window_offsets.shape, jnp.int32), pltpu.SemaphoreType.DMA],
        flops=4 * rows * 2 * W * cols,
        transcendentals=rows * 2 * W * heads,
    )[0]
    done = pltpu.with_memory_space_constraint(layer_out, pltpu.HBM)
    term = call(
        functools.partial(project_body, share),
        [((tm, far * piece, 2 * n), BF16)],
        (mine, both, got, done),
        [VMEM] * 3 + [HBM],
        flops=2 * rows * share * far * 2 * n,
    )[0]
    got = lax.all_to_all(term, "tm", 0, 0)
    term = call(functools.partial(spread_body, far), [((far * clips, piece, 2 * n), BF16)], (got,))[0]
    got = lax.all_to_all(term, ("space", "dp"), 0, 0, axis_index_groups=across)
    term = call(
        functools.partial(gather_body, 1.0 / math.sqrt(rows * tm * clips)),
        [((tm, piece, 2 * n), BF16)],
        (got,),
    )[0]
    got = lax.all_to_all(term, "tm", 0, 0)
    proj_grad = call(unpack_body, [((share, 2 * n), F32)], (got,))[0]
    return layer_out[None], input_grad[None], proj_grad


def solution(mesh):
    wide = P("dp", "tm", "space")
    return jax.shard_map(
        on_device,
        mesh=mesh,
        in_specs=(P("dp", "tm", None), P(), P(), wide, wide, wide, wide, wide, wide, P("dp", "tm")),
        out_specs=(wide, wide, P("space", None)),
        check_vma=False,
    )
```

```python
import functools
import math

import jax
import jax.numpy as jnp
from jax import lax
from jax.experimental import pallas as pl
from jax.experimental.pallas import tpu as pltpu
from jax.sharding import PartitionSpec as P

W = 128
QB = 128
F32 = jnp.float32
BF16 = jnp.bfloat16
VMEM = pl.BlockSpec(memory_space=pltpu.VMEM)
HBM = pl.BlockSpec(memory_space=pltpu.HBM)
SMEM = pl.BlockSpec(memory_space=pltpu.SMEM)
NEG = -1e30
EXTRA = 8
CHUNKS = 2


def dot(a, b, left, right, precision=None):
    return lax.dot_general(
        a, b, (((left,), (right,)), ((), ())), preferred_element_type=F32, precision=precision
    )


def call(body, out, args, specs=None, scratch=(), flops=0, transcendentals=0, moved=0):
    return pl.pallas_call(
        body,
        out_shape=[jax.ShapeDtypeStruct(s, t) for s, t in out],
        in_specs=specs or [VMEM] * len(args),
        out_specs=[VMEM] * len(out),
        scratch_shapes=scratch,
        compiler_params=pltpu.CompilerParams(vmem_limit_bytes=40 * 2**20),
        cost_estimate=pl.CostEstimate(
            flops=flops, transcendentals=transcendentals, bytes_accessed=moved
        ),
    )(*args)


def three_parts(value):
    high = value.astype(BF16)
    rest = value - high.astype(F32)
    middle = rest.astype(BF16)
    return high, middle, (rest - middle.astype(F32)).astype(BF16)


def put_totals(send, at, totals):
    row = lax.broadcasted_iota(jnp.int32, (EXTRA, send.shape[1]), 0)
    extra = jnp.zeros((EXTRA, send.shape[1]), F32)
    for h, total in enumerate(totals):
        for part, value in enumerate(three_parts(total)):
            extra = jnp.where(row == 3 * h + part, value.astype(F32), extra)
    send[at : at + EXTRA, :] = extra.astype(BF16)


def pre_body(heads, share, place, lat_in, wb_in, wc_in, x_in, cot_in, ld_in, b_out, c_out, cumc_out, cumr_out,
             fresh_out, back_out, table_out, send, mine_out, lat, w, x, cot, ld, sems):
    n = wb_in.shape[1]
    width = lat.shape[1]
    chunks = CHUNKS
    deep = lat.shape[1] // chunks
    pairs = [(ld_in, ld), (x_in, x), (cot_in, cot)]
    for i in range(chunks):
        part = slice(i * deep, (i + 1) * deep)
        pairs.append((wb_in.at[part, :], w.at[part, :n]))
        pairs.append((wc_in.at[part, :], w.at[part, n:]))
        pairs.append((lat_in.at[:, part], lat.at[:, part]))
    copies = [pltpu.make_async_copy(src, dst, sems.at[i]) for i, (src, dst) in enumerate(pairs)]
    for copy in copies:
        copy.start()
    rows = lat.shape[0]
    cols = x.shape[1]
    hd = cols // heads
    scale = 1.0 / math.sqrt(n)
    down = lax.broadcasted_iota(jnp.int32, (rows, rows), 0)
    along = lax.broadcasted_iota(jnp.int32, (rows, rows), 1)
    copies[0].wait()
    cumr = dot(ld[...], (down <= along).astype(F32), 1, 0, lax.Precision.HIGHEST)
    cumc = dot((along <= down).astype(F32), ld[...], 1, 1, lax.Precision.HIGHEST)
    cumc_out[...] = cumc
    cumr_out[...] = cumr
    tail = jnp.exp(cumr[:, rows - 1 : rows] - cumr)
    rise = jnp.exp(cumr) * scale
    table_out[...] = jnp.zeros_like(table_out)
    totals = []
    for h in range(heads):
        totals.append(jnp.broadcast_to(cumc[rows - 1 : rows, h : h + 1], (1, n)))
        table_out[h : h + 1, :] = totals[h]
    put_totals(send, 2 * cols, totals)
    copies[1].wait()
    copies[2].wait()
    decayed = []
    for h in range(heads):
        at = slice(h * hd, (h + 1) * hd)
        xs = (x[:, at].astype(F32).T * tail[h : h + 1, :]).astype(BF16)
        gs = (cot[:, at].astype(F32).T * rise[h : h + 1, :]).astype(BF16)
        decayed.append((xs, gs))
    projected = None
    for i in range(chunks):
        for copy in copies[3 + 3 * i : 6 + 3 * i]:
            copy.wait()
        part = slice(i * deep, (i + 1) * deep)
        one = dot(lat[:, part], w[part, :], 1, 0)
        projected = one if projected is None else projected + one
    b = projected[:, :n].astype(BF16)
    c = projected[:, n:].astype(BF16)
    for h, (xs, gs) in enumerate(decayed):
        at = slice(h * hd, (h + 1) * hd)
        fresh = dot(xs, b, 1, 0)
        back = dot(gs, c, 1, 0)
        fresh_out[at, :] = fresh
        back_out[at, :] = back
        send[at, :] = fresh.astype(BF16)
        send[cols + h * hd : cols + (h + 1) * hd, :] = back.astype(BF16)
    b_out[...] = b
    c_out[...] = c
    far = mine_out.shape[1] // share
    near = width // mine_out.shape[1]
    for g in range(far):
        start = pl.multiple_of((near * g + place[0] % near) * share, share)
        mine_out[:, g * share : (g + 1) * share] = lat[:, pl.ds(start, share)]


def totals_of(got, at):
    total = got[at : at + 1, :].astype(F32)
    for part in (1, 2):
        total = total + got[at + part : at + part + 1, :].astype(F32)
    return total


def pair_body(place, got, fwd, bwd, table, _, send):
    cols, n = fwd.shape
    slots, hd, _ = send.shape
    hd = hd - EXTRA
    me = place[0]
    late = me % 2
    chip = me // 2
    own = jnp.where(late == 1, table[1:2, :], table[0:1, :])
    theirs = jnp.where(
        late == 1, totals_of(got, 2 * cols + 3), totals_of(got, 2 * cols)
    )
    at = pl.ds(pl.multiple_of(late * hd, hd), hd)
    to = pl.ds(pl.multiple_of(cols + late * hd, hd), hd)
    got_f, got_b = got[at, :].astype(F32), got[to, :].astype(F32)
    by_own, by_theirs = jnp.exp(own), jnp.exp(theirs)
    early = late == 0
    f = jnp.where(early, by_theirs, 1.0) * fwd[at, :] + jnp.where(early, 1.0, by_own) * got_f
    b = jnp.where(early, 1.0, by_theirs) * bwd[at, :] + jnp.where(early, by_own, 1.0) * got_b
    row = lax.broadcasted_iota(jnp.int32, (EXTRA, n), 0)
    extra = jnp.zeros((EXTRA, n), F32)
    for part, value in enumerate(three_parts(own + theirs)):
        extra = jnp.where(row == part, value.astype(F32), extra)
    extra = extra.astype(BF16)
    for slot in range(slots):
        send[slot, :hd, :] = jnp.where(slot > chip, f, b).astype(BF16)
        send[slot, hd:, :] = extra


def scan_body(place, got, pair, fwd, bwd, table, keep, send):
    cols, n = fwd.shape
    slots, hd, _ = got.shape
    hd = hd - EXTRA
    late = place[0] % 2
    chip = place[0] // 2
    early = late == 0
    decays = [jnp.exp(totals_of(got.at[i], hd)) for i in range(slots)]
    state = jnp.zeros((hd, n), F32)
    grad = jnp.zeros((hd, n), F32)
    for i in range(slots):
        used = i < chip
        state = jnp.where(used, decays[i], 1.0) * state
        state = state + jnp.where(used, 1.0, 0.0) * got[i, :hd, :].astype(F32)
    for i in reversed(range(slots)):
        used = i > chip
        grad = jnp.where(used, decays[i], 1.0) * grad
        grad = grad + jnp.where(used, 1.0, 0.0) * got[i, :hd, :].astype(F32)
    by_own = jnp.exp(jnp.where(early, table[0:1, :], table[1:2, :]))
    by_theirs = jnp.exp(
        jnp.where(early, totals_of(pair, 2 * cols), totals_of(pair, 2 * cols + 3))
    )
    at = pl.ds(pl.multiple_of(late * hd, hd), hd)
    to = pl.ds(pl.multiple_of(cols + late * hd, hd), hd)
    after = jnp.where(early, fwd[at, :], pair[at, :].astype(F32))
    after = after + jnp.where(early, by_own, by_theirs) * state
    before = jnp.where(early, pair[to, :].astype(F32), bwd[at, :])
    before = before + jnp.where(early, by_theirs, by_own) * grad
    keep[:hd, :] = jnp.where(early, state, after).astype(BF16)
    keep[hd:, :] = jnp.where(early, before, grad).astype(BF16)
    send[:hd, :] = jnp.where(early, after, state).astype(BF16)
    send[hd:, :] = jnp.where(early, grad, before).astype(BF16)


def attend_body(heads, qb, place, offsets_in, q, k, v, tail, normed, out, offsets, sem):
    copy = pltpu.make_async_copy(offsets_in, offsets, sem)
    copy.start()
    rows = q.shape[0]
    hd = q.shape[1] // heads
    w = tail.shape[0]
    scale = 1.0 / math.sqrt(hd)
    i = lax.broadcasted_iota(jnp.int32, (qb, qb + w), 0)
    u = lax.broadcasted_iota(jnp.int32, (qb, qb + w), 1)

    def window(own, blk, at, behind):
        if blk == 0:
            return jnp.concatenate([tail[:, behind], own[:qb, at]], axis=0)
        return own[blk * qb - w : (blk + 1) * qb, at]

    places = [(blk, h) for blk in range(rows // qb) for h in range(heads)]
    scores = []
    for blk, h in places:
        at = slice(h * hd, (h + 1) * hd)
        keys = window(k, blk, at, at)
        scores.append(dot(q[blk * qb : (blk + 1) * qb, at], keys, 1, 1) * scale)
    copy.wait()
    for (blk, h), score in zip(places, scores):
        at = slice(h * hd, (h + 1) * hd)
        seen = (u <= i + w) & (u >= i + 1 + offsets[0, blk])
        if blk == 0:
            seen = seen & ((u >= w) | (place[0] > 0))
        score = jnp.where(seen, score, NEG)
        expo = jnp.exp(score - jnp.max(score, axis=-1, keepdims=True))
        probs = (expo / jnp.sum(expo, axis=-1, keepdims=True)).astype(BF16)
        values = window(v, blk, at, slice((heads + h) * hd, (heads + h + 1) * hd))
        own = slice(blk * qb, (blk + 1) * qb)
        out[own, at] = (normed[own, at] + dot(probs, values, 1, 0)).astype(BF16)


def local_body(heads, x, cot, b, c, cumc, cumr, inner_out, gx_out, both_out, token):
    token[...] = jnp.zeros_like(token)
    rows = x.shape[0]
    hd = x.shape[1] // heads
    n = b.shape[1]
    scale = 1.0 / math.sqrt(n)
    t = lax.broadcasted_iota(jnp.int32, (rows, rows), 0)
    s = lax.broadcasted_iota(jnp.int32, (rows, rows), 1)
    kern = dot(c[...], b[...], 1, 1) * scale
    weigh = None
    for h in range(heads):
        at = slice(h * hd, (h + 1) * hd)
        gap = cumc[:, h : h + 1] - cumr[h : h + 1, :]
        decay = jnp.exp(jnp.where(s <= t, gap, NEG))
        mixing = (kern * decay).astype(BF16)
        inner_out[:, at] = dot(mixing, x[:, at], 1, 0)
        gx_out[:, at] = dot(mixing, cot[:, at], 0, 0)
        one = dot(cot[:, at], x[:, at], 1, 1) * decay
        weigh = one if weigh is None else weigh + one
    weigh = (weigh * scale).astype(BF16)
    both_out[:, :n] = dot(weigh, c[...], 0, 0)
    both_out[:, n:] = dot(weigh, b[...], 1, 0)


def grads_body(heads, place, keep, got, x, cot, cumc, both, out, enter_out, leave_out):
    rows = x.shape[0]
    cols = x.shape[1]
    hd = cols // heads
    n = keep.shape[1]
    scale = 1.0 / math.sqrt(n)
    gb = both[:, :n]
    gc = both[:, n:]
    for h in range(heads):
        at = slice(h * hd, (h + 1) * hd)
        mine = place[0] % 2 == h
        state = jnp.where(mine, keep[:hd, :].astype(F32), got[:hd, :].astype(F32)).astype(BF16)
        grad = jnp.where(mine, keep[hd:, :].astype(F32), got[hd:, :].astype(F32)).astype(BF16)
        enter_out[at, :] = state
        leave_out[at, :] = grad
        cum = cumc[:, h : h + 1]
        tail = jnp.exp(cumc[rows - 1 : rows, h : h + 1] - cum)
        rise = jnp.exp(cum) * scale
        gb = gb + tail * dot(x[:, at], grad, 1, 0)
        gc = gc + rise * dot(cot[:, at], state, 1, 0)
    gb, gc = gb.astype(BF16), gc.astype(BF16)
    out[:, :n] = gb
    out[:, n:] = gc


def finish_body(heads, b, c, cumc, inner, gx, enter, leave, normed_out, input_grad):
    rows = b.shape[0]
    hd = inner.shape[1] // heads
    n = b.shape[1]
    scale = 1.0 / math.sqrt(n)
    for h in range(heads):
        at = slice(h * hd, (h + 1) * hd)
        cum = cumc[:, h : h + 1]
        tail = jnp.exp(cumc[rows - 1 : rows, h : h + 1] - cum)
        rise = jnp.exp(cum) * scale
        y = inner[:, at] + rise * dot(c[...], enter[at, :], 1, 1)
        y = y * lax.rsqrt(jnp.mean(y * y, axis=-1, keepdims=True) + 1e-05)
        normed_out[:, at] = y
        g = gx[:, at] + tail * dot(b[...], leave[at, :], 1, 1)
        input_grad[:, at] = g.astype(BF16)


def added(got):
    total = got[0].astype(F32)
    for i in range(1, got.shape[0]):
        total = total + got[i].astype(F32)
    return total


def pass_on_body(own, got, out):
    out[...] = (own[...].astype(F32) + got[...].astype(F32)).astype(BF16)


def project_body(share, place, mine, own, got, _, keep, send):
    heads_sum = (own[...].astype(F32) + got[...].astype(F32)).astype(BF16)
    term = dot(mine[...], heads_sum, 0, 0)
    far = term.shape[0] // share
    piece = keep.shape[1] // far
    late = place[0] % 2 == 1
    for k in range(keep.shape[0]):
        for g in range(far):
            start = g * share + 2 * k * piece
            first = term[start : start + piece, :]
            second = term[start + piece : start + 2 * piece, :]
            at = slice(g * piece, (g + 1) * piece)
            keep[k, at, :] = jnp.where(late, second, first).astype(BF16)
            send[k, at, :] = jnp.where(late, first, second).astype(BF16)


def spread_body(far, got, out):
    total = added(got).astype(BF16).astype(F32)
    piece = out.shape[1]
    clips = out.shape[0] // far
    for i in range(out.shape[0]):
        g = i // clips
        out[i] = total[g * piece : (g + 1) * piece, :].astype(BF16)


def gather_body(scale, got, out):
    total = (added(got) * scale).astype(BF16)
    for i in range(out.shape[0]):
        out[i] = total


def unpack_body(got, out):
    piece = got.shape[1]
    for i in range(got.shape[0]):
        out[i * piece : (i + 1) * piece, :] = got[i].astype(F32)


def shifted(block, axis, distance):
    devices = range(lax.axis_size(axis))
    route = [(i - distance, i) for i in devices if i - distance in devices]
    return lax.ppermute(block, axis, route)


def swapped(block, axis, distance):
    return lax.ppermute(block, axis, [(i, i ^ distance) for i in range(lax.axis_size(axis))])


def on_device(latents, proj_input, proj_output, scan_input, log_decay, att_queries, att_keys,
              att_values, scan_cotangent, window_offsets):
    _, rows, width = latents.shape
    heads = log_decay.shape[2]
    cols = scan_input.shape[2]
    hd = cols // heads
    n = proj_input.shape[1]
    share = width // lax.axis_size("space")
    assert heads == 2
    near = math.gcd(lax.axis_size("space"), 4)
    far = lax.axis_size("space") // near
    tm = lax.axis_size("tm")
    me = lax.axis_index("tm")
    lat, x, ld = latents[0], scan_input[0], log_decay[0].T
    q, k, v, cot = att_queries[0], att_keys[0], att_values[0], scan_cotangent[0]

    inputs = [
        pltpu.with_memory_space_constraint(a, pltpu.HBM)
        for a in (lat, proj_input, proj_output, x, cot, ld)
    ]
    state = ((cols, n), F32)
    wire = ((2 * cols + EXTRA, n), BF16)
    b, c, cumc, cumr, fwd, bwd, table, send, mine = call(
        functools.partial(pre_body, heads, share),
        [((rows, n), BF16), ((rows, n), BF16), ((rows, heads), F32), ((heads, rows), F32), state, state,
         ((24, n), F32), wire, ((rows, share * far), BF16)],
        (lax.axis_index("space")[None], *inputs),
        [SMEM] + [HBM] * 6,
        [
            pltpu.VMEM((rows, width), BF16),
            pltpu.VMEM((width, 2 * n), BF16),
            pltpu.VMEM((rows, cols), BF16),
            pltpu.VMEM((rows, cols), BF16),
            pltpu.VMEM((heads, rows), F32),
            pltpu.SemaphoreType.DMA((3 * CHUNKS + 3,)),
        ],
        flops=2 * rows * width * 2 * n + 4 * rows * cols * n,
    )
    inner, gx, both, token = call(
        functools.partial(local_body, heads),
        [((rows, cols), F32), ((rows, cols), F32), ((rows, 2 * n), F32), ((8, n), F32)],
        (x, cot, b, c, cumc, cumr),
        flops=8 * rows * rows * cols,
        transcendentals=rows * rows * heads,
    )
    pair = swapped(send, "tm", 1)
    spread = call(
        pair_body,
        [((tm // 2, hd + EXTRA, n), BF16)],
        (me[None], pair, fwd, bwd, table, token),
        [SMEM] + [VMEM] * 5,
    )[0]
    same_core = [list(range(core, tm, 2)) for core in range(2)]
    got = lax.all_to_all(spread, "tm", 0, 0, axis_index_groups=same_core)
    keep, send = call(
        scan_body,
        [((2 * hd, n), BF16), ((2 * hd, n), BF16)],
        (me[None], got, pair, fwd, bwd, table),
        [SMEM] + [VMEM] * 5,
    )
    got = swapped(send, "tm", 1)
    both, enter, leave = call(
        functools.partial(grads_body, heads),
        [((rows, 2 * n), BF16), ((cols, n), BF16), ((cols, n), BF16)],
        (me[None], keep, got, x, cot, cumc, both),
        [SMEM] + [VMEM] * 6,
        flops=4 * rows * cols * n,
    )
    normed, input_grad = call(
        functools.partial(finish_body, heads),
        [((rows, cols), F32), ((rows, cols), BF16)],
        (b, c, cumc, inner, gx, enter, leave),
        flops=4 * rows * cols * n,
    )
    clips = lax.axis_size("dp")
    across = [
        [(near * g + i) * clips + clip for g in range(far) for clip in range(clips)] for i in range(near)
    ]
    piece = share // tm
    distance = 1
    got = swapped(both, "space", distance)
    while 2 * distance < near:
        both = call(pass_on_body, [((rows, 2 * n), BF16)], (both, got))[0]
        distance *= 2
        got = swapped(both, "space", distance)
    tails = shifted(jnp.concatenate([k[rows - W :], v[rows - W :]], axis=1), "tm", 1)
    layer_out = call(
        functools.partial(attend_body, heads, QB),
        [((rows, cols), BF16)],
        (me[None], pltpu.with_memory_space_constraint(window_offsets, pltpu.HBM), q, k, v, tails, normed),
        [SMEM, HBM] + [VMEM] * 5,
        [pltpu.SMEM(window_offsets.shape, jnp.int32), pltpu.SemaphoreType.DMA],
        flops=4 * rows * 2 * W * cols,
        transcendentals=rows * 2 * W * heads,
    )[0]
    done = pltpu.with_memory_space_constraint(layer_out, pltpu.HBM)
    half = ((tm // 2, far * piece, 2 * n), BF16)
    term, send = call(
        functools.partial(project_body, share),
        [half, half],
        (me[None], mine, both, got, done),
        [SMEM] + [VMEM] * 3 + [HBM],
        flops=2 * rows * share * far * 2 * n,
    )
    term = call(pass_on_body, [half], (term, swapped(send, "tm", 1)))[0]
    got = lax.all_to_all(term, "tm", 0, 0, axis_index_groups=same_core)
    term = call(functools.partial(spread_body, far), [((far * clips, piece, 2 * n), BF16)], (got,))[0]
    got = lax.all_to_all(term, ("space", "dp"), 0, 0, axis_index_groups=across)
    term = call(
        functools.partial(gather_body, 1.0 / math.sqrt(rows * tm * clips)),
        [((tm, piece, 2 * n), BF16)],
        (got,),
    )[0]
    got = lax.all_to_all(term, "tm", 0, 0)
    proj_grad = call(unpack_body, [((share, 2 * n), F32)], (got,))[0]
    return layer_out[None], input_grad[None], proj_grad


def solution(mesh):
    wide = P("dp", "tm", "space")
    return jax.shard_map(
        on_device,
        mesh=mesh,
        in_specs=(P("dp", "tm", None), P(), P(), wide, wide, wide, wide, wide, wide, P("dp", "tm")),
        out_specs=(wide, wide, P("space", None)),
        check_vma=False,
    )
```

```python
import functools
import math

import jax
import jax.numpy as jnp
from jax import lax
from jax.experimental import pallas as pl
from jax.experimental.pallas import tpu as pltpu
from jax.sharding import PartitionSpec as P

W = 128
QB = 128
F32 = jnp.float32
BF16 = jnp.bfloat16
VMEM = pl.BlockSpec(memory_space=pltpu.VMEM)
HBM = pl.BlockSpec(memory_space=pltpu.HBM)
SMEM = pl.BlockSpec(memory_space=pltpu.SMEM)
NEG = -1e30
EXTRA = 8
CHUNKS = 2


def dot(a, b, left, right, precision=None):
    return lax.dot_general(
        a, b, (((left,), (right,)), ((), ())), preferred_element_type=F32, precision=precision
    )


def call(body, out, args, specs=None, scratch=(), flops=0, transcendentals=0, moved=0):
    return pl.pallas_call(
        body,
        out_shape=[jax.ShapeDtypeStruct(s, t) for s, t in out],
        in_specs=specs or [VMEM] * len(args),
        out_specs=[VMEM] * len(out),
        scratch_shapes=scratch,
        compiler_params=pltpu.CompilerParams(vmem_limit_bytes=40 * 2**20),
        cost_estimate=pl.CostEstimate(
            flops=flops, transcendentals=transcendentals, bytes_accessed=moved
        ),
    )(*args)


def three_parts(value):
    high = value.astype(BF16)
    rest = value - high.astype(F32)
    middle = rest.astype(BF16)
    return high, middle, (rest - middle.astype(F32)).astype(BF16)


def put_totals(send, at, totals):
    row = lax.broadcasted_iota(jnp.int32, (EXTRA, send.shape[1]), 0)
    extra = jnp.zeros((EXTRA, send.shape[1]), F32)
    for h, total in enumerate(totals):
        for part, value in enumerate(three_parts(total)):
            extra = jnp.where(row == 3 * h + part, value.astype(F32), extra)
    send[at : at + EXTRA, :] = extra.astype(BF16)


def pre_body(heads, share, place, lat_in, wb_in, wc_in, x_in, cot_in, ld_in, b_out, c_out, cumc_out, cumr_out,
             fresh_out, back_out, table_out, send, mine_out, x, cot, lat, w, ld, sems):
    n = wb_in.shape[1]
    width = lat.shape[1]
    chunks = CHUNKS
    deep = lat.shape[1] // chunks
    pairs = [(ld_in, ld), (x_in, x), (cot_in, cot)]
    for i in range(chunks):
        part = slice(i * deep, (i + 1) * deep)
        pairs.append((wb_in.at[part, :], w.at[part, :n]))
        pairs.append((wc_in.at[part, :], w.at[part, n:]))
        pairs.append((lat_in.at[:, part], lat.at[:, part]))
    copies = [pltpu.make_async_copy(src, dst, sems.at[i]) for i, (src, dst) in enumerate(pairs)]
    for copy in copies:
        copy.start()
    rows = lat.shape[0]
    cols = x.shape[1]
    hd = cols // heads
    scale = 1.0 / math.sqrt(n)
    down = lax.broadcasted_iota(jnp.int32, (rows, rows), 0)
    along = lax.broadcasted_iota(jnp.int32, (rows, rows), 1)
    copies[0].wait()
    cumr = dot(ld[...], (down <= along).astype(F32), 1, 0, lax.Precision.HIGHEST)
    cumc = dot((along <= down).astype(F32), ld[...], 1, 1, lax.Precision.HIGHEST)
    cumc_out[...] = cumc
    cumr_out[...] = cumr
    tail = jnp.exp(cumr[:, rows - 1 : rows] - cumr)
    rise = jnp.exp(cumr) * scale
    table_out[...] = jnp.zeros_like(table_out)
    totals = []
    for h in range(heads):
        totals.append(jnp.broadcast_to(cumc[rows - 1 : rows, h : h + 1], (1, n)))
        table_out[h : h + 1, :] = totals[h]
    put_totals(send, 2 * cols, totals)
    copies[1].wait()
    copies[2].wait()
    decayed = []
    for h in range(heads):
        at = slice(h * hd, (h + 1) * hd)
        xs = (x[:, at].astype(F32).T * tail[h : h + 1, :]).astype(BF16)
        gs = (cot[:, at].astype(F32).T * rise[h : h + 1, :]).astype(BF16)
        decayed.append((xs, gs))
    projected = None
    for i in range(chunks):
        for copy in copies[3 + 3 * i : 6 + 3 * i]:
            copy.wait()
        part = slice(i * deep, (i + 1) * deep)
        one = dot(lat[:, part], w[part, :], 1, 0)
        projected = one if projected is None else projected + one
    b = projected[:, :n].astype(BF16)
    c = projected[:, n:].astype(BF16)
    for h, (xs, gs) in enumerate(decayed):
        at = slice(h * hd, (h + 1) * hd)
        fresh = dot(xs, b, 1, 0)
        back = dot(gs, c, 1, 0)
        fresh_out[at, :] = fresh
        back_out[at, :] = back
        send[at, :] = fresh.astype(BF16)
        send[cols + h * hd : cols + (h + 1) * hd, :] = back.astype(BF16)
    b_out[...] = b
    c_out[...] = c
    far = mine_out.shape[1] // share
    near = width // mine_out.shape[1]
    for g in range(far):
        start = pl.multiple_of((near * g + place[0] % near) * share, share)
        mine_out[:, g * share : (g + 1) * share] = lat[:, pl.ds(start, share)]


def totals_of(got, at):
    total = got[at : at + 1, :].astype(F32)
    for part in (1, 2):
        total = total + got[at + part : at + part + 1, :].astype(F32)
    return total


def pair_body(place, got, fwd, bwd, table, _, send):
    cols, n = fwd.shape
    slots, hd, _ = send.shape
    hd = hd - EXTRA
    me = place[0]
    late = me % 2
    chip = me // 2
    own = jnp.where(late == 1, table[1:2, :], table[0:1, :])
    theirs = jnp.where(
        late == 1, totals_of(got, 2 * cols + 3), totals_of(got, 2 * cols)
    )
    at = pl.ds(pl.multiple_of(late * hd, hd), hd)
    to = pl.ds(pl.multiple_of(cols + late * hd, hd), hd)
    got_f, got_b = got[at, :].astype(F32), got[to, :].astype(F32)
    by_own, by_theirs = jnp.exp(own), jnp.exp(theirs)
    early = late == 0
    f = jnp.where(early, by_theirs, 1.0) * fwd[at, :] + jnp.where(early, 1.0, by_own) * got_f
    b = jnp.where(early, 1.0, by_theirs) * bwd[at, :] + jnp.where(early, by_own, 1.0) * got_b
    row = lax.broadcasted_iota(jnp.int32, (EXTRA, n), 0)
    extra = jnp.zeros((EXTRA, n), F32)
    for part, value in enumerate(three_parts(own + theirs)):
        extra = jnp.where(row == part, value.astype(F32), extra)
    extra = extra.astype(BF16)
    for slot in range(slots):
        send[slot, :hd, :] = jnp.where(slot > chip, f, b).astype(BF16)
        send[slot, hd:, :] = extra


def scan_body(place, got, pair, fwd, bwd, table, keep, send):
    cols, n = fwd.shape
    slots, hd, _ = got.shape
    hd = hd - EXTRA
    late = place[0] % 2
    chip = place[0] // 2
    early = late == 0
    decays = [jnp.exp(totals_of(got.at[i], hd)) for i in range(slots)]
    state = jnp.zeros((hd, n), F32)
    grad = jnp.zeros((hd, n), F32)
    for i in range(slots):
        used = i < chip
        state = jnp.where(used, decays[i], 1.0) * state
        state = state + jnp.where(used, 1.0, 0.0) * got[i, :hd, :].astype(F32)
    for i in reversed(range(slots)):
        used = i > chip
        grad = jnp.where(used, decays[i], 1.0) * grad
        grad = grad + jnp.where(used, 1.0, 0.0) * got[i, :hd, :].astype(F32)
    by_own = jnp.exp(jnp.where(early, table[0:1, :], table[1:2, :]))
    by_theirs = jnp.exp(
        jnp.where(early, totals_of(pair, 2 * cols), totals_of(pair, 2 * cols + 3))
    )
    at = pl.ds(pl.multiple_of(late * hd, hd), hd)
    to = pl.ds(pl.multiple_of(cols + late * hd, hd), hd)
    after = jnp.where(early, fwd[at, :], pair[at, :].astype(F32))
    after = after + jnp.where(early, by_own, by_theirs) * state
    before = jnp.where(early, pair[to, :].astype(F32), bwd[at, :])
    before = before + jnp.where(early, by_theirs, by_own) * grad
    keep[:hd, :] = jnp.where(early, state, after).astype(BF16)
    keep[hd:, :] = jnp.where(early, before, grad).astype(BF16)
    send[:hd, :] = jnp.where(early, after, state).astype(BF16)
    send[hd:, :] = jnp.where(early, grad, before).astype(BF16)


def attend_body(heads, qb, place, offsets_in, q, k, v, tail, normed, out, offsets, sem):
    copy = pltpu.make_async_copy(offsets_in, offsets, sem)
    copy.start()
    rows = q.shape[0]
    hd = q.shape[1] // heads
    w = tail.shape[0]
    scale = 1.0 / math.sqrt(hd)
    i = lax.broadcasted_iota(jnp.int32, (qb, qb + w), 0)
    u = lax.broadcasted_iota(jnp.int32, (qb, qb + w), 1)

    def window(own, blk, at, behind):
        if blk == 0:
            return jnp.concatenate([tail[:, behind], own[:qb, at]], axis=0)
        return own[blk * qb - w : (blk + 1) * qb, at]

    places = [(blk, h) for blk in range(rows // qb) for h in range(heads)]
    scores = []
    for blk, h in places:
        at = slice(h * hd, (h + 1) * hd)
        keys = window(k, blk, at, at)
        scores.append(dot(q[blk * qb : (blk + 1) * qb, at], keys, 1, 1) * scale)
    copy.wait()
    for (blk, h), score in zip(places, scores):
        at = slice(h * hd, (h + 1) * hd)
        seen = (u <= i + w) & (u >= i + 1 + offsets[0, blk])
        if blk == 0:
            seen = seen & ((u >= w) | (place[0] > 0))
        score = jnp.where(seen, score, NEG)
        expo = jnp.exp(score - jnp.max(score, axis=-1, keepdims=True))
        probs = (expo / jnp.sum(expo, axis=-1, keepdims=True)).astype(BF16)
        values = window(v, blk, at, slice((heads + h) * hd, (heads + h + 1) * hd))
        own = slice(blk * qb, (blk + 1) * qb)
        out[own, at] = (normed[own, at] + dot(probs, values, 1, 0)).astype(BF16)


def local_body(heads, x, cot, b, c, cumc, cumr, inner_out, gx_out, both_out, token):
    token[...] = jnp.zeros_like(token)
    rows = x.shape[0]
    hd = x.shape[1] // heads
    n = b.shape[1]
    scale = 1.0 / math.sqrt(n)
    t = lax.broadcasted_iota(jnp.int32, (rows, rows), 0)
    s = lax.broadcasted_iota(jnp.int32, (rows, rows), 1)
    kern = dot(c[...], b[...], 1, 1) * scale
    weigh = None
    for h in range(heads):
        at = slice(h * hd, (h + 1) * hd)
        gap = cumc[:, h : h + 1] - cumr[h : h + 1, :]
        decay = jnp.exp(jnp.where(s <= t, gap, NEG))
        mixing = (kern * decay).astype(BF16)
        inner_out[:, at] = dot(mixing, x[:, at], 1, 0)
        gx_out[:, at] = dot(mixing, cot[:, at], 0, 0)
        one = dot(cot[:, at], x[:, at], 1, 1) * decay
        weigh = one if weigh is None else weigh + one
    weigh = (weigh * scale).astype(BF16)
    both_out[:, :n] = dot(weigh, c[...], 0, 0)
    both_out[:, n:] = dot(weigh, b[...], 1, 0)


def grads_body(heads, place, keep, got, x, cot, cumc, both, out, enter_out, leave_out):
    rows = x.shape[0]
    cols = x.shape[1]
    hd = cols // heads
    n = keep.shape[1]
    scale = 1.0 / math.sqrt(n)
    gb = both[:, :n]
    gc = both[:, n:]
    for h in range(heads):
        at = slice(h * hd, (h + 1) * hd)
        mine = place[0] % 2 == h
        state = jnp.where(mine, keep[:hd, :].astype(F32), got[:hd, :].astype(F32)).astype(BF16)
        grad = jnp.where(mine, keep[hd:, :].astype(F32), got[hd:, :].astype(F32)).astype(BF16)
        enter_out[at, :] = state
        leave_out[at, :] = grad
        cum = cumc[:, h : h + 1]
        tail = jnp.exp(cumc[rows - 1 : rows, h : h + 1] - cum)
        rise = jnp.exp(cum) * scale
        gb = gb + tail * dot(x[:, at], grad, 1, 0)
        gc = gc + rise * dot(cot[:, at], state, 1, 0)
    gb, gc = gb.astype(BF16), gc.astype(BF16)
    out[:, :n] = gb
    out[:, n:] = gc


def finish_body(heads, b, c, cumc, inner, gx, enter, leave, normed_out, input_grad):
    rows = b.shape[0]
    hd = inner.shape[1] // heads
    n = b.shape[1]
    scale = 1.0 / math.sqrt(n)
    for h in range(heads):
        at = slice(h * hd, (h + 1) * hd)
        cum = cumc[:, h : h + 1]
        tail = jnp.exp(cumc[rows - 1 : rows, h : h + 1] - cum)
        rise = jnp.exp(cum) * scale
        y = inner[:, at] + rise * dot(c[...], enter[at, :], 1, 1)
        y = y * lax.rsqrt(jnp.mean(y * y, axis=-1, keepdims=True) + 1e-05)
        normed_out[:, at] = y
        g = gx[:, at] + tail * dot(b[...], leave[at, :], 1, 1)
        input_grad[:, at] = g.astype(BF16)


def added(got):
    total = got[0].astype(F32)
    for i in range(1, got.shape[0]):
        total = total + got[i].astype(F32)
    return total


def pass_on_body(own, got, out):
    out[...] = (own[...].astype(F32) + got[...].astype(F32)).astype(BF16)


def project_body(share, mine, own, got, _, out):
    heads_sum = (own[...].astype(F32) + got[...].astype(F32)).astype(BF16)
    term = dot(mine[...], heads_sum, 0, 0)
    far = term.shape[0] // share
    piece = out.shape[1] // far
    for k in range(out.shape[0]):
        for g in range(far):
            rows = slice(g * share + k * piece, g * share + (k + 1) * piece)
            out[k, g * piece : (g + 1) * piece, :] = term[rows, :].astype(BF16)


def spread_body(far, got, out):
    total = added(got).astype(BF16).astype(F32)
    piece = out.shape[1]
    clips = out.shape[0] // far
    for i in range(out.shape[0]):
        g = i // clips
        out[i] = total[g * piece : (g + 1) * piece, :].astype(BF16)


def gather_body(scale, got, out):
    total = (added(got) * scale).astype(BF16)
    for i in range(out.shape[0]):
        out[i] = total


def shifted(block, axis, distance):
    devices = range(lax.axis_size(axis))
    route = [(i - distance, i) for i in devices if i - distance in devices]
    return lax.ppermute(block, axis, route)


def swapped(block, axis, distance):
    return lax.ppermute(block, axis, [(i, i ^ distance) for i in range(lax.axis_size(axis))])


def on_device(latents, proj_input, proj_output, scan_input, log_decay, att_queries, att_keys,
              att_values, scan_cotangent, window_offsets):
    _, rows, width = latents.shape
    heads = log_decay.shape[2]
    cols = scan_input.shape[2]
    hd = cols // heads
    n = proj_input.shape[1]
    share = width // lax.axis_size("space")
    assert heads == 2
    near = math.gcd(lax.axis_size("space"), 4)
    far = lax.axis_size("space") // near
    tm = lax.axis_size("tm")
    me = lax.axis_index("tm")
    lat, x, ld = latents[0], scan_input[0], log_decay[0].T
    q, k, v, cot = att_queries[0], att_keys[0], att_values[0], scan_cotangent[0]

    inputs = [
        pltpu.with_memory_space_constraint(a, pltpu.HBM)
        for a in (lat, proj_input, proj_output, x, cot, ld)
    ]
    state = ((cols, n), F32)
    wire = ((2 * cols + EXTRA, n), BF16)
    b, c, cumc, cumr, fwd, bwd, table, send, mine, x, cot = call(
        functools.partial(pre_body, heads, share),
        [((rows, n), BF16), ((rows, n), BF16), ((rows, heads), F32), ((heads, rows), F32), state, state,
         ((24, n), F32), wire, ((rows, share * far), BF16), ((rows, cols), BF16), ((rows, cols), BF16)],
        (lax.axis_index("space")[None], *inputs),
        [SMEM] + [HBM] * 6,
        [
            pltpu.VMEM((rows, width), BF16),
            pltpu.VMEM((width, 2 * n), BF16),
            pltpu.VMEM((heads, rows), F32),
            pltpu.SemaphoreType.DMA((3 * CHUNKS + 3,)),
        ],
        flops=2 * rows * width * 2 * n + 4 * rows * cols * n,
    )
    inner, gx, both, token = call(
        functools.partial(local_body, heads),
        [((rows, cols), F32), ((rows, cols), F32), ((rows, 2 * n), F32), ((8, n), F32)],
        (x, cot, b, c, cumc, cumr),
        flops=8 * rows * rows * cols,
        transcendentals=rows * rows * heads,
    )
    pair = swapped(send, "tm", 1)
    spread = call(
        pair_body,
        [((tm // 2, hd + EXTRA, n), BF16)],
        (me[None], pair, fwd, bwd, table, token),
        [SMEM] + [VMEM] * 5,
    )[0]
    same_core = [list(range(core, tm, 2)) for core in range(2)]
    got = lax.all_to_all(spread, "tm", 0, 0, axis_index_groups=same_core)
    keep, send = call(
        scan_body,
        [((2 * hd, n), BF16), ((2 * hd, n), BF16)],
        (me[None], got, pair, fwd, bwd, table),
        [SMEM] + [VMEM] * 5,
    )
    got = swapped(send, "tm", 1)
    both, enter, leave = call(
        functools.partial(grads_body, heads),
        [((rows, 2 * n), BF16), ((cols, n), BF16), ((cols, n), BF16)],
        (me[None], keep, got, x, cot, cumc, both),
        [SMEM] + [VMEM] * 6,
        flops=4 * rows * cols * n,
    )
    normed, input_grad = call(
        functools.partial(finish_body, heads),
        [((rows, cols), F32), ((rows, cols), BF16)],
        (b, c, cumc, inner, gx, enter, leave),
        flops=4 * rows * cols * n,
    )
    clips = lax.axis_size("dp")
    across = [
        [(near * g + i) * clips + clip for g in range(far) for clip in range(clips)] for i in range(near)
    ]
    piece = share // tm
    distance = 1
    got = swapped(both, "space", distance)
    while 2 * distance < near:
        both = call(pass_on_body, [((rows, 2 * n), BF16)], (both, got))[0]
        distance *= 2
        got = swapped(both, "space", distance)
    tails = shifted(jnp.concatenate([k[rows - W :], v[rows - W :]], axis=1), "tm", 1)
    layer_out = call(
        functools.partial(attend_body, heads, QB),
        [((rows, cols), BF16)],
        (me[None], pltpu.with_memory_space_constraint(window_offsets, pltpu.HBM), q, k, v, tails, normed),
        [SMEM, HBM] + [VMEM] * 5,
        [pltpu.SMEM(window_offsets.shape, jnp.int32), pltpu.SemaphoreType.DMA],
        flops=4 * rows * 2 * W * cols,
        transcendentals=rows * 2 * W * heads,
    )[0]
    done = pltpu.with_memory_space_constraint(layer_out, pltpu.HBM)
    term = call(
        functools.partial(project_body, share),
        [((tm, far * piece, 2 * n), BF16)],
        (mine, both, got, done),
        [VMEM] * 3 + [HBM],
        flops=2 * rows * share * far * 2 * n,
    )[0]
    got = lax.all_to_all(term, "tm", 0, 0)
    term = call(functools.partial(spread_body, far), [((far * clips, piece, 2 * n), BF16)], (got,))[0]
    got = lax.all_to_all(term, ("space", "dp"), 0, 0, axis_index_groups=across)
    term = call(
        functools.partial(gather_body, 1.0 / math.sqrt(rows * tm * clips)),
        [((tm, piece, 2 * n), BF16)],
        (got,),
    )[0]
    got = lax.all_to_all(term, "tm", 0, 0)
    proj_grad = got.reshape(share, 2 * n).astype(F32)
    return layer_out[None], input_grad[None], proj_grad


def solution(mesh):
    wide = P("dp", "tm", "space")
    return jax.shard_map(
        on_device,
        mesh=mesh,
        in_specs=(P("dp", "tm", None), P(), P(), wide, wide, wide, wide, wide, wide, P("dp", "tm")),
        out_specs=(wide, wide, P("space", None)),
        check_vma=False,
    )
```
